32 devices in a mesh: batch: 4 (over x, core), seq: 8 (over z, y).
Axes of the slice: x: 2, y: 2, z: 4, core: 2. Of those that a mesh axis runs over, the one named last changes fastest.
Arguments:
- inputs: float32 [8, 2048, 512], P('batch', 'seq'), may hold values from -12 to 12
- norm_gain: float32 [512], replicated, may hold values from 0.25 to 1.75
- norm_bias: float32 [512], replicated, may hold values from -3 to 3
- query_weight: float32 [512, 512], replicated, may hold values from -0.25 to 0.25
- query_bias: float32 [512], replicated, may hold values from -3 to 3
- key_weight: float32 [512, 512], replicated, may hold values from -0.25 to 0.25
- value_weight: float32 [512, 512], replicated, may hold values from -0.25 to 0.25
- value_bias: float32 [512], replicated, may hold values from -3 to 3
- mixer_weight: float32 [512, 512], replicated, may hold values from -0.5 to 0.5
- mixer_bias: float32 [512], replicated, may hold values from -3 to 3
- final_gain: float32 [512], replicated, may hold values from 0.25 to 1.75
- final_bias: float32 [512], replicated, may hold values from -3 to 3
- inner_weight: float32 [512, 2048], replicated, may hold values from -0.25 to 0.25
- inner_bias: float32 [2048], replicated, may hold values from -3 to 3
- outer_weight: float32 [2048, 512], replicated, may hold values from -0.125 to 0.125
- outer_bias: float32 [512], replicated, may hold values from -3 to 3
- cotangent: float32 [8, 2048, 512], P('batch', 'seq'), may hold values from -6 to 6
Outputs:
- outputs: float32 [8, 2048, 512], P('batch', 'seq')
- inputs_grad: float32 [8, 2048, 512], P('batch', 'seq')
- norm_gain_grad: float32 [512], replicated
- norm_bias_grad: float32 [512], replicated
- query_weight_grad: float32 [512, 512], replicated
- query_bias_grad: float32 [512], replicated
- key_weight_grad: float32 [512, 512], replicated
- value_weight_grad: float32 [512, 512], replicated
- value_bias_grad: float32 [512], replicated
- mixer_weight_grad: float32 [512, 512], replicated
- mixer_bias_grad: float32 [512], replicated
- final_gain_grad: float32 [512], replicated
- final_bias_grad: float32 [512], replicated
- inner_weight_grad: float32 [512, 2048], replicated
- inner_bias_grad: float32 [2048], replicated
- outer_weight_grad: float32 [2048, 512], replicated
- outer_bias_grad: float32 [512], replicated
The draws below stay inside these ranges and needn't reach their ends.
All inputs are finite; a program needn't handle non-finite values.
Results may differ from the reference program's by a relative error of at most 0.0003.
Values sent between devices are 32-bit elements; how exact they have to be, the bound alone decides.
No kernel may reach another device: no remote copies, remote signals or barrier semaphores. Data moves between devices by JAX's collectives and lax.ppermute only.
A program may use at most 192 MiB of HBM per device.

```python
import math
import jax
import jax.numpy as jnp
from jax import lax

D = 512
HEADS = 8
HEAD = 64
FF = 2048
SEQS = 8
LENGTH = 2048


def draw_inputs(key, part):
    subkeys = jax.random.split(key, 5)
    summed = jax.random.truncated_normal(subkeys[0], -4.0, 4.0, (SEQS, LENGTH, D), jnp.float32)
    number = 1
    for stride in (8, 32, 128, 512):
        if stride <= LENGTH:
            coarse = jax.random.truncated_normal(subkeys[number], -3.0, 3.0, (SEQS, LENGTH // stride, D), jnp.float32)
            summed = summed + 0.6 * jnp.repeat(coarse, stride, axis=1)
        number = number + 1
    return summed


def block_levels(own_key, shape, cuts, least, high):
    factor_of = 1.0
    for dim, blocks in cuts:
        heights = jax.random.uniform(jax.random.fold_in(jax.random.fold_in(own_key, 6), dim), (blocks,), jnp.float32, least / len(cuts), high / len(cuts))
        factor_of = factor_of * jnp.repeat(jnp.exp(heights), shape[dim] // blocks).reshape((-1,) + (1,) * (len(shape) - 1 - dim))
    return factor_of


def scatter_about(rng, extent, scale, most, cuts=(), kind=jnp.bfloat16):
    loudness = block_levels(rng, extent, cuts, -0.22, 0.18) if cuts else 1.0
    entries = jax.random.normal(rng, extent, jnp.float32) * scale * loudness
    return jnp.minimum(jnp.maximum(entries, -most), most).astype(kind)


def setup_inputs(seed: int = 0) -> dict:
    key_list = jax.random.split(jax.random.key(seed), 18)
    return {
        "inputs": draw_inputs(jax.random.fold_in(key_list[17], 71), 0),
        "norm_gain": jnp.clip(1.0 + 0.15 * jax.random.normal(key_list[1], (D,), jnp.float32), 0.25, 1.75),
        "norm_bias": scatter_about(key_list[2], (D,), 0.5, 3.0, (), jnp.float32),
        "query_weight": scatter_about(key_list[3], (D, D), D ** -0.5, 0.25, (), jnp.float32),
        "query_bias": scatter_about(key_list[4], (D,), 0.5, 3.0, (), jnp.float32),
        "key_weight": scatter_about(key_list[5], (D, D), D ** -0.5, 0.25, (), jnp.float32),
        "value_weight": scatter_about(key_list[6], (D, D), D ** -0.5, 0.25, (), jnp.float32),
        "value_bias": scatter_about(key_list[7], (D,), 0.5, 3.0, (), jnp.float32),
        "mixer_weight": scatter_about(key_list[8], (D, D), (D // 4) ** -0.5, 0.5, (), jnp.float32),
        "mixer_bias": scatter_about(key_list[9], (D,), 0.5, 3.0, (), jnp.float32),
        "final_gain": jnp.clip(1.0 + 0.15 * jax.random.normal(key_list[10], (D,), jnp.float32), 0.25, 1.75),
        "final_bias": scatter_about(key_list[11], (D,), 0.5, 3.0, (), jnp.float32),
        "inner_weight": scatter_about(key_list[12], (D, FF), D ** -0.5, 0.25, (), jnp.float32),
        "inner_bias": scatter_about(key_list[13], (FF,), 0.5, 3.0, (), jnp.float32),
        "outer_weight": scatter_about(key_list[14], (FF, D), FF ** -0.5, 0.125, (), jnp.float32),
        "outer_bias": scatter_about(key_list[15], (D,), 0.5, 3.0, (), jnp.float32),
        "cotangent": scatter_about(key_list[16], (SEQS, LENGTH, D), 1.0, 6.0, ((0, 4), (1, 8)), jnp.float32),
    }


@jax.custom_vjp
def low(v):
    return lax.optimization_barrier(v.astype(jnp.bfloat16)).astype(jnp.float32)

@jax.custom_vjp
def low_back(v):
    return v

def low_keep(v):
    return (low(v), None)

def low_pass(kept, grad):
    return (grad,)

def back_keep(v):
    return (v, None)

def back_low(kept, grad):
    return (low(grad),)
low.defvjp(low_keep, low_pass)
low_back.defvjp(back_keep, back_low)
highest = lax.Precision.HIGHEST

def matmul(left_side, right_side):
    return jnp.dot(left_side, right_side, precision=highest)

def layer_norm(values, gain_vec, shift_vec):
    center = values - lax.optimization_barrier(jnp.mean(values, axis=-1, keepdims=True))
    return center * lax.rsqrt(lax.optimization_barrier(jnp.mean(center * center, axis=-1, keepdims=True)) + 1e-06) * gain_vec + shift_vec

def pair_mean(values):
    return lax.optimization_barrier(jnp.mean(values.reshape((values.shape[0] // 2, 2) + values.shape[1:]), axis=1))

def partner_blocks(source, block_count):
    grouped = source.reshape((block_count // 2, 2, 16) + source.shape[1:])
    return grouped[:, ::-1].reshape((block_count, 16) + source.shape[1:])

def pairs_forward(queries, key_vecs, values, factor):
    weights = jnp.exp(jnp.einsum('bqhe,bkhe->bhqk', queries, key_vecs, precision=highest)) * factor
    numerator = jnp.einsum('bhqk,bkhe->bqhe', weights, values, precision=highest)
    denominator = jnp.transpose(lax.optimization_barrier(jnp.sum(weights, axis=-1)), (0, 2, 1))
    return (numerator, denominator)

def windows(source, blocks):
    padded = jnp.pad(source, ((16, 16), (0, 0), (0, 0)))
    grouped = padded.reshape((blocks + 2, 16) + source.shape[1:])
    return jnp.concatenate([grouped[:-2], grouped[1:-1], grouped[2:]], axis=1)

def attend(queries, key_vecs, values):
    length = queries.shape[0]
    blocks = length // 16
    slot_ids = jnp.arange(48)
    block_ids = jnp.arange(blocks)
    is_valid = ((block_ids[:, None] > 0) | (slot_ids[None, :] >= 16)) & ((block_ids[:, None] < blocks - 1) | (slot_ids[None, :] < 32))
    factor = is_valid.astype(jnp.float32)[:, None, None, :]
    numerator, denominator = pairs_forward(queries.reshape((blocks, 16) + queries.shape[1:]), windows(key_vecs, blocks), windows(values, blocks), factor)
    numerator = numerator.reshape(queries.shape)
    denominator = denominator.reshape(queries.shape[:2])
    coarse_query, coarse_key, coarse_value = (queries, key_vecs, values)
    stride = 1
    while 64 * stride <= length:
        stride = stride * 2
        coarse_query = pair_mean(coarse_query)
        coarse_key = pair_mean(coarse_key)
        coarse_value = pair_mean(coarse_value)
        block_count = length // stride // 16
        part_num, part_den = pairs_forward(coarse_query.reshape((block_count, 16) + coarse_query.shape[1:]), partner_blocks(coarse_key, block_count), partner_blocks(coarse_value, block_count), float(stride))
        numerator = numerator + jnp.repeat(part_num.reshape(coarse_query.shape), stride, axis=0)
        denominator = denominator + jnp.repeat(part_den.reshape(coarse_query.shape[:2]), stride, axis=0)
    return numerator / denominator[..., None]

def forward(sequence, params):
    norm_gain, norm_bias, query_weight, query_bias, key_weight, value_weight, value_bias, mixer_weight, mixer_bias, final_gain, final_bias, inner_weight, inner_bias, outer_weight, outer_bias = params
    normed = layer_norm(sequence, norm_gain, norm_bias)
    head_shape = (sequence.shape[0], HEADS, HEAD)
    queries = ((matmul(normed, query_weight) + query_bias) * (1.0 / math.sqrt(HEAD))).reshape(head_shape)
    key_vecs = matmul(normed, key_weight).reshape(head_shape)
    values = (matmul(normed, value_weight) + value_bias).reshape(head_shape)
    mixed = attend(queries, key_vecs, values).reshape(sequence.shape)
    middle = sequence + matmul(mixed, mixer_weight) + mixer_bias
    hidden = jax.nn.gelu(matmul(layer_norm(middle, final_gain, final_bias), inner_weight) + inner_bias, approximate=False)
    return middle + matmul(hidden, outer_weight) + outer_bias

def reference(inputs, norm_gain, norm_bias, query_weight, query_bias, key_weight, value_weight, value_bias, mixer_weight, mixer_bias, final_gain, final_bias, inner_weight, inner_bias, outer_weight, outer_bias, cotangent):
    params = (norm_gain, norm_bias, query_weight, query_bias, key_weight, value_weight, value_bias, mixer_weight, mixer_bias, final_gain, final_bias, inner_weight, inner_bias, outer_weight, outer_bias)

    def one_sequence(totals, sequence_pair):
        sequence, tangent = sequence_pair
        output, pullback = jax.vjp(forward, sequence, params)
        sequence_grad, params_grad = pullback(tangent)
        return (jax.tree.map(jnp.add, totals, params_grad), (output, sequence_grad))
    totals, (outputs, inputs_grad) = lax.scan(one_sequence, jax.tree.map(jnp.zeros_like, params), (inputs, cotangent))
    return (outputs, inputs_grad, totals[0], totals[1], totals[2], totals[3], totals[4], totals[5], totals[6], totals[7], totals[8], totals[9], totals[10], totals[11], totals[12], totals[13], totals[14])
```

```python
import functools
import math

import jax
import jax.numpy as jnp
import numpy as np
from jax import lax
from jax.experimental import pallas as pl
from jax.experimental.pallas import tpu as pltpu
from jax.sharding import PartitionSpec as P

HEADS = 8
BLOCK = 16
LOG2E = 1.4426950408889634
LN2 = 0.6931471805599453
ROOT_HALF = 0.7071067811865476
INV_ROOT_TWO_PI = 0.3989422804014327
EPS = 1e-06
FAR = -1e30

bf16 = jnp.bfloat16
f32 = jnp.float32
VMEM = pl.BlockSpec(memory_space=pltpu.VMEM)
SMEM = pl.BlockSpec(memory_space=pltpu.SMEM)


def split(value):
    high = value.astype(bf16)
    return high, (value - high.astype(f32)).astype(bf16)


def dg(left, right, left_dim=1, right_dim=0):
    return lax.dot_general(
        left, right, (((left_dim,), (right_dim,)), ((), ())), preferred_element_type=f32
    )


def dot3(left, right, left_dim=1, right_dim=0):
    return (
        dg(left[0], right[0], left_dim, right_dim)
        + dg(left[0], right[1], left_dim, right_dim)
        + dg(left[1], right[0], left_dim, right_dim)
    )


def dot2(left, exact, left_dim=1, right_dim=0):
    return dg(left[0], exact, left_dim, right_dim) + dg(left[1], exact, left_dim, right_dim)


def exact_dot2(exact, right, left_dim=1, right_dim=0):
    return dg(exact, right[0], left_dim, right_dim) + dg(exact, right[1], left_dim, right_dim)


def two_diagonal(pair_rows):
    half = pair_rows.shape[0] // 2
    zero = jnp.zeros((half, pair_rows.shape[1]), pair_rows.dtype)
    return jnp.concatenate(
        [
            jnp.concatenate([pair_rows[:half], zero], axis=1),
            jnp.concatenate([zero, pair_rows[half:]], axis=1),
        ],
        axis=0,
    )


def two_masked(pair_lanes):
    half = pair_lanes.shape[1] // 2
    lower = lax.broadcasted_iota(jnp.int32, pair_lanes.shape, 1) < half
    wide = pair_lanes.astype(f32)
    return jnp.concatenate(
        [jnp.where(lower, wide, 0.0), jnp.where(lower, 0.0, wide)], axis=0
    ).astype(bf16)


def take_diagonal(product):
    half, width = product.shape[0] // 2, product.shape[1] // 2
    return jnp.concatenate([product[:half, :width], product[half:, width:]], axis=0)


def pair_weights(keys, queries_t, bias):
    diag_high, diag_low = two_diagonal(queries_t[0]), two_diagonal(queries_t[1])
    scores = dg(
        jnp.concatenate([keys[0], keys[1], keys[0]], axis=1),
        jnp.concatenate([diag_high, diag_high, diag_low], axis=0),
    )
    return jnp.exp2(scores + bias)


def tile_forward(keys, values_t, queries_t, bias):
    weights = pair_weights(keys, queries_t, bias)
    denominator = jnp.sum(weights, axis=0, keepdims=True)
    high, low = split(weights)
    wide = dg(jnp.concatenate([values_t[0], values_t[1]], axis=0), high)
    size = values_t[0].shape[0]
    product = wide[:size] + wide[size:] + dg(values_t[0], low)
    width = denominator.shape[1] // 2
    return (
        take_diagonal(product),
        jnp.concatenate([denominator[:, :width], denominator[:, width:]], axis=0),
    )


def tile_backward(keys, keys_t, values, queries_t, queries_m, grads_t, grads_m, grad_den, bias):
    weights = pair_weights(keys, queries_t, bias)
    diag_high, diag_low = two_diagonal(grads_t[0]), two_diagonal(grads_t[1])
    grad_weights = (
        dg(
            jnp.concatenate([values[0], values[1], values[0]], axis=1),
            jnp.concatenate([diag_high, diag_high, diag_low], axis=0),
        )
        + grad_den
    )
    scores = split(weights * grad_weights)
    weights = split(weights)

    def gather(pairs, masked):
        wide = dg(pairs[0], jnp.concatenate([masked[0], masked[1]], axis=1))
        half = wide.shape[1] // 2
        return wide[:, :half] + wide[:, half:] + dg(pairs[1], masked[0])

    grad_values = gather(weights, grads_m)
    grad_keys = gather(scores, queries_m)
    wide = dg(jnp.concatenate([keys_t[0], keys_t[1]], axis=0), scores[0])
    size = keys_t[0].shape[0]
    product = wide[:size] + wide[size:] + dg(keys_t[0], scores[1])
    return take_diagonal(product), grad_keys, grad_values


def lanes(parts, start, size):
    return tuple(part[:, start : start + size] for part in parts)


def rows(parts, start, size):
    return tuple(part[start : start + size] for part in parts)


def block_of(parts, row, row_size, lane, lane_size):
    return tuple(part[row : row + row_size, lane : lane + lane_size] for part in parts)


def stack(first, second):
    return tuple(jnp.concatenate([one, two], axis=0) for one, two in zip(first, second))


def norm_rows(values):
    center = values - jnp.mean(values, axis=-1, keepdims=True)
    inverse = lax.rsqrt(jnp.mean(center * center, axis=-1, keepdims=True) + EPS)
    return center * inverse, inverse


def norm_grad(grad_rows, unit_rows, inverse, gain):
    grad_unit = grad_rows * gain
    return inverse * (
        grad_unit
        - jnp.mean(grad_unit, axis=-1, keepdims=True)
        - unit_rows * jnp.mean(grad_unit * unit_rows, axis=-1, keepdims=True)
    )


def first_norm_kernel(groups, span, start_ref, x_ref, unit_ref, inv_ref, inner_ref, outer_ref):
    width = x_ref.shape[-1]
    for group in range(groups):
        own = slice(group * span, (group + 1) * span)
        unit, inverse = norm_rows(x_ref[own, :])
        unit_ref[own, :] = unit
        inv_ref[own, :] = inverse
        runs = span // BLOCK
        inner_ref[group, BLOCK:, :] = jnp.mean(unit.reshape(BLOCK, runs, width), axis=1)
        inner_start = pl.multiple_of(group * span + start_ref[0], BLOCK)
        outer_start = pl.multiple_of(group * span + start_ref[1], BLOCK)
        inner_ref[group, :BLOCK, :] = unit_ref[pl.ds(inner_start, BLOCK), :]
        outer_ref[group] = unit_ref[pl.ds(outer_start, BLOCK), :]


def project_kernel(
    groups, span, scale, unit_ref, gain_ref, shift_ref, qw_ref, qb_ref, kw_ref, vw_ref, vb_ref,
    mean_ref, q_ref, k_ref, v_ref, qc_ref, kc_ref, vc_ref,
):
    normed = split(unit_ref[...] * gain_ref[...] + shift_ref[...])
    means = mean_ref[...]
    coarse = means.shape[0]

    def finish(result, fine_ref, coarse_ref):
        fine_ref[...] = result
        for group in range(groups):
            part = split(result[group * span : (group + 1) * span])
            coarse_ref[group * coarse : (group + 1) * coarse, :] = exact_dot2(means, part)

    finish((dot3(normed, split(qw_ref[...])) + qb_ref[...]) * scale, q_ref, qc_ref)
    finish(dot3(normed, split(kw_ref[...])), k_ref, kc_ref)
    finish(dot3(normed, split(vw_ref[...])) + vb_ref[...], v_ref, vc_ref)


def local_kernel(
    groups, span, edge_ref, q_ref, k_ref, v_ref, qc_ref, kc_ref, vc_ref, halo_ref, gain_ref,
    shift_ref, kw_ref, vw_ref, vb_ref, near_ref, one_ref,
    num_ref, den_ref, numc_ref, denc_ref, hk_ref, hv_ref, bias_ref,
):
    width = q_ref.shape[-1]
    half = span // 2
    coarse = qc_ref.shape[0] // groups
    pairs = HEADS // 2
    pair_width = width // pairs
    tile_keys = half + 2 * BLOCK
    bias_ref[0] = near_ref[...]
    bias_ref[1] = near_ref[...]
    bias_ref[0, :BLOCK, :] = near_ref[:BLOCK, :] + edge_ref[0]
    bias_ref[1, tile_keys - BLOCK :, :] = near_ref[tile_keys - BLOCK :, :] + edge_ref[1]
    normed = split(halo_ref[...] * gain_ref[...] + shift_ref[...])
    halo_keys = dot3(normed, split(kw_ref[...]))
    halo_values = dot3(normed, split(vw_ref[...])) + vb_ref[...]
    hk_ref[...] = halo_keys
    hv_ref[...] = halo_values
    for group in range(groups):
        own = slice(group * span, (group + 1) * span)
        left = slice(group * 2 * BLOCK, group * 2 * BLOCK + BLOCK)
        right = slice(group * 2 * BLOCK + BLOCK, (group + 1) * 2 * BLOCK)
        own_c = slice(group * coarse, group * coarse + half)
        keys = split(jnp.concatenate([halo_keys[left], k_ref[own, :], halo_keys[right]], axis=0))
        values = jnp.concatenate([halo_values[left], v_ref[own, :], halo_values[right]], axis=0)
        values_t = split(values.T)
        queries_t = split(q_ref[own, :].T)
        keys_c = split(kc_ref[own_c, :])
        values_ct = split(vc_ref[own_c, :].T)
        queries_ct = split(qc_ref[own_c, :].T)
        for pair in range(pairs):
            at = pair * pair_width
            out = slice(group * width + at, group * width + at + pair_width)
            heads = slice((group * pairs + pair) * 2, (group * pairs + pair) * 2 + 2)
            for tile in range(2):
                num, den = tile_forward(
                    block_of(keys, tile * half, tile_keys, at, pair_width),
                    block_of(values_t, at, pair_width, tile * half, tile_keys),
                    block_of(queries_t, at, pair_width, tile * half, half),
                    bias_ref[tile],
                )
                num_ref[out, tile * half : (tile + 1) * half] = num
                den_ref[heads, tile * half : (tile + 1) * half] = den
            num, den = tile_forward(
                lanes(keys_c, at, pair_width),
                rows(values_ct, at, pair_width),
                rows(queries_ct, at, pair_width),
                one_ref[...],
            )
            numc_ref[out, :] = num
            denc_ref[heads, :] = den


def remote_kernel(
    groups, span, x_ref, num_ref, den_ref, numc_ref, denc_ref, qc_ref, kc_ref, vc_ref, far_ref,
    gain_ref, shift_ref, kw_ref, vw_ref, vb_ref, rest_ref, expand_ref, mw_ref, mb_ref, fgain_ref,
    fshift_ref, ob_ref,
    rk_ref, rv_ref, mixed_ref, rden_ref, unit_ref, inv_ref, fnorm_ref, acc_ref, mid_ref,
):
    width = x_ref.shape[-1]
    half = span // 2
    coarse = qc_ref.shape[0] // groups
    far = far_ref.shape[0] // groups
    pairs = HEADS // 2
    pair_width = width // pairs
    head_width = width // HEADS
    local_rest = rest_ref.shape[0] - far
    normed = split(far_ref[...] * gain_ref[...] + shift_ref[...])
    far_keys = dot3(normed, split(kw_ref[...]))
    far_values = dot3(normed, split(vw_ref[...])) + vb_ref[...]
    rk_ref[...] = far_keys
    rv_ref[...] = far_values
    expand = expand_ref[...]
    for group in range(groups):
        rest = slice(group * coarse + half, group * coarse + half + local_rest)
        remote = slice(group * far, (group + 1) * far)
        keys = split(jnp.concatenate([kc_ref[rest, :], far_keys[remote]], axis=0))
        values_t = split(jnp.concatenate([vc_ref[rest, :], far_values[remote]], axis=0).T)
        queries_t = split(qc_ref[group * coarse + half : (group + 1) * coarse, :].T)
        nums, dens = [], []
        for pair in range(pairs):
            at = pair * pair_width
            num, den = tile_forward(
                lanes(keys, at, pair_width),
                rows(values_t, at, pair_width),
                rows(queries_t, at, pair_width),
                rest_ref[...],
            )
            nums.append(num)
            dens.append(den)
        own_t = slice(group * width, (group + 1) * width)
        own_h = slice(group * HEADS, (group + 1) * HEADS)
        numc = jnp.concatenate([numc_ref[own_t, :], jnp.concatenate(nums, axis=0)], axis=1)
        denc = jnp.concatenate([denc_ref[own_h, :], jnp.concatenate(dens, axis=0)], axis=1)
        num = num_ref[own_t, :] + dot2(split(numc), expand)
        den = den_ref[own_h, :] + dot2(split(denc), expand)
        inverse = 1.0 / den
        rden_ref[own_h, :] = inverse
        spread = jnp.concatenate(
            [
                jnp.broadcast_to(inverse[head : head + 1], (head_width, span))
                for head in range(HEADS)
            ],
            axis=0,
        )
        mixed_t = num * spread
        own = slice(group * span, (group + 1) * span)
        mixed_ref[own_t, :] = mixed_t
        mid_ref[own, :] = mixed_t.T
    middle = x_ref[...] + dot3(split(mid_ref[...]), split(mw_ref[...])) + mb_ref[...]
    unit, inverse = norm_rows(middle)
    unit_ref[...] = unit
    inv_ref[...] = inverse
    fnorm_ref[...] = unit * fgain_ref[...] + fshift_ref[...]
    acc_ref[...] = middle + ob_ref[...]


def feed_kernel(
    first, which_ref, fnorm_ref, cot_ref, iw_ref, ib_ref, ow_ref, acc_ref, gacc_ref,
    gow_ref, giw_ref, gib_ref, nacc_ref, ngacc_ref,
):
    fnorm = split(fnorm_ref[...])
    iw = split(iw_ref[...])
    inner = dot3(fnorm, iw) + ib_ref[...]
    cumulative = 0.5 * (1.0 + lax.erf(inner * ROOT_HALF))
    hidden = split(inner * cumulative)
    slope = cumulative + inner * jnp.exp(-0.5 * inner * inner) * INV_ROOT_TWO_PI
    ow = split(ow_ref[...])
    nacc_ref[...] = acc_ref[...] + dot3(hidden, ow)
    cot = split(cot_ref[...])
    gow_ref[...] = dot3(hidden, cot, 0, 0)
    grad_inner = dot3(cot, ow, 1, 1) * slope
    gib_ref[...] = jnp.sum(grad_inner, axis=0, keepdims=True)
    grad_inner = split(grad_inner)
    giw_ref[...] = dot3(fnorm, grad_inner, 0, 0)
    grad_fnorm = dot3(grad_inner, iw, 1, 1)
    ngacc_ref[...] = grad_fnorm if first else gacc_ref[...] + grad_fnorm


def middle_grad_kernel(
    groups, span, cot_ref, gf_ref, unit_ref, inv_ref, fgain_ref, mixed_ref, rden_ref, mw_ref,
    expand_ref,
    gmid_ref, gmw_ref, vec_ref, gnum_ref, gnumt_ref, gden_ref, gnumct_ref, gdenc_ref,
):
    width = cot_ref.shape[-1]
    head_width = width // HEADS
    cot = cot_ref[...]
    gf = gf_ref[...]
    unit = unit_ref[...]
    gmid = cot + norm_grad(gf, unit, inv_ref[...], fgain_ref[...])
    gmid_ref[...] = gmid
    vec_ref[0:1, :] = jnp.sum(gf * unit, axis=0, keepdims=True)
    vec_ref[1:2, :] = jnp.sum(gf, axis=0, keepdims=True)
    vec_ref[2:3, :] = jnp.sum(gmid, axis=0, keepdims=True)
    vec_ref[3:4, :] = jnp.sum(cot, axis=0, keepdims=True)
    gmid = split(gmid)
    expand = expand_ref[...]
    grad_mixed = dot3(gmid, split(mw_ref[...]), 1, 1)
    total = None
    for group in range(groups):
        own = slice(group * span, (group + 1) * span)
        own_t = slice(group * width, (group + 1) * width)
        own_h = slice(group * HEADS, (group + 1) * HEADS)
        mixed_t = mixed_ref[own_t, :]
        part = dot3(split(mixed_t), rows(gmid, group * span, span))
        total = part if total is None else total + part
        grad_t = grad_mixed[own].T
        inverse = rden_ref[own_h, :]
        spread = jnp.concatenate(
            [
                jnp.broadcast_to(inverse[head : head + 1], (head_width, span))
                for head in range(HEADS)
            ],
            axis=0,
        )
        product = grad_t * mixed_t
        dens = jnp.concatenate(
            [
                jnp.sum(product[head * head_width : (head + 1) * head_width], axis=0, keepdims=True)
                for head in range(HEADS)
            ],
            axis=0,
        )
        gden = -dens * inverse
        gnum_t = grad_t * spread
        gnumt_ref[own_t, :] = gnum_t
        gnum_ref[own, :] = gnum_t.T
        gden_ref[own_h, :] = gden
        gnumct_ref[own_t, :] = dot2(split(gnum_t), expand, 1, 1)
        gdenc_ref[own_h, :] = dot2(split(gden), expand, 1, 1)
    gmw_ref[...] = total


def pairs_grad_kernel(
    span, edge_ref, q_ref, k_ref, v_ref, qc_ref, kc_ref, vc_ref, hk_ref, hv_ref, rk_ref, rv_ref,
    gnum_ref, gnumt_ref, gden_ref, gnumct_ref, gdenc_ref, near_ref, one_ref, rest_ref, mean_ref,
    dq_ref, dk_ref, dv_ref, hdk_ref, hdv_ref, rdk_ref, rdv_ref,
    bias_ref, dkx_ref, dvx_ref, dkc_ref, dvc_ref, dqt_ref, dqct_ref,
):
    width = q_ref.shape[-1]
    half = span // 2
    coarse = qc_ref.shape[0]
    far = rk_ref.shape[0]
    pairs = HEADS // 2
    pair_width = width // pairs
    tile_keys = half + 2 * BLOCK
    local_rest = rest_ref.shape[0] - far
    local_coarse = half + local_rest
    bias_ref[0] = near_ref[...]
    bias_ref[1] = near_ref[...]
    bias_ref[0, :BLOCK, :] = near_ref[:BLOCK, :] + edge_ref[0]
    bias_ref[1, tile_keys - BLOCK :, :] = near_ref[tile_keys - BLOCK :, :] + edge_ref[1]

    keys_f = jnp.concatenate([hk_ref[:BLOCK, :], k_ref[...], hk_ref[BLOCK:, :]], axis=0)
    keys, keys_t = split(keys_f), split(keys_f.T)
    values = split(jnp.concatenate([hv_ref[:BLOCK, :], v_ref[...], hv_ref[BLOCK:, :]], axis=0))
    q = q_ref[...]
    queries, queries_t = split(q), split(q.T)
    grads, grads_t = split(gnum_ref[...]), split(gnumt_ref[...])
    keys_cf = jnp.concatenate([kc_ref[:local_coarse, :], rk_ref[...]], axis=0)
    keys_c, keys_ct = split(keys_cf), split(keys_cf.T)
    values_c = split(jnp.concatenate([vc_ref[:local_coarse, :], rv_ref[...]], axis=0))
    qc = qc_ref[...]
    queries_c, queries_ct = split(qc), split(qc.T)
    gnumct = gnumct_ref[...]
    grads_c, grads_ct = split(gnumct.T), split(gnumct)
    rest_keys = local_rest + far
    for pair in range(pairs):
        at = pair * pair_width
        cols = slice(at, at + pair_width)

        def den_rows(ref, start):
            both = ref[2 * pair : 2 * pair + 2, start : start + half]
            return jnp.concatenate([both[0:1], both[1:2]], axis=1)

        for tile in range(2):
            start = tile * half
            dq, dk, dv = tile_backward(
                block_of(keys, start, tile_keys, at, pair_width),
                block_of(keys_t, at, pair_width, start, tile_keys),
                block_of(values, start, tile_keys, at, pair_width),
                block_of(queries_t, at, pair_width, start, half),
                tuple(two_masked(part) for part in block_of(queries, start, half, at, pair_width)),
                block_of(grads_t, at, pair_width, start, half),
                tuple(two_masked(part) for part in block_of(grads, start, half, at, pair_width)),
                den_rows(gden_ref, start),
                bias_ref[tile],
            )
            dqt_ref[cols, start : start + half] = dq
            if tile == 0:
                dkx_ref[:tile_keys, cols] = dk
                dvx_ref[:tile_keys, cols] = dv
            else:
                shared = slice(start, start + 2 * BLOCK)
                fresh = slice(start + 2 * BLOCK, start + tile_keys)
                dkx_ref[shared, cols] = dkx_ref[shared, cols] + dk[: 2 * BLOCK]
                dvx_ref[shared, cols] = dvx_ref[shared, cols] + dv[: 2 * BLOCK]
                dkx_ref[fresh, cols] = dk[2 * BLOCK :]
                dvx_ref[fresh, cols] = dv[2 * BLOCK :]
        for start, count, bias in ((0, half, one_ref), (half, rest_keys, rest_ref)):
            dq, dk, dv = tile_backward(
                block_of(keys_c, start, count, at, pair_width),
                block_of(keys_ct, at, pair_width, start, count),
                block_of(values_c, start, count, at, pair_width),
                block_of(queries_ct, at, pair_width, start, half),
                tuple(two_masked(part) for part in block_of(queries_c, start, half, at, pair_width)),
                block_of(grads_ct, at, pair_width, start, half),
                tuple(two_masked(part) for part in block_of(grads_c, start, half, at, pair_width)),
                den_rows(gdenc_ref, start),
                bias[...],
            )
            dqct_ref[cols, start : start + half] = dq
            dkc_ref[start : start + count, cols] = dk
            dvc_ref[start : start + count, cols] = dv
    rdk_ref[...] = dkc_ref[local_coarse:, :] * LN2
    rdv_ref[...] = dvc_ref[local_coarse:, :]
    hdk_ref[:BLOCK, :] = dkx_ref[:BLOCK, :] * LN2
    hdk_ref[BLOCK:, :] = dkx_ref[span + BLOCK :, :] * LN2
    hdv_ref[:BLOCK, :] = dvx_ref[:BLOCK, :]
    hdv_ref[BLOCK:, :] = dvx_ref[span + BLOCK :, :]
    means = mean_ref[...]
    zero = jnp.zeros((coarse - local_coarse, width), f32)

    def spread(ref):
        return exact_dot2(means, split(jnp.concatenate([ref[:local_coarse, :], zero], axis=0)), 0, 0)

    dk_ref[...] = (dkx_ref[BLOCK : span + BLOCK, :] + spread(dkc_ref)) * LN2
    dv_ref[...] = dvx_ref[BLOCK : span + BLOCK, :] + spread(dvc_ref)
    dqt = dqt_ref[...] + dot2(split(dqct_ref[...]), means)
    dq_ref[...] = dqt.T


def project_grad_kernel(
    scale, unit_ref, far_ref, gain_ref, shift_ref, dq_ref, dk_ref, dv_ref, fdk_ref, fdv_ref,
    qw_ref, kw_ref, vw_ref,
    gqw_ref, gkw_ref, gvw_ref, vec_ref, gnorm_ref, gfar_ref,
):
    unit = unit_ref[...]
    far = far_ref[...]
    gain = gain_ref[...]
    shift = shift_ref[...]
    normed = split(unit * gain + shift)
    normed_far = split(far * gain + shift)
    dq_f = dq_ref[...] * scale
    dv_f, fdv_f = dv_ref[...], fdv_ref[...]
    dq, dk, dv = split(dq_f), split(dk_ref[...]), split(dv_f)
    fdk, fdv = split(fdk_ref[...]), split(fdv_f)
    gqw_ref[...] = dot3(normed, dq, 0, 0)
    gkw_ref[...] = dot3(normed, dk, 0, 0) + dot3(normed_far, fdk, 0, 0)
    gvw_ref[...] = dot3(normed, dv, 0, 0) + dot3(normed_far, fdv, 0, 0)
    qw, kw, vw = split(qw_ref[...]), split(kw_ref[...]), split(vw_ref[...])
    gnorm = dot3(dq, qw, 1, 1) + dot3(dk, kw, 1, 1) + dot3(dv, vw, 1, 1)
    gfar = dot3(fdk, kw, 1, 1) + dot3(fdv, vw, 1, 1)
    gnorm_ref[...] = gnorm
    gfar_ref[...] = gfar
    vec_ref[0:1, :] = jnp.sum(gnorm * unit, axis=0, keepdims=True) + jnp.sum(
        gfar * far, axis=0, keepdims=True
    )
    vec_ref[1:2, :] = jnp.sum(gnorm, axis=0, keepdims=True) + jnp.sum(gfar, axis=0, keepdims=True)
    vec_ref[2:3, :] = jnp.sum(dq_f, axis=0, keepdims=True)
    vec_ref[3:4, :] = jnp.sum(dv_f, axis=0, keepdims=True) + jnp.sum(fdv_f, axis=0, keepdims=True)


def first_grad_kernel(
    groups, span, start_ref, gmid_ref, gnorm_ref, inner_ref, outer_ref, four_ref, unit_ref, inv_ref,
    gain_ref, out_ref, total_ref,
):
    width = gmid_ref.shape[-1]
    runs = span // BLOCK
    for group in range(groups):
        own = slice(group * span, (group + 1) * span)
        spread = jnp.broadcast_to(
            four_ref[group].reshape(BLOCK, 1, width) * (1.0 / runs), (BLOCK, runs, width)
        ).reshape(span, width)
        total_ref[own, :] = gnorm_ref[own, :] + spread
        inner_at = pl.ds(pl.multiple_of(group * span + start_ref[0], BLOCK), BLOCK)
        outer_at = pl.ds(pl.multiple_of(group * span + start_ref[1], BLOCK), BLOCK)
        total_ref[inner_at, :] = total_ref[inner_at, :] + inner_ref[group]
        total_ref[outer_at, :] = total_ref[outer_at, :] + outer_ref[group]
    out_ref[...] = gmid_ref[...] + norm_grad(
        total_ref[...], unit_ref[...], inv_ref[...], gain_ref[...]
    )


def level_tables(span, crossing):
    half = span // 2
    top = int(math.log2(span // BLOCK // 2)) + crossing
    local_top = top - crossing
    expand = np.zeros((span, span), np.float32)
    means = np.zeros((span, span), np.float32)
    levels, at = [], 0
    for level in range(1, top + 1):
        count = span >> level
        for row in range(count):
            expand[at + row, row << level : (row + 1) << level] = 1.0
            means[at + row, row << level : (row + 1) << level] = 0.5**level
        levels.append((level, at, count))
        at += count
    near = np.full((half + 2 * BLOCK, half), FAR, np.float32)
    for query_block in range(half // BLOCK):
        near[
            query_block * BLOCK : (query_block + 3) * BLOCK,
            query_block * BLOCK : (query_block + 1) * BLOCK,
        ] = 0.0
    local_rows = sum(count for level, _, count in levels if level <= local_top)
    coarse = np.full((local_rows + BLOCK * crossing, span), FAR, np.float32)
    for level, start, count in levels:
        if level <= local_top:
            for block in range(count // BLOCK):
                key = start + (block ^ 1) * BLOCK
                query = start + block * BLOCK
                coarse[key : key + BLOCK, query : query + BLOCK] = level
        else:
            key = local_rows + (level - local_top - 1) * BLOCK
            coarse[key : key + BLOCK, start : start + count] = level
    one = coarse[:half, :half]
    rest = coarse[half:, half:]
    twice = lambda table: jnp.asarray(np.concatenate([table, table], axis=1))
    return (
        jnp.asarray(expand, bf16),
        jnp.asarray(means, bf16),
        twice(near),
        twice(one),
        twice(rest),
    )


def call(kernel, outs, ins, scratch=(), limit=32):
    shapes = tuple(jax.ShapeDtypeStruct(shape, f32) for shape in outs)
    return pl.pallas_call(
        kernel,
        out_shape=shapes,
        in_specs=[SMEM if value.dtype == jnp.int32 or value.shape == (2,) else VMEM for value in ins],
        out_specs=tuple(VMEM for _ in outs),
        scratch_shapes=list(scratch),
        compiler_params=pltpu.CompilerParams(vmem_limit_bytes=limit << 20),
    )(*ins)


def feed_call(first, which, fnorm, cot, iw, ib, ow, acc, gacc, block):
    tokens, width = fnorm.shape
    full = pl.BlockSpec((tokens, width), lambda i, w: (0, 0))
    down = pl.BlockSpec((block, width), lambda i, w: (w[0], 0))
    across = pl.BlockSpec((width, block), lambda i, w: (0, w[0]))
    return pl.pallas_call(
        functools.partial(feed_kernel, first),
        grid_spec=pltpu.PrefetchScalarGridSpec(
            num_scalar_prefetch=1,
            grid=(1,),
            in_specs=[
                full, full, across, pl.BlockSpec((1, block), lambda i, w: (0, w[0])), down, full, full,
            ],
            out_specs=[
                pl.BlockSpec((block, width), lambda i, w: (0, 0)),
                pl.BlockSpec((width, block), lambda i, w: (0, 0)),
                pl.BlockSpec((1, block), lambda i, w: (0, 0)),
                full,
                full,
            ],
        ),
        out_shape=[
            jax.ShapeDtypeStruct((block, width), f32),
            jax.ShapeDtypeStruct((width, block), f32),
            jax.ShapeDtypeStruct((1, block), f32),
            jax.ShapeDtypeStruct((tokens, width), f32),
            jax.ShapeDtypeStruct((tokens, width), f32),
        ],
        compiler_params=pltpu.CompilerParams(vmem_limit_bytes=48 << 20),
    )(which, fnorm, cot, iw, ib, ow, acc, gacc)


def pair_mean(values):
    lead = values.shape
    return jnp.mean(values.reshape((lead[0], lead[1] // 2, 2) + lead[2:]), axis=2)


def pair_spread(grads):
    return jnp.repeat(grads, 2, axis=1) * 0.5


def per_device(
    inputs, norm_gain, norm_bias, query_weight, query_bias, key_weight, value_weight, value_bias,
    mixer_weight, mixer_bias, final_gain, final_bias, inner_weight, inner_bias, outer_weight,
    outer_bias, cotangent,
):
    groups, span, width = inputs.shape
    tokens = groups * span
    hidden_width = inner_weight.shape[1]
    seq_index = lax.axis_index("seq")
    seq_count = lax.axis_size("seq")
    crossing = seq_count.bit_length() - 1
    far_rows = BLOCK * crossing
    expand, means, near, one, rest = level_tables(span, crossing)
    row = lambda vec: vec.reshape(1, -1)
    scale = 1.0 / math.sqrt(width // HEADS)
    x = inputs.reshape(tokens, width)
    cot = cotangent.reshape(tokens, width)
    odd = seq_index % 2
    starts = jnp.stack([jnp.where(odd == 1, 0, span - BLOCK), jnp.where(odd == 1, span - BLOCK, 0)])
    starts = starts.astype(jnp.int32)
    edges = jnp.stack(
        [jnp.where(seq_index == 0, FAR, 0.0), jnp.where(seq_index == seq_count - 1, FAR, 0.0)]
    ).astype(f32)
    inner_pairs = [(i, i ^ 1) for i in range(seq_count)]
    outer_pairs = [
        (i, j)
        for i in range(seq_count)
        for j in [i + 1 if i % 2 else i - 1]
        if 0 <= j < seq_count
    ]

    unit, inv, inner_send, outer_send = call(
        functools.partial(first_norm_kernel, groups, span),
        [(tokens, width), (tokens, 1), (groups, 2 * BLOCK, width), (groups, BLOCK, width)],
        [starts, x],
    )
    inner_got = lax.ppermute(inner_send, "seq", inner_pairs)
    outer_got = lax.ppermute(outer_send, "seq", outer_pairs)
    coarse = means.shape[0]
    gain, shift = row(norm_gain), row(norm_bias)
    q, k, v, qc, kc, vc = call(
        functools.partial(project_kernel, groups, span, scale * LOG2E),
        [(tokens, width)] * 3 + [(groups * coarse, width)] * 3,
        [unit, gain, shift, query_weight, row(query_bias), key_weight, value_weight,
         row(value_bias), means],
    )
    halo = jnp.where(
        odd == 1,
        jnp.concatenate([inner_got[:, :BLOCK], outer_got], axis=1),
        jnp.concatenate([outer_got, inner_got[:, :BLOCK]], axis=1),
    ).reshape(groups * 2 * BLOCK, width)
    far_parts = [inner_got[:, BLOCK:]]
    own = inner_send[:, BLOCK:]
    for bit in range(1, crossing):
        lower = seq_index // 2 ** (bit - 1) % 2 == 0
        joined = jnp.where(
            lower,
            jnp.concatenate([own, far_parts[-1]], axis=1),
            jnp.concatenate([far_parts[-1], own], axis=1),
        )
        own = pair_mean(joined)
        far_parts.append(
            lax.ppermute(own, "seq", [(i, i ^ 1 << bit) for i in range(seq_count)])
        )
    far = jnp.concatenate(far_parts, axis=1).reshape(groups * far_rows, width)
    half = span // 2
    num, den, numc, denc, hk, hv = call(
        functools.partial(local_kernel, groups, span),
        [(groups * width, span), (groups * HEADS, span), (groups * width, half),
         (groups * HEADS, half), (groups * 2 * BLOCK, width), (groups * 2 * BLOCK, width)],
        [edges, q, k, v, qc, kc, vc, halo, gain, shift, key_weight, value_weight, row(value_bias),
         near, one],
        [pltpu.VMEM((2,) + near.shape, f32)],
    )
    rk, rv, mixed_t, rden, unit2, inv2, fnorm, acc = call(
        functools.partial(remote_kernel, groups, span),
        [(groups * far_rows, width), (groups * far_rows, width), (groups * width, span),
         (groups * HEADS, span), (tokens, width), (tokens, 1), (tokens, width), (tokens, width)],
        [x, num, den, numc, denc, qc, kc, vc, far, gain, shift, key_weight, value_weight,
         row(value_bias), rest, expand, mixer_weight, row(mixer_bias), row(final_gain),
         row(final_bias), row(outer_bias)],
        [pltpu.VMEM((tokens, width), f32)],
    )
    block = hidden_width // 4
    gow, giw, gib = [], [], []
    gacc = acc
    for index in range(4):
        which = jnp.full((1,), index, jnp.int32)
        one_gow, one_giw, one_gib, acc, gacc = feed_call(
            index == 0, which, fnorm, cot, inner_weight, row(inner_bias), outer_weight, acc, gacc,
            block,
        )
        gow.append(one_gow)
        giw.append(one_giw)
        gib.append(one_gib)
    gmid, gmw, vec_mid, gnum, gnum_t, gden, gnumct, gdenc = call(
        functools.partial(middle_grad_kernel, groups, span),
        [(tokens, width), (width, width), (8, width), (tokens, width), (groups * width, span),
         (groups * HEADS, span), (groups * width, coarse), (groups * HEADS, coarse)],
        [cot, gacc, unit2, inv2, row(final_gain), mixed_t, rden, mixer_weight, expand],
    )
    parts = []
    for group in range(groups):
        cut = lambda value: lax.slice_in_dim(
            value, group * (value.shape[0] // groups), (group + 1) * (value.shape[0] // groups)
        )
        parts.append(
            call(
                functools.partial(pairs_grad_kernel, span),
                [(span, width)] * 3 + [(2 * BLOCK, width)] * 2 + [(far_rows, width)] * 2,
                [edges] + [cut(value) for value in (q, k, v, qc, kc, vc, hk, hv, rk, rv, gnum,
                                                    gnum_t, gden, gnumct, gdenc)]
                + [near, one, rest, means],
                [
                    pltpu.VMEM((2,) + near.shape, f32),
                    pltpu.VMEM((span + 2 * BLOCK, width), f32),
                    pltpu.VMEM((span + 2 * BLOCK, width), f32),
                    pltpu.VMEM((half + rest.shape[0], width), f32),
                    pltpu.VMEM((half + rest.shape[0], width), f32),
                    pltpu.VMEM((width, span), f32),
                    pltpu.VMEM((width, coarse), f32),
                ],
            )
        )
    dq, dk, dv, hdk, hdv, rdk, rdv = [jnp.concatenate(both, axis=0) for both in zip(*parts)]
    outside = jnp.concatenate([halo, far], axis=0)
    gqw, gkw, gvw, vec_first, gnorm, gfar = call(
        functools.partial(project_grad_kernel, scale),
        [(width, width)] * 3 + [(8, width), (tokens, width), outside.shape],
        [unit, outside, gain, shift, dq, dk, dv, jnp.concatenate([hdk, rdk], axis=0),
         jnp.concatenate([hdv, rdv], axis=0), query_weight, key_weight, value_weight],
    )
    ghalo = gfar[: groups * 2 * BLOCK].reshape(groups, 2 * BLOCK, width)
    gfar = gfar[groups * 2 * BLOCK :].reshape(groups, crossing, BLOCK, width)
    low, high = ghalo[:, :BLOCK], ghalo[:, BLOCK:]
    inner_back = jnp.where(odd == 1, low, high)
    outer_back = lax.ppermute(jnp.where(odd == 1, high, low), "seq", outer_pairs)
    grad_own = None
    for bit in range(crossing - 1, -1, -1):
        sent = gfar[:, bit]
        mine = None
        if grad_own is not None:
            wide = pair_spread(grad_own)
            lower = seq_index // 2**bit % 2 == 0
            mine = jnp.where(lower, wide[:, :BLOCK], wide[:, BLOCK:])
            sent = sent + jnp.where(lower, wide[:, BLOCK:], wide[:, :BLOCK])
        if bit == 0:
            sent = jnp.concatenate([inner_back, sent], axis=1)
        got = lax.ppermute(sent, "seq", [(i, i ^ 1 << bit) for i in range(seq_count)])
        if bit == 0:
            inner_back, got = got[:, :BLOCK], got[:, BLOCK:]
        grad_own = got if mine is None else got + mine
    (inputs_grad,) = call(
        functools.partial(first_grad_kernel, groups, span),
        [(tokens, width)],
        [starts, gmid, gnorm, inner_back, outer_back, grad_own, unit, inv, gain],
        [pltpu.VMEM((tokens, width), f32)],
    )
    total = lax.psum(
        (
            vec_first[0], vec_first[1], gqw, vec_first[2], gkw, gvw, vec_first[3], gmw, vec_mid[2],
            vec_mid[0], vec_mid[1], jnp.concatenate(giw, axis=1),
            jnp.concatenate(gib, axis=1).reshape(-1), jnp.concatenate(gow, axis=0), vec_mid[3],
        ),
        ("batch", "seq"),
    )
    return (acc.reshape(inputs.shape), inputs_grad.reshape(inputs.shape)) + tuple(total)


def solution(mesh):
    split_spec = P("batch", "seq", None)
    return jax.shard_map(
        per_device,
        mesh=mesh,
        in_specs=(split_spec,) + (P(),) * 15 + (split_spec,),
        out_specs=(split_spec, split_spec) + (P(),) * 15,
        check_vma=False,
    )
```

```python
import functools
import math
import types

import jax
import jax.numpy as jnp
import numpy as np
from jax import lax
from jax.experimental import pallas as pl
from jax.experimental.pallas import tpu as pltpu
from jax.sharding import PartitionSpec as P

HEADS = 8
BLOCK = 16
LOG2E = 1.4426950408889634
LN2 = 0.6931471805599453
ROOT_HALF = 0.7071067811865476
INV_ROOT_TWO_PI = 0.3989422804014327
EPS = 1e-06
FAR = -1e30
SPARE = 16
TOKEN = (8, 128)
PLAN = (
    "first_norm", "project_qk", "project_v", "coarser", "rest_coarser", "local", "remote",
    "outer0", "outer1", "inner0", "A", "inner1", "middle_grad", "B", "A", "pairs0", "pairs1", "A",
    "rows_grad", "B", "A", "finer", "square0", "finer", "B", "C", "square1", "A", "C", "A", "B",
    "C", "first_grad", "D", "A", "C", "B", "D", "D", "C", "B", "D", "A", "C", "D", "B", "D", "C",
    "B", "D", "write_inner", "write_outer", "C", "D", "write_square0", "write_square1",
)
COST = 10**10
INNER, OUTER, ODD, FIRST, LAST, CORE = range(6)

bf16 = jnp.bfloat16
f32 = jnp.float32
VMEM = pl.BlockSpec(memory_space=pltpu.VMEM)
ANY = pl.BlockSpec(memory_space=pl.ANY)
HBM = pl.BlockSpec(memory_space=pltpu.MemorySpace.HBM)


def split(value):
    high = value.astype(bf16)
    return high, (value - high.astype(f32)).astype(bf16)


def dg(left, right, left_dim=1, right_dim=0):
    return lax.dot_general(
        left, right, (((left_dim,), (right_dim,)), ((), ())), preferred_element_type=f32
    )


def dot3(left, right, left_dim=1, right_dim=0):
    return (
        dg(left[0], right[0], left_dim, right_dim)
        + dg(left[0], right[1], left_dim, right_dim)
        + dg(left[1], right[0], left_dim, right_dim)
    )


def dot2(left, exact, left_dim=1, right_dim=0):
    return dg(left[0], exact, left_dim, right_dim) + dg(left[1], exact, left_dim, right_dim)


def exact_dot2(exact, right, left_dim=1, right_dim=0):
    return dg(exact, right[0], left_dim, right_dim) + dg(exact, right[1], left_dim, right_dim)


def two_diagonal(pair_rows):
    half = pair_rows.shape[0] // 2
    zero = jnp.zeros((half, pair_rows.shape[1]), pair_rows.dtype)
    return jnp.concatenate(
        [
            jnp.concatenate([pair_rows[:half], zero], axis=1),
            jnp.concatenate([zero, pair_rows[half:]], axis=1),
        ],
        axis=0,
    )


def two_masked(pair_lanes):
    half = pair_lanes.shape[1] // 2
    lower = lax.broadcasted_iota(jnp.int32, pair_lanes.shape, 1) < half
    wide = pair_lanes.astype(f32)
    return jnp.concatenate(
        [jnp.where(lower, wide, 0.0), jnp.where(lower, 0.0, wide)], axis=0
    ).astype(bf16)


def take_diagonal(product):
    half, width = product.shape[0] // 2, product.shape[1] // 2
    return jnp.concatenate([product[:half, :width], product[half:, width:]], axis=0)


def pair_weights(keys, queries_t, bias):
    diag_high, diag_low = two_diagonal(queries_t[0]), two_diagonal(queries_t[1])
    scores = dg(
        jnp.concatenate([keys[0], keys[1], keys[0]], axis=1),
        jnp.concatenate([diag_high, diag_high, diag_low], axis=0),
    )
    return jnp.exp2(scores + bias)


def tile_forward(keys, values_t, queries_t, bias):
    weights = pair_weights(keys, queries_t, bias)
    denominator = jnp.sum(weights, axis=0, keepdims=True)
    high, low = split(weights)
    wide = dg(jnp.concatenate([values_t[0], values_t[1]], axis=0), high)
    size = values_t[0].shape[0]
    product = wide[:size] + wide[size:] + dg(values_t[0], low)
    width = denominator.shape[1] // 2
    return (
        take_diagonal(product),
        jnp.concatenate([denominator[:, :width], denominator[:, width:]], axis=0),
    )


def tile_backward(keys, keys_t, values, queries_t, queries_m, grads_t, grads_m, grad_den, bias):
    weights = pair_weights(keys, queries_t, bias)
    diag_high, diag_low = two_diagonal(grads_t[0]), two_diagonal(grads_t[1])
    grad_weights = (
        dg(
            jnp.concatenate([values[0], values[1], values[0]], axis=1),
            jnp.concatenate([diag_high, diag_high, diag_low], axis=0),
        )
        + grad_den
    )
    scores = split(weights * grad_weights)
    weights = split(weights)

    def gather(pairs, masked):
        wide = dg(pairs[0], jnp.concatenate([masked[0], masked[1]], axis=1))
        half = wide.shape[1] // 2
        return wide[:, :half] + wide[:, half:] + dg(pairs[1], masked[0])

    grad_values = gather(weights, grads_m)
    grad_keys = gather(scores, queries_m)
    wide = dg(jnp.concatenate([keys_t[0], keys_t[1]], axis=0), scores[0])
    size = keys_t[0].shape[0]
    product = wide[:size] + wide[size:] + dg(keys_t[0], scores[1])
    return take_diagonal(product), grad_keys, grad_values


def lanes(parts, start, size):
    return tuple(part[:, start : start + size] for part in parts)


def rows(parts, start, size):
    return tuple(part[start : start + size] for part in parts)


def block_of(parts, row, row_size, lane, lane_size):
    return tuple(part[row : row + row_size, lane : lane + lane_size] for part in parts)


def stack(first, second):
    return tuple(jnp.concatenate([one, two], axis=0) for one, two in zip(first, second))


def norm_rows(values):
    center = values - jnp.mean(values, axis=-1, keepdims=True)
    inverse = lax.rsqrt(jnp.mean(center * center, axis=-1, keepdims=True) + EPS)
    return center * inverse, inverse


def norm_grad(grad_rows, unit_rows, inverse, gain):
    grad_unit = grad_rows * gain
    return inverse * (
        grad_unit
        - jnp.mean(grad_unit, axis=-1, keepdims=True)
        - unit_rows * jnp.mean(grad_unit * unit_rows, axis=-1, keepdims=True)
    )


def first_norm_kernel(groups, span, place_ref, x_ref, unit_ref, inv_ref, inner_ref, outer_ref):
    width = x_ref.shape[-1]
    for group in range(groups):
        own = slice(group * span, (group + 1) * span)
        unit, inverse = norm_rows(x_ref[own, :])
        unit_ref[own, :] = unit
        inv_ref[own, :] = inverse
        runs = span // BLOCK
        inner_ref[group, BLOCK:, :] = jnp.mean(unit.reshape(BLOCK, runs, width), axis=1)
        inner_start = pl.multiple_of(group * span + place_ref[INNER], BLOCK)
        outer_start = pl.multiple_of(group * span + place_ref[OUTER], BLOCK)
        inner_ref[group, :BLOCK, :] = unit_ref[pl.ds(inner_start, BLOCK), :]
        outer_ref[group] = unit_ref[pl.ds(outer_start, BLOCK), :]


def project_kernel(groups, span, scales, unit_ref, gain_ref, shift_ref, mean_ref, *refs):
    count = len(scales)
    weights, refs = refs[:count], refs[count:]
    biased = [scale is not None for scale in scales]
    biases, outs = list(refs[: sum(biased)]), refs[sum(biased) :]
    normed = split(unit_ref[...] * gain_ref[...] + shift_ref[...])
    means = mean_ref[...]
    coarse = means.shape[0]
    for index, (weight, scale) in enumerate(zip(weights, scales)):
        result = dot3(normed, split(weight[...]))
        if scale is not None:
            result = result + biases.pop(0)[...]
            if scale != 1.0:
                result = result * scale
        outs[2 * index][...] = result
        for group in range(groups):
            part = split(result[group * span : (group + 1) * span])
            outs[2 * index + 1][group * coarse : (group + 1) * coarse, :] = exact_dot2(means, part)


def fill_bias(bias_ref, near_ref, place_ref):
    rows_total = near_ref.shape[0]
    bias_ref[0] = near_ref[...]
    bias_ref[1] = near_ref[...]
    before = place_ref[FIRST].astype(f32) * FAR
    after = place_ref[LAST].astype(f32) * FAR
    bias_ref[0, :BLOCK, :] = near_ref[:BLOCK, :] + before
    bias_ref[1, rows_total - BLOCK :, :] = near_ref[rows_total - BLOCK :, :] + after


def local_kernel(
    groups, span, place_ref, q_ref, k_ref, v_ref, qc_ref, kc_ref, vc_ref, inner_ref, outer_ref,
    gain_ref, shift_ref, kw_ref, vw_ref, vb_ref, near_ref, one_ref,
    num_ref, den_ref, numc_ref, denc_ref, halo_ref, hk_ref, hv_ref, bias_ref,
):
    width = q_ref.shape[-1]
    half = span // 2
    coarse = qc_ref.shape[0] // groups
    pairs = HEADS // 2
    pair_width = width // pairs
    tile_keys = half + 2 * BLOCK
    fill_bias(bias_ref, near_ref, place_ref)
    odd = place_ref[ODD].astype(f32)
    for group in range(groups):
        inner, outer = inner_ref[group, :BLOCK, :], outer_ref[group]
        at = group * 2 * BLOCK
        halo_ref[at : at + BLOCK, :] = inner * odd + outer * (1.0 - odd)
        halo_ref[at + BLOCK : at + 2 * BLOCK, :] = inner * (1.0 - odd) + outer * odd
    normed = split(halo_ref[...] * gain_ref[...] + shift_ref[...])
    halo_keys = dot3(normed, split(kw_ref[...]))
    halo_values = dot3(normed, split(vw_ref[...])) + vb_ref[...]
    hk_ref[...] = halo_keys
    hv_ref[...] = halo_values
    for group in range(groups):
        own = slice(group * span, (group + 1) * span)
        left = slice(group * 2 * BLOCK, group * 2 * BLOCK + BLOCK)
        right = slice(group * 2 * BLOCK + BLOCK, (group + 1) * 2 * BLOCK)
        own_c = slice(group * coarse, group * coarse + half)
        keys = split(jnp.concatenate([halo_keys[left], k_ref[own, :], halo_keys[right]], axis=0))
        values = jnp.concatenate([halo_values[left], v_ref[own, :], halo_values[right]], axis=0)
        values_t = split(values.T)
        queries_t = split(q_ref[own, :].T)
        keys_c = split(kc_ref[own_c, :])
        values_ct = split(vc_ref[own_c, :].T)
        queries_ct = split(qc_ref[own_c, :].T)
        for pair in range(pairs):
            at = pair * pair_width
            out = slice(group * width + at, group * width + at + pair_width)
            heads = slice((group * pairs + pair) * 2, (group * pairs + pair) * 2 + 2)
            for tile in range(2):
                num, den = tile_forward(
                    block_of(keys, tile * half, tile_keys, at, pair_width),
                    block_of(values_t, at, pair_width, tile * half, tile_keys),
                    block_of(queries_t, at, pair_width, tile * half, half),
                    bias_ref[tile],
                )
                num_ref[out, tile * half : (tile + 1) * half] = num
                den_ref[heads, tile * half : (tile + 1) * half] = den
            num, den = tile_forward(
                lanes(keys_c, at, pair_width),
                rows(values_ct, at, pair_width),
                rows(queries_ct, at, pair_width),
                one_ref[...],
            )
            numc_ref[out, :] = num
            denc_ref[heads, :] = den


def remote_kernel(
    groups, span, crossing, *refs
):
    far_parts, refs = refs[:crossing], refs[crossing:]
    (
        x_ref, num_ref, den_ref, numc_ref, denc_ref, qc_ref, kc_ref, vc_ref, gain_ref, shift_ref,
        kw_ref, vw_ref, vb_ref, rest_ref, expand_ref, mw_ref, mb_ref, fgain_ref, fshift_ref, ob_ref,
        cot_ref,
        far_ref, rk_ref, rv_ref, mixed_ref, rden_ref, unit_ref, inv_ref, acc_ref, fhigh_ref, flow_ref,
        chigh_ref, clow_ref, mid_ref,
    ) = refs
    width = x_ref.shape[-1]
    half = span // 2
    coarse = qc_ref.shape[0] // groups
    far = far_ref.shape[0] // groups
    pairs = HEADS // 2
    pair_width = width // pairs
    head_width = width // HEADS
    local_rest = rest_ref.shape[0] - far
    for group in range(groups):
        for level, part in enumerate(far_parts):
            at = group * far + level * BLOCK
            far_ref[at : at + BLOCK, :] = part[group, part.shape[1] - BLOCK :, :]
    normed = split(far_ref[...] * gain_ref[...] + shift_ref[...])
    far_keys = dot3(normed, split(kw_ref[...]))
    far_values = dot3(normed, split(vw_ref[...])) + vb_ref[...]
    rk_ref[...] = far_keys
    rv_ref[...] = far_values
    expand = expand_ref[...]
    for group in range(groups):
        rest = slice(group * coarse + half, group * coarse + half + local_rest)
        remote = slice(group * far, (group + 1) * far)
        keys = split(jnp.concatenate([kc_ref[rest, :], far_keys[remote]], axis=0))
        values_t = split(jnp.concatenate([vc_ref[rest, :], far_values[remote]], axis=0).T)
        queries_t = split(qc_ref[group * coarse + half : (group + 1) * coarse, :].T)
        nums, dens = [], []
        for pair in range(pairs):
            at = pair * pair_width
            num, den = tile_forward(
                lanes(keys, at, pair_width),
                rows(values_t, at, pair_width),
                rows(queries_t, at, pair_width),
                rest_ref[...],
            )
            nums.append(num)
            dens.append(den)
        own_t = slice(group * width, (group + 1) * width)
        own_h = slice(group * HEADS, (group + 1) * HEADS)
        numc = jnp.concatenate([numc_ref[own_t, :], jnp.concatenate(nums, axis=0)], axis=1)
        denc = jnp.concatenate([denc_ref[own_h, :], jnp.concatenate(dens, axis=0)], axis=1)
        num = num_ref[own_t, :] + dot2(split(numc), expand)
        den = den_ref[own_h, :] + dot2(split(denc), expand)
        inverse = 1.0 / den
        rden_ref[own_h, :] = inverse
        spread = jnp.concatenate(
            [
                jnp.broadcast_to(inverse[head : head + 1], (head_width, span))
                for head in range(HEADS)
            ],
            axis=0,
        )
        mixed_t = num * spread
        own = slice(group * span, (group + 1) * span)
        mixed_ref[own_t, :] = mixed_t
        mid_ref[own, :] = mixed_t.T
    middle = x_ref[...] + dot3(split(mid_ref[...]), split(mw_ref[...])) + mb_ref[...]
    unit, inverse = norm_rows(middle)
    unit_ref[...] = unit
    inv_ref[...] = inverse
    fhigh_ref[...], flow_ref[...] = split(unit * fgain_ref[...] + fshift_ref[...])
    chigh_ref[...], clow_ref[...] = split(cot_ref[...])
    acc_ref[...] = middle + ob_ref[...]


def half_of(own, place_ref, size):
    side = place_ref[CORE] if own else 1 - place_ref[CORE]
    return pl.ds(pl.multiple_of(side * size, size), size)


def outer_kernel(
    own, place_ref, fhigh_ref, flow_ref, chigh_ref, clow_ref, iw_ref, ib_ref,
    joint_ref, hhigh_ref, hlow_ref, slope_ref,
):
    units = half_of(own, place_ref, slope_ref.shape[1])
    inner = dot3((fhigh_ref[...], flow_ref[...]), split(iw_ref[:, units])) + ib_ref[:, units]
    cumulative = 0.5 * (1.0 + lax.erf(inner * ROOT_HALF))
    hidden = split(inner * cumulative)
    slope_ref[...] = cumulative + inner * jnp.exp(-0.5 * inner * inner) * INV_ROOT_TWO_PI
    hhigh_ref[...], hlow_ref[...] = hidden
    joint_ref[...] = dot3(hidden, (chigh_ref[...], clow_ref[...]), 0, 0)


def inner_kernel(
    own, place_ref, fhigh_ref, flow_ref, chigh_ref, clow_ref, hhigh_ref, hlow_ref, slope_ref,
    iw_ref, ow_ref, acc_ref, *refs
):
    giw_ref, gib_ref, nacc_ref, ngacc_ref = refs[-4:]
    units = half_of(own, place_ref, slope_ref.shape[1])
    cot = chigh_ref[...], clow_ref[...]
    hidden = hhigh_ref[...], hlow_ref[...]
    iw, ow = split(iw_ref[:, units]), split(ow_ref[units, :])
    grad_inner = dot3(cot, ow, 1, 1) * slope_ref[...]
    gib_ref[...] = jnp.sum(grad_inner, axis=0, keepdims=True)
    grad_inner = split(grad_inner)
    giw = dot3((fhigh_ref[...], flow_ref[...]), grad_inner, 0, 0)
    width = giw.shape[0]
    giw_ref[:width, :] = giw[:, :width]
    giw_ref[width:, :] = giw[:, width:]
    nacc_ref[...] = acc_ref[...] + dot3(hidden, ow)
    grad_fnorm = dot3(grad_inner, iw, 1, 1)
    ngacc_ref[...] = refs[0][...] + grad_fnorm if own else grad_fnorm


def middle_grad_kernel(
    groups, span, cot_ref, gf_ref, unit_ref, inv_ref, fgain_ref, mixed_ref, rden_ref, mw_ref,
    expand_ref,
    gmid_ref, gmw_ref, vec_ref, gnum_ref, gnumt_ref, gden_ref, gnumct_ref, gdenc_ref,
):
    width = cot_ref.shape[-1]
    head_width = width // HEADS
    cot = cot_ref[...]
    gf = gf_ref[...]
    unit = unit_ref[...]
    gmid = cot + norm_grad(gf, unit, inv_ref[...], fgain_ref[...])
    gmid_ref[...] = gmid
    vec_ref[0:1, :] = jnp.sum(gf * unit, axis=0, keepdims=True)
    vec_ref[1:2, :] = jnp.sum(gf, axis=0, keepdims=True)
    vec_ref[2:3, :] = jnp.sum(gmid, axis=0, keepdims=True)
    vec_ref[3:4, :] = jnp.sum(cot, axis=0, keepdims=True)
    gmid = split(gmid)
    expand = expand_ref[...]
    grad_mixed = dot3(gmid, split(mw_ref[...]), 1, 1)
    total = None
    for group in range(groups):
        own = slice(group * span, (group + 1) * span)
        own_t = slice(group * width, (group + 1) * width)
        own_h = slice(group * HEADS, (group + 1) * HEADS)
        mixed_t = mixed_ref[own_t, :]
        part = dot3(split(mixed_t), rows(gmid, group * span, span))
        total = part if total is None else total + part
        grad_t = grad_mixed[own].T
        inverse = rden_ref[own_h, :]
        spread = jnp.concatenate(
            [
                jnp.broadcast_to(inverse[head : head + 1], (head_width, span))
                for head in range(HEADS)
            ],
            axis=0,
        )
        product = grad_t * mixed_t
        dens = jnp.concatenate(
            [
                jnp.sum(product[head * head_width : (head + 1) * head_width], axis=0, keepdims=True)
                for head in range(HEADS)
            ],
            axis=0,
        )
        gden = -dens * inverse
        gnum_t = grad_t * spread
        gnumt_ref[own_t, :] = gnum_t
        gnum_ref[own, :] = gnum_t.T
        gden_ref[own_h, :] = gden
        gnumct_ref[own_t, :] = dot2(split(gnum_t), expand, 1, 1)
        gdenc_ref[own_h, :] = dot2(split(gden), expand, 1, 1)
    gmw_ref[...] = total


def pairs_grad_kernel(
    groups, part, span, place_ref, q_ref, k_ref, v_ref, qc_ref, kc_ref, vc_ref, hk_ref, hv_ref,
    rk_ref, rv_ref, gnum_ref, gnumt_ref, gden_ref, gnumct_ref, gdenc_ref, near_ref, one_ref,
    rest_ref, mean_ref,
    dq_ref, dk_ref, dv_ref, odk_ref, odv_ref,
    bias_ref, dkx_ref, dvx_ref, dkc_ref, dvc_ref, dqt_ref, dqct_ref,
):
    full = q_ref.shape[-1]
    width = full // 2
    half = span // 2
    coarse = qc_ref.shape[0] // groups
    far = rk_ref.shape[0] // groups
    pairs = HEADS // 4
    pair_width = width // pairs
    tile_keys = half + 2 * BLOCK
    local_rest = rest_ref.shape[0] - far
    local_coarse = half + local_rest
    rest_keys = local_rest + far
    ours = slice(part * width, (part + 1) * width)
    fill_bias(bias_ref, near_ref, place_ref)
    means = mean_ref[...]
    zero = jnp.zeros((coarse - local_coarse, width), f32)
    for group in range(groups):
        fine = slice(group * span, (group + 1) * span)
        rough = slice(group * coarse, group * coarse + coarse)
        near_rough = slice(group * coarse, group * coarse + local_coarse)
        left = slice(group * 2 * BLOCK, group * 2 * BLOCK + BLOCK)
        right = slice(group * 2 * BLOCK + BLOCK, (group + 1) * 2 * BLOCK)
        remote = slice(group * far, (group + 1) * far)
        ours_t = slice(group * full + part * width, group * full + (part + 1) * width)
        keys_f = jnp.concatenate(
            [hk_ref[left, ours], k_ref[fine, ours], hk_ref[right, ours]], axis=0
        )
        keys, keys_t = split(keys_f), split(keys_f.T)
        values = split(
            jnp.concatenate([hv_ref[left, ours], v_ref[fine, ours], hv_ref[right, ours]], axis=0)
        )
        q = q_ref[fine, ours]
        queries, queries_t = split(q), split(q.T)
        grads, grads_t = split(gnum_ref[fine, ours]), split(gnumt_ref[ours_t, :])
        keys_cf = jnp.concatenate([kc_ref[near_rough, ours], rk_ref[remote, ours]], axis=0)
        keys_c, keys_ct = split(keys_cf), split(keys_cf.T)
        values_c = split(
            jnp.concatenate([vc_ref[near_rough, ours], rv_ref[remote, ours]], axis=0)
        )
        qc = qc_ref[rough, ours]
        queries_c, queries_ct = split(qc), split(qc.T)
        gnumct = gnumct_ref[ours_t, :]
        grads_c, grads_ct = split(gnumct.T), split(gnumct)
        for pair in range(pairs):
            at = pair * pair_width
            cols = slice(at, at + pair_width)
            head = group * HEADS + part * (HEADS // 2) + 2 * pair

            def den_rows(ref, start):
                both = ref[head : head + 2, start : start + half]
                return jnp.concatenate([both[0:1], both[1:2]], axis=1)

            def masked(parts, start):
                return tuple(
                    two_masked(value) for value in block_of(parts, start, half, at, pair_width)
                )

            for tile in range(2):
                start = tile * half
                dq, dk, dv = tile_backward(
                    block_of(keys, start, tile_keys, at, pair_width),
                    block_of(keys_t, at, pair_width, start, tile_keys),
                    block_of(values, start, tile_keys, at, pair_width),
                    block_of(queries_t, at, pair_width, start, half),
                    masked(queries, start),
                    block_of(grads_t, at, pair_width, start, half),
                    masked(grads, start),
                    den_rows(gden_ref, start),
                    bias_ref[tile],
                )
                dqt_ref[cols, start : start + half] = dq
                if tile == 0:
                    dkx_ref[:tile_keys, cols] = dk
                    dvx_ref[:tile_keys, cols] = dv
                else:
                    shared = slice(start, start + 2 * BLOCK)
                    fresh = slice(start + 2 * BLOCK, start + tile_keys)
                    dkx_ref[shared, cols] = dkx_ref[shared, cols] + dk[: 2 * BLOCK]
                    dvx_ref[shared, cols] = dvx_ref[shared, cols] + dv[: 2 * BLOCK]
                    dkx_ref[fresh, cols] = dk[2 * BLOCK :]
                    dvx_ref[fresh, cols] = dv[2 * BLOCK :]
            for start, count, bias in ((0, half, one_ref), (half, rest_keys, rest_ref)):
                dq, dk, dv = tile_backward(
                    block_of(keys_c, start, count, at, pair_width),
                    block_of(keys_ct, at, pair_width, start, count),
                    block_of(values_c, start, count, at, pair_width),
                    block_of(queries_ct, at, pair_width, start, half),
                    masked(queries_c, start),
                    block_of(grads_ct, at, pair_width, start, half),
                    masked(grads_c, start),
                    den_rows(gdenc_ref, start),
                    bias[...],
                )
                dqct_ref[cols, start : start + half] = dq
                dkc_ref[start : start + count, cols] = dk
                dvc_ref[start : start + count, cols] = dv
        distant = slice(
            groups * 2 * BLOCK + group * far, groups * 2 * BLOCK + (group + 1) * far
        )
        odk_ref[distant, :] = dkc_ref[local_coarse:, :] * LN2
        odv_ref[distant, :] = dvc_ref[local_coarse:, :]
        odk_ref[left, :] = dkx_ref[:BLOCK, :] * LN2
        odk_ref[right, :] = dkx_ref[span + BLOCK :, :] * LN2
        odv_ref[left, :] = dvx_ref[:BLOCK, :]
        odv_ref[right, :] = dvx_ref[span + BLOCK :, :]

        def spread(ref):
            local = jnp.concatenate([ref[:local_coarse, :], zero], axis=0)
            return exact_dot2(means, split(local), 0, 0)

        dk_ref[fine, :] = (dkx_ref[BLOCK : span + BLOCK, :] + spread(dkc_ref)) * LN2
        dv_ref[fine, :] = dvx_ref[BLOCK : span + BLOCK, :] + spread(dvc_ref)
        dq_ref[fine, :] = (dqt_ref[...] + dot2(split(dqct_ref[...]), means)).T


def square_grad_kernel(
    part, scale, place_ref, unit_ref, halo_ref, far_ref, gain_ref, shift_ref, gmw_ref,
    dq_ref, dk_ref, dv_ref, odk_ref, odv_ref, own_ref, send_ref, full_ref,
):
    width = unit_ref.shape[-1]
    half = width // 2
    core = place_ref[CORE]
    mine = pl.ds(pl.multiple_of(core * half, half), half)
    other = pl.ds(pl.multiple_of((1 - core) * half, half), half)
    outside = jnp.concatenate([halo_ref[...], far_ref[...]], axis=0)
    normed = split(unit_ref[...] * gain_ref[...] + shift_ref[...])
    normed_out = split(outside * gain_ref[...] + shift_ref[...])
    full_ref[0] = dot3(normed, split(dq_ref[...] * scale), 0, 0)
    full_ref[1] = dot3(normed, split(dk_ref[...]), 0, 0) + dot3(
        normed_out, split(odk_ref[...]), 0, 0
    )
    full_ref[2] = dot3(normed, split(dv_ref[...]), 0, 0) + dot3(
        normed_out, split(odv_ref[...]), 0, 0
    )
    for target, at in ((own_ref, mine), (send_ref, other)):
        target[:half, :half] = full_ref[0, at, :]
        target[:half, half:] = full_ref[1, at, :]
        target[half:, :half] = full_ref[2, at, :]
        target[half:, half:] = gmw_ref[at, part * half : (part + 1) * half]


def rows_grad_kernel(groups, crossing, scale, place_ref, unit_ref, halo_ref, far_ref, *refs):
    parts, refs = (refs[:5], refs[5:10]), refs[10:]
    qw_ref, kw_ref, vw_ref, mid_ref = refs[:4]
    gib_refs, refs = refs[4:6], refs[6:]
    vec_ref, gnorm_ref, inner_ref, outer_ref = refs[:4]
    gfar_refs = refs[4:]
    joined = lambda index: jnp.concatenate([part[index][...] for part in parts], axis=1)
    width = unit_ref.shape[-1]
    unit = unit_ref[...]
    outside = jnp.concatenate([halo_ref[...], far_ref[...]], axis=0)
    dq_f, dv_f, odv_f = joined(0) * scale, joined(2), joined(4)
    dq, dk, dv = split(dq_f), split(joined(1)), split(dv_f)
    odk, odv = split(joined(3)), split(odv_f)
    qw, kw, vw = split(qw_ref[...]), split(kw_ref[...]), split(vw_ref[...])
    gnorm = dot3(dq, qw, 1, 1) + dot3(dk, kw, 1, 1) + dot3(dv, vw, 1, 1)
    gout = dot3(odk, kw, 1, 1) + dot3(odv, vw, 1, 1)
    gnorm_ref[...] = gnorm
    odd = place_ref[ODD].astype(f32)
    far = far_ref.shape[0] // groups
    for group in range(groups):
        at = group * 2 * BLOCK
        low, high = gout[at : at + BLOCK], gout[at + BLOCK : at + 2 * BLOCK]
        inner_ref[group] = low * odd + high * (1.0 - odd)
        outer_ref[group] = low * (1.0 - odd) + high * odd
        for level, gfar_ref in enumerate(gfar_refs):
            at = groups * 2 * BLOCK + group * far + level * BLOCK
            gfar_ref[group] = gout[at : at + BLOCK]
    first = place_ref[CORE].astype(f32)
    other_gib, own_gib = gib_refs[0][...], gib_refs[1][...]
    low_gib = own_gib * (1.0 - first) + other_gib * first
    high_gib = own_gib * first + other_gib * (1.0 - first)
    vec_ref[...] = jnp.concatenate(
        [
            jnp.sum(gnorm * unit, axis=0, keepdims=True)
            + jnp.sum(gout * outside, axis=0, keepdims=True),
            jnp.sum(gnorm, axis=0, keepdims=True) + jnp.sum(gout, axis=0, keepdims=True),
            jnp.sum(dq_f, axis=0, keepdims=True),
            jnp.sum(dv_f, axis=0, keepdims=True) + jnp.sum(odv_f, axis=0, keepdims=True),
            mid_ref[0:4, :],
            low_gib[:, :width],
            low_gib[:, width:],
            high_gib[:, :width],
            high_gib[:, width:],
            jnp.zeros((SPARE - 12, width), f32),
        ],
        axis=0,
    )


def first_grad_kernel(
    groups, span, place_ref, gmid_ref, gnorm_ref, got_ref, mine_ref, outer_ref, unit_ref, inv_ref,
    gain_ref, out_ref, total_ref,
):
    width = gmid_ref.shape[-1]
    runs = span // BLOCK
    for group in range(groups):
        own = slice(group * span, (group + 1) * span)
        four = (got_ref[group, BLOCK:, :] + mine_ref[group]) * (1.0 / runs)
        spread = jnp.broadcast_to(four.reshape(BLOCK, 1, width), (BLOCK, runs, width)).reshape(
            span, width
        )
        total_ref[own, :] = gnorm_ref[own, :] + spread
        inner_at = pl.ds(pl.multiple_of(group * span + place_ref[INNER], BLOCK), BLOCK)
        outer_at = pl.ds(pl.multiple_of(group * span + place_ref[OUTER], BLOCK), BLOCK)
        total_ref[inner_at, :] = total_ref[inner_at, :] + got_ref[group, :BLOCK, :]
        total_ref[outer_at, :] = total_ref[outer_at, :] + outer_ref[group]
    out_ref[...] = gmid_ref[...] + norm_grad(
        total_ref[...], unit_ref[...], inv_ref[...], gain_ref[...]
    )


def pair_matrix(few, many):
    row_ids = lax.broadcasted_iota(jnp.int32, (few, many), 0)
    col_ids = lax.broadcasted_iota(jnp.int32, (few, many), 1)
    return jnp.where(col_ids // 2 == row_ids, 0.5, 0.0).astype(bf16)


def coarser_kernel(slot, place_ref, own_ref, got_ref, out_ref):
    half = BLOCK // 2
    bit = place_ref[slot]
    matrix = pair_matrix(half, BLOCK)
    for ref, at in ((own_ref, bit), (got_ref, 1 - bit)):
        start = ref.shape[1] - BLOCK
        at = pl.multiple_of(at * half, half)
        for group in range(ref.shape[0]):
            out_ref[group, pl.ds(at, half), :] = exact_dot2(
                matrix, split(ref[group, start:, :])
            )


def finer_kernel(slot, with_rim, passing, place_ref, *refs):
    wide_ref, refs = refs[-1], refs[:-1]
    if passing:
        refs[-1][...] = refs[0][...]
        refs = refs[1:-1]
    mine_ref, send_ref = refs[-2:]
    *sums, part_ref = refs[: -2 - with_rim]
    half = BLOCK // 2
    bit = place_ref[slot]
    offset = send_ref.shape[1] - BLOCK
    matrix = pair_matrix(half, BLOCK)
    for group in range(mine_ref.shape[0]):
        if with_rim:
            send_ref[group, :BLOCK, :] = refs[-3][group]
        wide = sums[0][group]
        for other in sums[1:]:
            wide = wide + other[group]
        wide_ref[...] = wide

        def handed(at):
            at = pl.ds(pl.multiple_of(at * half, half), half)
            return exact_dot2(matrix, split(wide_ref[at, :]), 0, 0)

        mine_ref[group] = handed(bit)
        send_ref[group, offset:, :] = handed(1 - bit) + part_ref[group]


def fold_kernel(slot, size, extra, place_ref, keep_ref, got_ref, *refs):
    if extra == "fresh":
        fresh_ref, refs = refs[0], refs[1:]
    if slot is None:
        refs[0][...] = keep_ref[:size, :] + got_ref[:size, :]
        if extra:
            refs[1][...] = keep_ref[size:, :] + got_ref[size:, :]
        return
    half = size // 2
    bit = place_ref[slot]
    for target, side in zip(refs, (bit, 1 - bit)):
        at = pl.ds(pl.multiple_of(side * half, half), half)
        target[:half, :] = keep_ref[at, :] + got_ref[at, :]
        if extra == "fresh":
            target[half:, :] = fresh_ref[...]
        elif extra:
            target[half:, :] = keep_ref[size:, :] + got_ref[size:, :]


def share_kernel(size, extra, place_ref, keep_ref, got_ref, *refs):
    keep, send = refs
    keep[...] = keep_ref[...] + got_ref[...]
    send[...] = keep[...]


def join_kernel(slot, place_ref, own_ref, got_ref, *refs):
    out_ref = refs[-1]
    half = own_ref.shape[0]
    bit = place_ref[slot]
    for source, side in ((own_ref, bit), (got_ref, 1 - bit)):
        out_ref[pl.ds(pl.multiple_of(side * half, half), half), :] = source[...]
    if len(refs) == 2:
        out_ref[2 * half :, :] = refs[0][...]


def run_copies(copies, sems):
    copies = [
        pltpu.make_async_copy(source, target, sems.at[index])
        for index, (source, target) in enumerate(copies)
    ]
    for copy in copies:
        copy.start()
    for copy in copies:
        copy.wait()


def place_outer_kernel(place_ref, own_ref, sib_ref, out_ref, sems):
    core, size = place_ref[CORE], own_ref.shape[0]
    run_copies(
        [
            (source, out_ref.at[pl.ds(pl.multiple_of(side * size, size), size), :])
            for source, side in ((own_ref, core), (sib_ref, 1 - core))
        ],
        sems,
    )


def place_inner_kernel(place_ref, own_ref, sib_ref, out_ref, sems):
    core, size = place_ref[CORE], out_ref.shape[0]
    copies = []
    for source, side in ((own_ref, core), (sib_ref, 1 - core)):
        for index in range(2):
            at = pl.ds(pl.multiple_of((side * 2 + index) * size, size), size)
            copies.append((source.at[index * size : (index + 1) * size, :], out_ref.at[:, at]))
    run_copies(copies, sems)


def place_square_kernel(part, place_ref, own_ref, sib_ref, *refs):
    *outs, sems = refs[-5:]
    half = outs[0].shape[0] // 2
    core = place_ref[CORE]
    copies = []
    for slot, out_ref in enumerate(outs):
        down, across = slot // 2 * half, slot % 2 * half
        for source, side in ((own_ref, core), (sib_ref, 1 - core)):
            at = pl.ds(pl.multiple_of(side * half, half), half)
            copies.append(
                (
                    source.at[down : down + half, across : across + half],
                    out_ref.at[at, part * half : (part + 1) * half],
                )
            )
    run_copies(copies, sems)


def vectors_kernel(own_ref, sib_ref, *outs):
    last = own_ref.shape[0] - SPARE
    vec_ref = own_ref[last:, :] + sib_ref[last:, :]
    for index, out in enumerate(outs):
        if index < 8:
            out[...] = vec_ref[index : index + 1, :]
        else:
            width = vec_ref.shape[-1]
            for part in range(4):
                out[:, part * width : (part + 1) * width] = vec_ref[8 + part : 9 + part, :]


def level_tables(span, crossing):
    half = span // 2
    top = int(math.log2(span // BLOCK // 2)) + crossing
    local_top = top - crossing
    expand = np.zeros((span, span), np.float32)
    means = np.zeros((span, span), np.float32)
    levels, at = [], 0
    for level in range(1, top + 1):
        count = span >> level
        for row in range(count):
            expand[at + row, row << level : (row + 1) << level] = 1.0
            means[at + row, row << level : (row + 1) << level] = 0.5**level
        levels.append((level, at, count))
        at += count
    near = np.full((half + 2 * BLOCK, half), FAR, np.float32)
    for query_block in range(half // BLOCK):
        near[
            query_block * BLOCK : (query_block + 3) * BLOCK,
            query_block * BLOCK : (query_block + 1) * BLOCK,
        ] = 0.0
    local_rows = sum(count for level, _, count in levels if level <= local_top)
    coarse = np.full((local_rows + BLOCK * crossing, span), FAR, np.float32)
    for level, start, count in levels:
        if level <= local_top:
            for block in range(count // BLOCK):
                key = start + (block ^ 1) * BLOCK
                query = start + block * BLOCK
                coarse[key : key + BLOCK, query : query + BLOCK] = level
        else:
            key = local_rows + (level - local_top - 1) * BLOCK
            coarse[key : key + BLOCK, start : start + count] = level
    one = coarse[:half, :half]
    rest = coarse[half:, half:]
    twice = lambda table: jnp.asarray(np.concatenate([table, table], axis=1))
    return (
        jnp.asarray(expand, bf16),
        jnp.asarray(means, bf16),
        twice(near),
        twice(one),
        twice(rest),
    )


class Here:
    def __init__(self, span, seq_count, steps):
        self.span, self.seq_count, self.steps = span, seq_count, steps

    def __getitem__(self, slot):
        seq, batch = lax.axis_index("seq"), lax.axis_index("batch")
        odd, core = seq & 1, batch & 1
        if slot == INNER:
            return (1 - odd) * (self.span - BLOCK)
        if slot == OUTER:
            return odd * (self.span - BLOCK)
        if slot == ODD:
            return odd
        if slot == FIRST:
            return (seq == 0).astype(jnp.int32)
        if slot == LAST:
            return (seq == self.seq_count - 1).astype(jnp.int32)
        if slot == CORE:
            return core
        slot -= CORE + 1
        crossing = self.seq_count.bit_length() - 1
        if slot < crossing:
            return seq >> slot & 1
        sides = [(batch, seq)[axis] >> bit & 1 for axis, bit in self.steps[slot - crossing]]
        return sides[0] + core * (sides[1] - sides[0])


class Order:
    def __init__(self):
        self.last = None

    def call(self, kernel, outs, ins, tag="", scratch=(), limit=8, spaces=None, out_space=VMEM,
             aliases=None):
        shapes = tuple(
            shape if isinstance(shape, jax.ShapeDtypeStruct) else jax.ShapeDtypeStruct(shape, f32)
            for shape in outs
        )
        spaces, aliases = spaces or {}, aliases or {}
        given = [index for index, value in enumerate(ins) if not isinstance(value, Here)]
        count, before = len(given), [] if self.last is None else [self.last]
        first_out = count + len(before)
        last_out = first_out + len(outs)

        def body(*refs):
            refs[last_out][...] = jnp.zeros(TOKEN, f32)
            taken = list(ins)
            for index, ref in zip(given, refs):
                taken[index] = ref
            kernel(*taken, *refs[first_out:last_out], *refs[last_out + 1 :])

        *results, self.last = pl.pallas_call(
            body,
            out_shape=shapes + (jax.ShapeDtypeStruct(TOKEN, f32),),
            in_specs=[spaces.get(index, VMEM) for index in given] + [ANY] * len(before),
            out_specs=tuple(out_space for _ in outs) + (VMEM,),
            name=getattr(kernel, "func", kernel).__name__ + str(tag),
            scratch_shapes=list(scratch),
            input_output_aliases={given.index(index): out for index, out in aliases.items()},
            cost_estimate=pl.CostEstimate(
                flops=COST, bytes_accessed=0, transcendentals=0
            ),
            compiler_params=pltpu.CompilerParams(vmem_limit_bytes=limit << 20),
        )(*[ins[index] for index in given], *before)
        return results


class Everywhere:
    def __init__(self, batch_count, seq_count):
        self.counts = batch_count, seq_count
        across = batch_count.bit_length() - 1
        along = seq_count.bit_length() - 1
        wide = [(0, bit) for bit in range(1, across)]
        tail = [(1, bit) for bit in range(1, along)]
        self.steps = list(zip(wide + [(1, 0)] + tail, [(1, 0)] + wide + tail))
        self.core = ((0, 0), (0, 0))

    def swap(self, array, step):
        batch_count, seq_count = self.counts
        pairs = []
        for batch in range(batch_count):
            for seq in range(seq_count):
                axis, bit = step[batch % 2]
                other = (batch ^ 1 << bit, seq) if axis == 0 else (batch, seq ^ 1 << bit)
                pairs.append((batch * seq_count + seq, other[0] * seq_count + other[1]))
        return lax.ppermute(array, ("batch", "seq"), pairs)

    def chunk(self, call, place, slot, kept, got, extra=None):
        size, width = kept.shape
        more = 0 if extra is None else extra.shape[0]
        keep = kept
        for index, step in enumerate(self.steps):
            fresh = extra is not None and index == 0
            mode = "fresh" if fresh else extra is not None
            keep, send = call(
                functools.partial(fold_kernel, slot + index, size, mode),
                [(size // 2 + more, width)] * 2,
                [place, keep, got] + ([extra] if fresh else []),
            )
            size //= 2
            got = self.swap(send, step)
            if index + 2 == len(self.steps):
                break
            yield
        yield
        keep, send = call(
            functools.partial(share_kernel, size, more),
            [(size + more, width)] * 2, [place, keep, got],
        )
        got = self.swap(send, self.steps[-1])
        yield
        own = call(
            functools.partial(fold_kernel, None, size, extra is not None),
            [(size, width)] + ([(more, width)] if more else []), [place, keep, got],
        )
        own, rest = own[0], own[1:]
        for index in range(len(self.steps) - 2, -1, -1):
            got = self.swap(own, self.steps[index])
            yield
            last = list(rest) if index == 0 else []
            (own,) = call(
                functools.partial(join_kernel, slot + index),
                [(2 * size + (more if last else 0), width)], [place, own, got] + last,
            )
            size *= 2
        return own, self.swap(own, self.core)


class Run:
    def __init__(self, turns):
        self.turns, self.result = turns, None

    def step(self, count=1):
        for _ in range(count if self.result is None else 0):
            try:
                next(self.turns)
            except StopIteration as end:
                self.result = end.value


def per_device(
    inputs, norm_gain, norm_bias, query_weight, query_bias, key_weight, value_weight, value_bias,
    mixer_weight, mixer_bias, final_gain, final_bias, inner_weight, inner_bias, outer_weight,
    outer_bias, cotangent,
):
    groups, span, width = inputs.shape
    tokens = groups * span
    half = span // 2
    hidden_width = inner_weight.shape[1]
    block = hidden_width // 4
    seq_count, batch_count = lax.axis_size("seq"), lax.axis_size("batch")
    crossing = seq_count.bit_length() - 1
    far_rows = BLOCK * crossing
    expand, means, near, one, rest = level_tables(span, crossing)
    coarse = means.shape[0]
    row = lambda vec: vec.reshape(1, -1)
    scale = 1.0 / math.sqrt(width // HEADS)
    x = inputs.reshape(tokens, width)
    cot = cotangent.reshape(tokens, width)
    everywhere = Everywhere(batch_count, seq_count)
    seq_slot = CORE + 1
    step_slot = seq_slot + crossing
    place = Here(span, seq_count, everywhere.steps)
    inner_pairs = [(i, i ^ 1) for i in range(seq_count)]
    outer_pairs = [
        (i, j)
        for i in range(seq_count)
        for j in [i + 1 if i % 2 else i - 1]
        if 0 <= j < seq_count
    ]
    order = Order()
    gain, shift = row(norm_gain), row(norm_bias)
    part_of_feed = hidden_width // 2
    narrow = lambda *shape: jax.ShapeDtypeStruct(shape, bf16)
    at = types.SimpleNamespace(hidden={}, gib={}, pairs={}, kept={}, got={}, fine={}, rough={})
    sums, turns = {}, {}

    call = order.call

    def start_sum(name, send, extra=None):
        at.got[name] = everywhere.swap(send, everywhere.core)

    def turn(name):
        if name not in sums:
            turns[name] = 0
            extra = at.vec if name == "D" else None
            sums[name] = Run(
                everywhere.chunk(
                    lambda *rest: call(*rest, name + str(turns[name])), place, step_slot, at.kept[name], at.got[name],
                    extra,
                )
            )
        sums[name].step()
        turns[name] += 1

    def first_norm():
        at.unit, at.inv, at.inner_send, outer_send = call(
            functools.partial(first_norm_kernel, groups, span),
            [(tokens, width), (tokens, 1), (groups, 2 * BLOCK, width), (groups, BLOCK, width)],
            [place, x],
        )
        at.far = [lax.ppermute(at.inner_send, "seq", inner_pairs)]
        at.outer_got = lax.ppermute(outer_send, "seq", outer_pairs)
        at.coarse_own = at.inner_send

    def project(kinds):
        weights = {"q": query_weight, "k": key_weight, "v": value_weight}
        biases = {"q": [row(query_bias)], "k": [], "v": [row(value_bias)]}
        scales = {"q": scale * LOG2E, "k": None, "v": 1.0}
        outs = call(
            functools.partial(project_kernel, groups, span, [scales[kind] for kind in kinds]),
            [(tokens, width), (groups * coarse, width)] * len(kinds),
            [at.unit, gain, shift, means] + [weights[kind] for kind in kinds]
            + [bias for kind in kinds for bias in biases[kind]], kinds,
        )
        for index, kind in enumerate(kinds):
            at.fine[kind], at.rough[kind] = outs[2 * index], outs[2 * index + 1]

    def project_qk():
        project("qk")

    def project_v():
        project("v")

    def coarser():
        bit = len(at.far)
        (at.coarse_own,) = call(
            functools.partial(coarser_kernel, seq_slot + bit - 1),
            [(groups, BLOCK, width)], [place, at.coarse_own, at.far[-1]],
        )
        at.far.append(
            lax.ppermute(at.coarse_own, "seq", [(i, i ^ 1 << bit) for i in range(seq_count)])
        )

    def rest_coarser():
        while len(at.far) < crossing:
            coarser()

    def local():
        at.num, at.den, at.numc, at.denc, at.halo, at.hk, at.hv = call(
            functools.partial(local_kernel, groups, span),
            [(groups * width, span), (groups * HEADS, span), (groups * width, half),
             (groups * HEADS, half)] + [(groups * 2 * BLOCK, width)] * 3,
            [place] + [at.fine[kind] for kind in "qkv"] + [at.rough[kind] for kind in "qkv"]
            + [at.far[0], at.outer_got, gain, shift, key_weight, value_weight,
               row(value_bias), near, one],
            scratch=[pltpu.VMEM((2,) + near.shape, f32)],
        )

    def remote():
        ins = at.far + [x, at.num, at.den, at.numc, at.denc]
        ins += [at.rough[kind] for kind in "qkv"]
        ins += [
            gain, shift, key_weight, value_weight, row(value_bias), rest, expand, mixer_weight,
            row(mixer_bias), row(final_gain), row(final_bias), row(outer_bias), cot,
        ]
        (
            at.far_rows, at.rk, at.rv, at.mixed, at.rden, at.unit2, at.inv2,
            at.acc, *at.split
        ) = call(
            functools.partial(remote_kernel, groups, span, crossing),
            [(groups * far_rows, width)] * 3 + [(groups * width, span), (groups * HEADS, span),
             (tokens, width), (tokens, 1), (tokens, width)] + [narrow(tokens, width)] * 4,
            ins, scratch=[pltpu.VMEM((tokens, width), f32)],
        )

    def outer(own):
        joint, *at.hidden[own] = call(
            functools.partial(outer_kernel, own),
            [(part_of_feed, width)] + [narrow(tokens, part_of_feed)] * 2 + [(tokens, part_of_feed)],
            [place] + at.split + [inner_weight, row(inner_bias)], own, limit=16,
        )
        if own:
            at.kept["A"] = joint
        else:
            start_sum("A", joint)

    def inner(own):
        joint, at.gib[own], at.acc, at.gacc = call(
            functools.partial(inner_kernel, own),
            [(2 * width, part_of_feed // 2), (1, part_of_feed), (tokens, width), (tokens, width)],
            [place] + at.split + at.hidden[own] + [inner_weight, outer_weight, at.acc]
            + ([at.gacc] if own else []),
            own, limit=16,
        )
        if own:
            at.kept["B"] = joint
        else:
            start_sum("B", joint)

    def middle_grad():
        (
            at.gmid, at.gmw, at.vec_mid, at.gnum, at.gnumt, at.gden, at.gnumct,
            at.gdenc,
        ) = call(
            functools.partial(middle_grad_kernel, groups, span),
            [(tokens, width), (width, width), (8, width), (tokens, width), (groups * width, span),
             (groups * HEADS, span), (groups * width, coarse), (groups * HEADS, coarse)],
            [cot, at.gacc, at.unit2, at.inv2, row(final_gain), at.mixed, at.rden,
             mixer_weight, expand],
        )

    outside_rows = groups * (2 * BLOCK + far_rows)

    def pairs(part):
        at.pairs[part] = call(
            functools.partial(pairs_grad_kernel, groups, part, span),
            [(tokens, half_width)] * 3 + [(outside_rows, half_width)] * 2,
            [place] + [at.fine[kind] for kind in "qkv"] + [at.rough[kind] for kind in "qkv"]
            + [at.hk, at.hv, at.rk, at.rv, at.gnum, at.gnumt, at.gden, at.gnumct, at.gdenc, near, one,
               rest, means], part,
            scratch=[
                pltpu.VMEM((2,) + near.shape, f32),
                pltpu.VMEM((span + 2 * BLOCK, half_width), f32),
                pltpu.VMEM((span + 2 * BLOCK, half_width), f32),
                pltpu.VMEM((half + rest.shape[0], half_width), f32),
                pltpu.VMEM((half + rest.shape[0], half_width), f32),
                pltpu.VMEM((half_width, span), f32),
                pltpu.VMEM((half_width, coarse), f32),
            ],
        )

    half_width = width // 2

    def square(part):
        name = "CD"[part]
        at.kept[name], send = call(
            functools.partial(square_grad_kernel, part, scale),
            [(width, width)] * 2,
            [place, at.unit, at.halo, at.far_rows, gain, shift, at.gmw]
            + list(at.pairs[part]), part,
            scratch=[pltpu.VMEM((3, width, half_width), f32)],
        )
        start_sum(name, send)

    def rows_grad():
        at.vec, at.gnorm, at.inner_back, outer_back, *gfar = call(
            functools.partial(rows_grad_kernel, groups, crossing, scale),
            [(SPARE, width), (tokens, width)] + [(groups, BLOCK, width)] * (2 + crossing),
            [place, at.unit, at.halo, at.far_rows] + list(at.pairs[0])
            + list(at.pairs[1]) + [query_weight, key_weight, value_weight, at.vec_mid,
                                     at.gib[0], at.gib[1]],
        )
        at.outer_back = lax.ppermute(outer_back, "seq", outer_pairs)
        at.gfar = gfar
        at.back = [
            lax.ppermute(gfar[-1], "seq", [(i, i ^ 1 << crossing - 1) for i in range(seq_count)])
        ]
        at.back_bit = crossing - 1

    def finer():
        at.back_bit -= 1
        bit = at.back_bit
        rim = [] if bit else [at.inner_back]
        passing = [at.outer_back] if bit == crossing - 2 else []
        mine, send, *passed = call(
            functools.partial(finer_kernel, seq_slot + bit, len(rim), bool(passing)),
            [(groups, BLOCK, width), (groups, BLOCK * (1 + len(rim)), width)]
            + [value.shape for value in passing],
            [place] + passing + at.back + [at.gfar[bit]] + rim,
            scratch=[pltpu.VMEM((BLOCK, width), f32)],
        )
        if passed:
            at.outer_back = passed[0]
        at.back = [
            lax.ppermute(send, "seq", [(i, i ^ 1 << bit) for i in range(seq_count)]), mine
        ]

    def first_grad():
        while at.back_bit:
            finer()
        (at.inputs_grad,) = call(
            functools.partial(first_grad_kernel, groups, span),
            [(tokens, width)],
            [place, at.gmid, at.gnorm] + at.back
            + [at.outer_back, at.unit, at.inv, gain],
            scratch=[pltpu.VMEM((tokens, width), f32)],
        )

    def write(name, kernel, shapes, count, before=()):
        while name not in sums or sums[name].result is None:
            turn(name)
        ins = [place] + list(sums[name].result) + list(before)
        return call(
            kernel, shapes, ins, name, scratch=[pltpu.SemaphoreType.DMA((count,))],
            out_space=HBM, spaces={3 + index: HBM for index in range(len(before))},
            aliases={3 + index: index for index in range(len(before))},
        )

    def write_outer():
        at.gow = write("A", place_outer_kernel, [(hidden_width, width)], 2)

    def write_inner():
        at.giw = write("B", place_inner_kernel, [(width, hidden_width)], 4)

    def write_square(part):
        at.squares = write(
            "CD"[part], functools.partial(place_square_kernel, part), [(width, width)] * 4, 8,
            getattr(at, "squares", ()),
        )
        if part:
            at.vecs = call(
                vectors_kernel, [(1, width)] * 8 + [(1, hidden_width)],
                list(sums["D"].result),
            )

    acts = (
        first_norm, project_qk, project_v, coarser, rest_coarser, local, remote, outer, inner,
        middle_grad, pairs, square, rows_grad, finer, first_grad, write_outer, write_inner,
        write_square,
    )
    acts = {act.__name__: act for act in acts}
    for name in PLAN:
        if name.isupper():
            turn(name)
        else:
            acts[name.rstrip("01")](*[int(digit) for digit in name if digit.isdigit()])
    gng, gnb, gqb, gvb, gfg, gfb, gmb, gob, gib = [vec.reshape(-1) for vec in at.vecs]
    gqw, gkw, gvw, gmw = at.squares
    return (
        at.acc.reshape(inputs.shape), at.inputs_grad.reshape(inputs.shape), gng, gnb, gqw,
        gqb, gkw, gvw, gvb, gmw, gmb, gfg, gfb, at.giw[0], gib, at.gow[0], gob,
    )


def solution(mesh):
    split_spec = P("batch", "seq", None)
    return jax.shard_map(
        per_device,
        mesh=mesh,
        in_specs=(split_spec,) + (P(),) * 15 + (split_spec,),
        out_specs=(split_spec, split_spec) + (P(),) * 15,
        check_vma=False,
    )
```

```python
import functools
import math
import types

import jax
import jax.numpy as jnp
import numpy as np
from jax import lax
from jax.experimental import pallas as pl
from jax.experimental.pallas import tpu as pltpu
from jax.sharding import PartitionSpec as P

HEADS = 8
BLOCK = 16
LOG2E = 1.4426950408889634
LN2 = 0.6931471805599453
ROOT_HALF = 0.7071067811865476
INV_ROOT_TWO_PI = 0.3989422804014327
EPS = 1e-06
FAR = -1e30
SPARE = 16
TOKEN = (8, 128)
PLAN = (
    "first_norm", "project_qk", "project_v", "coarser", "rest_coarser", "local", "remote",
    "outer0", "outer1", "inner0", "A", "inner1", "middle_grad", "B", "A", "pairs1", "pairs0", "A",
    "rows_grad", "B", "A", "finer", "square0", "finer", "B", "C", "square1", "first_grad", "A",
    "C", "B", "A", "D", "C", "A", "C", "D", "B", "D", "C", "B", "D", "C", "B", "D", "A", "B", "D",
    "C", "write_outer", "D", "write_inner", "C", "D", "write_square0", "write_square1",
)
COST = 10**10
INNER, OUTER, ODD, FIRST, LAST, CORE = range(6)

bf16 = jnp.bfloat16
f32 = jnp.float32
VMEM = pl.BlockSpec(memory_space=pltpu.VMEM)
ANY = pl.BlockSpec(memory_space=pl.ANY)
HBM = pl.BlockSpec(memory_space=pltpu.MemorySpace.HBM)


def split(value):
    high = value.astype(bf16)
    return high, (value - high.astype(f32)).astype(bf16)


def dg(left, right, left_dim=1, right_dim=0):
    return lax.dot_general(
        left, right, (((left_dim,), (right_dim,)), ((), ())), preferred_element_type=f32
    )


def dot3(left, right, left_dim=1, right_dim=0):
    return (
        dg(left[0], right[0], left_dim, right_dim)
        + dg(left[0], right[1], left_dim, right_dim)
        + dg(left[1], right[0], left_dim, right_dim)
    )


def dot2(left, exact, left_dim=1, right_dim=0):
    return dg(left[0], exact, left_dim, right_dim) + dg(left[1], exact, left_dim, right_dim)


def exact_dot2(exact, right, left_dim=1, right_dim=0):
    return dg(exact, right[0], left_dim, right_dim) + dg(exact, right[1], left_dim, right_dim)


def two_diagonal(pair_rows):
    half = pair_rows.shape[0] // 2
    zero = jnp.zeros((half, pair_rows.shape[1]), pair_rows.dtype)
    return jnp.concatenate(
        [
            jnp.concatenate([pair_rows[:half], zero], axis=1),
            jnp.concatenate([zero, pair_rows[half:]], axis=1),
        ],
        axis=0,
    )


def two_masked(pair_lanes):
    half = pair_lanes.shape[1] // 2
    lower = lax.broadcasted_iota(jnp.int32, pair_lanes.shape, 1) < half
    wide = pair_lanes.astype(f32)
    return jnp.concatenate(
        [jnp.where(lower, wide, 0.0), jnp.where(lower, 0.0, wide)], axis=0
    ).astype(bf16)


def take_diagonal(product):
    half, width = product.shape[0] // 2, product.shape[1] // 2
    return jnp.concatenate([product[:half, :width], product[half:, width:]], axis=0)


def pair_weights(keys, queries_t, bias):
    diag_high, diag_low = two_diagonal(queries_t[0]), two_diagonal(queries_t[1])
    scores = dg(
        jnp.concatenate([keys[0], keys[1], keys[0]], axis=1),
        jnp.concatenate([diag_high, diag_high, diag_low], axis=0),
    )
    return jnp.exp2(scores + bias)


def tile_forward(keys, values_t, queries_t, bias):
    weights = pair_weights(keys, queries_t, bias)
    denominator = jnp.sum(weights, axis=0, keepdims=True)
    high, low = split(weights)
    wide = dg(jnp.concatenate([values_t[0], values_t[1]], axis=0), high)
    size = values_t[0].shape[0]
    product = wide[:size] + wide[size:] + dg(values_t[0], low)
    width = denominator.shape[1] // 2
    return (
        take_diagonal(product),
        jnp.concatenate([denominator[:, :width], denominator[:, width:]], axis=0),
    )


def tile_backward(keys, keys_t, values, queries_t, queries_m, grads_t, grads_m, grad_den, bias):
    weights = pair_weights(keys, queries_t, bias)
    diag_high, diag_low = two_diagonal(grads_t[0]), two_diagonal(grads_t[1])
    grad_weights = (
        dg(
            jnp.concatenate([values[0], values[1], values[0]], axis=1),
            jnp.concatenate([diag_high, diag_high, diag_low], axis=0),
        )
        + grad_den
    )
    scores = split(weights * grad_weights)
    weights = split(weights)

    def gather(pairs, masked):
        wide = dg(pairs[0], jnp.concatenate([masked[0], masked[1]], axis=1))
        half = wide.shape[1] // 2
        return wide[:, :half] + wide[:, half:] + dg(pairs[1], masked[0])

    grad_values = gather(weights, grads_m)
    grad_keys = gather(scores, queries_m)
    wide = dg(jnp.concatenate([keys_t[0], keys_t[1]], axis=0), scores[0])
    size = keys_t[0].shape[0]
    product = wide[:size] + wide[size:] + dg(keys_t[0], scores[1])
    return take_diagonal(product), grad_keys, grad_values


def lanes(parts, start, size):
    return tuple(part[:, start : start + size] for part in parts)


def rows(parts, start, size):
    return tuple(part[start : start + size] for part in parts)


def block_of(parts, row, row_size, lane, lane_size):
    return tuple(part[row : row + row_size, lane : lane + lane_size] for part in parts)


def stack(first, second):
    return tuple(jnp.concatenate([one, two], axis=0) for one, two in zip(first, second))


def norm_rows(values):
    center = values - jnp.mean(values, axis=-1, keepdims=True)
    inverse = lax.rsqrt(jnp.mean(center * center, axis=-1, keepdims=True) + EPS)
    return center * inverse, inverse


def norm_grad(grad_rows, unit_rows, inverse, gain):
    grad_unit = grad_rows * gain
    return inverse * (
        grad_unit
        - jnp.mean(grad_unit, axis=-1, keepdims=True)
        - unit_rows * jnp.mean(grad_unit * unit_rows, axis=-1, keepdims=True)
    )


def first_norm_kernel(groups, span, place_ref, x_ref, unit_ref, inv_ref, inner_ref, outer_ref):
    width = x_ref.shape[-1]
    for group in range(groups):
        own = slice(group * span, (group + 1) * span)
        unit, inverse = norm_rows(x_ref[own, :])
        unit_ref[own, :] = unit
        inv_ref[own, :] = inverse
        runs = span // BLOCK
        inner_ref[group, BLOCK:, :] = jnp.mean(unit.reshape(BLOCK, runs, width), axis=1)
        inner_start = pl.multiple_of(group * span + place_ref[INNER], BLOCK)
        outer_start = pl.multiple_of(group * span + place_ref[OUTER], BLOCK)
        inner_ref[group, :BLOCK, :] = unit_ref[pl.ds(inner_start, BLOCK), :]
        outer_ref[group] = unit_ref[pl.ds(outer_start, BLOCK), :]


def project_kernel(groups, span, scales, unit_ref, gain_ref, shift_ref, mean_ref, *refs):
    count = len(scales)
    weights, refs = refs[:count], refs[count:]
    biased = [scale is not None for scale in scales]
    biases, outs = list(refs[: sum(biased)]), refs[sum(biased) :]
    normed = split(unit_ref[...] * gain_ref[...] + shift_ref[...])
    means = mean_ref[...]
    coarse = means.shape[0]
    for index, (weight, scale) in enumerate(zip(weights, scales)):
        result = dot3(normed, split(weight[...]))
        if scale is not None:
            result = result + biases.pop(0)[...]
            if scale != 1.0:
                result = result * scale
        outs[2 * index][...] = result
        for group in range(groups):
            part = split(result[group * span : (group + 1) * span])
            outs[2 * index + 1][group * coarse : (group + 1) * coarse, :] = exact_dot2(means, part)


def fill_bias(bias_ref, near_ref, place_ref):
    rows_total = near_ref.shape[0]
    bias_ref[0] = near_ref[...]
    bias_ref[1] = near_ref[...]
    before = place_ref[FIRST].astype(f32) * FAR
    after = place_ref[LAST].astype(f32) * FAR
    bias_ref[0, :BLOCK, :] = near_ref[:BLOCK, :] + before
    bias_ref[1, rows_total - BLOCK :, :] = near_ref[rows_total - BLOCK :, :] + after


def local_kernel(
    groups, span, place_ref, q_ref, k_ref, v_ref, qc_ref, kc_ref, vc_ref, inner_ref, outer_ref,
    gain_ref, shift_ref, kw_ref, vw_ref, vb_ref, near_ref, one_ref,
    num_ref, den_ref, numc_ref, denc_ref, halo_ref, hk_ref, hv_ref, bias_ref,
):
    width = q_ref.shape[-1]
    half = span // 2
    coarse = qc_ref.shape[0] // groups
    pairs = HEADS // 2
    pair_width = width // pairs
    tile_keys = half + 2 * BLOCK
    fill_bias(bias_ref, near_ref, place_ref)
    odd = place_ref[ODD].astype(f32)
    for group in range(groups):
        inner, outer = inner_ref[group, :BLOCK, :], outer_ref[group]
        at = group * 2 * BLOCK
        halo_ref[at : at + BLOCK, :] = inner * odd + outer * (1.0 - odd)
        halo_ref[at + BLOCK : at + 2 * BLOCK, :] = inner * (1.0 - odd) + outer * odd
    normed = split(halo_ref[...] * gain_ref[...] + shift_ref[...])
    halo_keys = dot3(normed, split(kw_ref[...]))
    halo_values = dot3(normed, split(vw_ref[...])) + vb_ref[...]
    hk_ref[...] = halo_keys
    hv_ref[...] = halo_values
    for group in range(groups):
        own = slice(group * span, (group + 1) * span)
        left = slice(group * 2 * BLOCK, group * 2 * BLOCK + BLOCK)
        right = slice(group * 2 * BLOCK + BLOCK, (group + 1) * 2 * BLOCK)
        own_c = slice(group * coarse, group * coarse + half)
        keys = split(jnp.concatenate([halo_keys[left], k_ref[own, :], halo_keys[right]], axis=0))
        values = jnp.concatenate([halo_values[left], v_ref[own, :], halo_values[right]], axis=0)
        values_t = split(values.T)
        queries_t = split(q_ref[own, :].T)
        keys_c = split(kc_ref[own_c, :])
        values_ct = split(vc_ref[own_c, :].T)
        queries_ct = split(qc_ref[own_c, :].T)
        for pair in range(pairs):
            at = pair * pair_width
            out = slice(group * width + at, group * width + at + pair_width)
            heads = slice((group * pairs + pair) * 2, (group * pairs + pair) * 2 + 2)
            for tile in range(2):
                num, den = tile_forward(
                    block_of(keys, tile * half, tile_keys, at, pair_width),
                    block_of(values_t, at, pair_width, tile * half, tile_keys),
                    block_of(queries_t, at, pair_width, tile * half, half),
                    bias_ref[tile],
                )
                num_ref[out, tile * half : (tile + 1) * half] = num
                den_ref[heads, tile * half : (tile + 1) * half] = den
            num, den = tile_forward(
                lanes(keys_c, at, pair_width),
                rows(values_ct, at, pair_width),
                rows(queries_ct, at, pair_width),
                one_ref[...],
            )
            numc_ref[out, :] = num
            denc_ref[heads, :] = den


def remote_kernel(
    groups, span, crossing, *refs
):
    far_parts, refs = refs[:crossing], refs[crossing:]
    (
        x_ref, num_ref, den_ref, numc_ref, denc_ref, qc_ref, kc_ref, vc_ref, gain_ref, shift_ref,
        kw_ref, vw_ref, vb_ref, rest_ref, expand_ref, mw_ref, mb_ref, fgain_ref, fshift_ref, ob_ref,
        cot_ref,
        far_ref, rk_ref, rv_ref, mixed_ref, rden_ref, unit_ref, inv_ref, acc_ref, fhigh_ref, flow_ref,
        chigh_ref, clow_ref, mid_ref,
    ) = refs
    width = x_ref.shape[-1]
    half = span // 2
    coarse = qc_ref.shape[0] // groups
    far = far_ref.shape[0] // groups
    pairs = HEADS // 2
    pair_width = width // pairs
    head_width = width // HEADS
    local_rest = rest_ref.shape[0] - far
    for group in range(groups):
        for level, part in enumerate(far_parts):
            at = group * far + level * BLOCK
            far_ref[at : at + BLOCK, :] = part[group, part.shape[1] - BLOCK :, :]
    normed = split(far_ref[...] * gain_ref[...] + shift_ref[...])
    far_keys = dot3(normed, split(kw_ref[...]))
    far_values = dot3(normed, split(vw_ref[...])) + vb_ref[...]
    rk_ref[...] = far_keys
    rv_ref[...] = far_values
    expand = expand_ref[...]
    for group in range(groups):
        rest = slice(group * coarse + half, group * coarse + half + local_rest)
        remote = slice(group * far, (group + 1) * far)
        keys = split(jnp.concatenate([kc_ref[rest, :], far_keys[remote]], axis=0))
        values_t = split(jnp.concatenate([vc_ref[rest, :], far_values[remote]], axis=0).T)
        queries_t = split(qc_ref[group * coarse + half : (group + 1) * coarse, :].T)
        nums, dens = [], []
        for pair in range(pairs):
            at = pair * pair_width
            num, den = tile_forward(
                lanes(keys, at, pair_width),
                rows(values_t, at, pair_width),
                rows(queries_t, at, pair_width),
                rest_ref[...],
            )
            nums.append(num)
            dens.append(den)
        own_t = slice(group * width, (group + 1) * width)
        own_h = slice(group * HEADS, (group + 1) * HEADS)
        numc = jnp.concatenate([numc_ref[own_t, :], jnp.concatenate(nums, axis=0)], axis=1)
        denc = jnp.concatenate([denc_ref[own_h, :], jnp.concatenate(dens, axis=0)], axis=1)
        num = num_ref[own_t, :] + dot2(split(numc), expand)
        den = den_ref[own_h, :] + dot2(split(denc), expand)
        inverse = 1.0 / den
        rden_ref[own_h, :] = inverse
        spread = jnp.concatenate(
            [
                jnp.broadcast_to(inverse[head : head + 1], (head_width, span))
                for head in range(HEADS)
            ],
            axis=0,
        )
        mixed_t = num * spread
        own = slice(group * span, (group + 1) * span)
        mixed_ref[own_t, :] = mixed_t
        mid_ref[own, :] = mixed_t.T
    middle = x_ref[...] + dot3(split(mid_ref[...]), split(mw_ref[...])) + mb_ref[...]
    unit, inverse = norm_rows(middle)
    unit_ref[...] = unit
    inv_ref[...] = inverse
    fhigh_ref[...], flow_ref[...] = split(unit * fgain_ref[...] + fshift_ref[...])
    chigh_ref[...], clow_ref[...] = split(cot_ref[...])
    acc_ref[...] = middle + ob_ref[...]


def half_of(own, place_ref, size):
    side = place_ref[CORE] if own else 1 - place_ref[CORE]
    return pl.ds(pl.multiple_of(side * size, size), size)


def outer_kernel(
    own, place_ref, fhigh_ref, flow_ref, chigh_ref, clow_ref, iw_ref, ib_ref,
    joint_ref, hhigh_ref, hlow_ref, slope_ref,
):
    units = half_of(own, place_ref, slope_ref.shape[1])
    inner = dot3((fhigh_ref[...], flow_ref[...]), split(iw_ref[:, units])) + ib_ref[:, units]
    cumulative = 0.5 * (1.0 + lax.erf(inner * ROOT_HALF))
    hidden = split(inner * cumulative)
    slope_ref[...] = cumulative + inner * jnp.exp(-0.5 * inner * inner) * INV_ROOT_TWO_PI
    hhigh_ref[...], hlow_ref[...] = hidden
    joint_ref[...] = dot3(hidden, (chigh_ref[...], clow_ref[...]), 0, 0)


def inner_kernel(
    own, place_ref, fhigh_ref, flow_ref, chigh_ref, clow_ref, hhigh_ref, hlow_ref, slope_ref,
    iw_ref, ow_ref, acc_ref, *refs
):
    giw_ref, gib_ref, nacc_ref, ngacc_ref = refs[-4:]
    units = half_of(own, place_ref, slope_ref.shape[1])
    cot = chigh_ref[...], clow_ref[...]
    hidden = hhigh_ref[...], hlow_ref[...]
    iw, ow = split(iw_ref[:, units]), split(ow_ref[units, :])
    grad_inner = dot3(cot, ow, 1, 1) * slope_ref[...]
    gib_ref[...] = jnp.sum(grad_inner, axis=0, keepdims=True)
    grad_inner = split(grad_inner)
    giw = dot3((fhigh_ref[...], flow_ref[...]), grad_inner, 0, 0)
    width = giw.shape[0]
    giw_ref[:width, :] = giw[:, :width]
    giw_ref[width:, :] = giw[:, width:]
    nacc_ref[...] = acc_ref[...] + dot3(hidden, ow)
    grad_fnorm = dot3(grad_inner, iw, 1, 1)
    ngacc_ref[...] = refs[0][...] + grad_fnorm if own else grad_fnorm


def middle_grad_kernel(
    groups, span, cot_ref, gf_ref, unit_ref, inv_ref, fgain_ref, mixed_ref, rden_ref, mw_ref,
    expand_ref,
    gmid_ref, gmw_ref, vec_ref, gnum_ref, gnumt_ref, gden_ref, gnumct_ref, gdenc_ref,
):
    width = cot_ref.shape[-1]
    head_width = width // HEADS
    cot = cot_ref[...]
    gf = gf_ref[...]
    unit = unit_ref[...]
    gmid = cot + norm_grad(gf, unit, inv_ref[...], fgain_ref[...])
    gmid_ref[...] = gmid
    vec_ref[0:1, :] = jnp.sum(gf * unit, axis=0, keepdims=True)
    vec_ref[1:2, :] = jnp.sum(gf, axis=0, keepdims=True)
    vec_ref[2:3, :] = jnp.sum(gmid, axis=0, keepdims=True)
    vec_ref[3:4, :] = jnp.sum(cot, axis=0, keepdims=True)
    gmid = split(gmid)
    expand = expand_ref[...]
    grad_mixed = dot3(gmid, split(mw_ref[...]), 1, 1)
    total = None
    for group in range(groups):
        own = slice(group * span, (group + 1) * span)
        own_t = slice(group * width, (group + 1) * width)
        own_h = slice(group * HEADS, (group + 1) * HEADS)
        mixed_t = mixed_ref[own_t, :]
        part = dot3(split(mixed_t), rows(gmid, group * span, span))
        total = part if total is None else total + part
        grad_t = grad_mixed[own].T
        inverse = rden_ref[own_h, :]
        spread = jnp.concatenate(
            [
                jnp.broadcast_to(inverse[head : head + 1], (head_width, span))
                for head in range(HEADS)
            ],
            axis=0,
        )
        product = grad_t * mixed_t
        dens = jnp.concatenate(
            [
                jnp.sum(product[head * head_width : (head + 1) * head_width], axis=0, keepdims=True)
                for head in range(HEADS)
            ],
            axis=0,
        )
        gden = -dens * inverse
        gnum_t = grad_t * spread
        gnumt_ref[own_t, :] = gnum_t
        gnum_ref[own, :] = gnum_t.T
        gden_ref[own_h, :] = gden
        gnumct_ref[own_t, :] = dot2(split(gnum_t), expand, 1, 1)
        gdenc_ref[own_h, :] = dot2(split(gden), expand, 1, 1)
    gmw_ref[...] = total


def pairs_grad_kernel(
    groups, part, span, place_ref, q_ref, k_ref, v_ref, qc_ref, kc_ref, vc_ref, hk_ref, hv_ref,
    rk_ref, rv_ref, gnum_ref, gnumt_ref, gden_ref, gnumct_ref, gdenc_ref, near_ref, one_ref,
    rest_ref, mean_ref,
    dq_ref, dk_ref, dv_ref, odk_ref, odv_ref,
    bias_ref, dkx_ref, dvx_ref, dkc_ref, dvc_ref, dqt_ref, dqct_ref,
):
    full = q_ref.shape[-1]
    width = full // 2
    half = span // 2
    coarse = qc_ref.shape[0] // groups
    far = rk_ref.shape[0] // groups
    pairs = HEADS // 4
    pair_width = width // pairs
    tile_keys = half + 2 * BLOCK
    local_rest = rest_ref.shape[0] - far
    local_coarse = half + local_rest
    rest_keys = local_rest + far
    ours = slice(part * width, (part + 1) * width)
    fill_bias(bias_ref, near_ref, place_ref)
    means = mean_ref[...]
    zero = jnp.zeros((coarse - local_coarse, width), f32)
    for group in range(groups):
        fine = slice(group * span, (group + 1) * span)
        rough = slice(group * coarse, group * coarse + coarse)
        near_rough = slice(group * coarse, group * coarse + local_coarse)
        left = slice(group * 2 * BLOCK, group * 2 * BLOCK + BLOCK)
        right = slice(group * 2 * BLOCK + BLOCK, (group + 1) * 2 * BLOCK)
        remote = slice(group * far, (group + 1) * far)
        ours_t = slice(group * full + part * width, group * full + (part + 1) * width)
        keys_f = jnp.concatenate(
            [hk_ref[left, ours], k_ref[fine, ours], hk_ref[right, ours]], axis=0
        )
        keys, keys_t = split(keys_f), split(keys_f.T)
        values = split(
            jnp.concatenate([hv_ref[left, ours], v_ref[fine, ours], hv_ref[right, ours]], axis=0)
        )
        q = q_ref[fine, ours]
        queries, queries_t = split(q), split(q.T)
        grads, grads_t = split(gnum_ref[fine, ours]), split(gnumt_ref[ours_t, :])
        keys_cf = jnp.concatenate([kc_ref[near_rough, ours], rk_ref[remote, ours]], axis=0)
        keys_c, keys_ct = split(keys_cf), split(keys_cf.T)
        values_c = split(
            jnp.concatenate([vc_ref[near_rough, ours], rv_ref[remote, ours]], axis=0)
        )
        qc = qc_ref[rough, ours]
        queries_c, queries_ct = split(qc), split(qc.T)
        gnumct = gnumct_ref[ours_t, :]
        grads_c, grads_ct = split(gnumct.T), split(gnumct)
        for pair in range(pairs):
            at = pair * pair_width
            cols = slice(at, at + pair_width)
            head = group * HEADS + part * (HEADS // 2) + 2 * pair

            def den_rows(ref, start):
                both = ref[head : head + 2, start : start + half]
                return jnp.concatenate([both[0:1], both[1:2]], axis=1)

            def masked(parts, start):
                return tuple(
                    two_masked(value) for value in block_of(parts, start, half, at, pair_width)
                )

            for tile in range(2):
                start = tile * half
                dq, dk, dv = tile_backward(
                    block_of(keys, start, tile_keys, at, pair_width),
                    block_of(keys_t, at, pair_width, start, tile_keys),
                    block_of(values, start, tile_keys, at, pair_width),
                    block_of(queries_t, at, pair_width, start, half),
                    masked(queries, start),
                    block_of(grads_t, at, pair_width, start, half),
                    masked(grads, start),
                    den_rows(gden_ref, start),
                    bias_ref[tile],
                )
                dqt_ref[cols, start : start + half] = dq
                if tile == 0:
                    dkx_ref[:tile_keys, cols] = dk
                    dvx_ref[:tile_keys, cols] = dv
                else:
                    shared = slice(start, start + 2 * BLOCK)
                    fresh = slice(start + 2 * BLOCK, start + tile_keys)
                    dkx_ref[shared, cols] = dkx_ref[shared, cols] + dk[: 2 * BLOCK]
                    dvx_ref[shared, cols] = dvx_ref[shared, cols] + dv[: 2 * BLOCK]
                    dkx_ref[fresh, cols] = dk[2 * BLOCK :]
                    dvx_ref[fresh, cols] = dv[2 * BLOCK :]
            for start, count, bias in ((0, half, one_ref), (half, rest_keys, rest_ref)):
                dq, dk, dv = tile_backward(
                    block_of(keys_c, start, count, at, pair_width),
                    block_of(keys_ct, at, pair_width, start, count),
                    block_of(values_c, start, count, at, pair_width),
                    block_of(queries_ct, at, pair_width, start, half),
                    masked(queries_c, start),
                    block_of(grads_ct, at, pair_width, start, half),
                    masked(grads_c, start),
                    den_rows(gdenc_ref, start),
                    bias[...],
                )
                dqct_ref[cols, start : start + half] = dq
                dkc_ref[start : start + count, cols] = dk
                dvc_ref[start : start + count, cols] = dv
        distant = slice(
            groups * 2 * BLOCK + group * far, groups * 2 * BLOCK + (group + 1) * far
        )
        odk_ref[distant, :] = dkc_ref[local_coarse:, :] * LN2
        odv_ref[distant, :] = dvc_ref[local_coarse:, :]
        odk_ref[left, :] = dkx_ref[:BLOCK, :] * LN2
        odk_ref[right, :] = dkx_ref[span + BLOCK :, :] * LN2
        odv_ref[left, :] = dvx_ref[:BLOCK, :]
        odv_ref[right, :] = dvx_ref[span + BLOCK :, :]

        def spread(ref):
            local = jnp.concatenate([ref[:local_coarse, :], zero], axis=0)
            return exact_dot2(means, split(local), 0, 0)

        dk_ref[fine, :] = (dkx_ref[BLOCK : span + BLOCK, :] + spread(dkc_ref)) * LN2
        dv_ref[fine, :] = dvx_ref[BLOCK : span + BLOCK, :] + spread(dvc_ref)
        dq_ref[fine, :] = (dqt_ref[...] + dot2(split(dqct_ref[...]), means)).T


def square_grad_kernel(
    part, scale, place_ref, unit_ref, halo_ref, far_ref, gain_ref, shift_ref, gmw_ref,
    dq_ref, dk_ref, dv_ref, odk_ref, odv_ref, own_ref, send_ref, full_ref,
):
    width = unit_ref.shape[-1]
    half = width // 2
    core = place_ref[CORE]
    mine = pl.ds(pl.multiple_of(core * half, half), half)
    other = pl.ds(pl.multiple_of((1 - core) * half, half), half)
    outside = jnp.concatenate([halo_ref[...], far_ref[...]], axis=0)
    normed = split(unit_ref[...] * gain_ref[...] + shift_ref[...])
    normed_out = split(outside * gain_ref[...] + shift_ref[...])
    full_ref[0] = dot3(normed, split(dq_ref[...] * scale), 0, 0)
    full_ref[1] = dot3(normed, split(dk_ref[...]), 0, 0) + dot3(
        normed_out, split(odk_ref[...]), 0, 0
    )
    full_ref[2] = dot3(normed, split(dv_ref[...]), 0, 0) + dot3(
        normed_out, split(odv_ref[...]), 0, 0
    )
    for target, at in ((own_ref, mine), (send_ref, other)):
        target[:half, :half] = full_ref[0, at, :]
        target[:half, half:] = full_ref[1, at, :]
        target[half:, :half] = full_ref[2, at, :]
        target[half:, half:] = gmw_ref[at, part * half : (part + 1) * half]


def rows_grad_kernel(groups, crossing, scale, place_ref, unit_ref, halo_ref, far_ref, *refs):
    parts, refs = (refs[:5], refs[5:10]), refs[10:]
    qw_ref, kw_ref, vw_ref, mid_ref = refs[:4]
    gib_refs, refs = refs[4:6], refs[6:]
    vec_ref, gnorm_ref, inner_ref, outer_ref = refs[:4]
    gfar_refs = refs[4:]
    joined = lambda index: jnp.concatenate([part[index][...] for part in parts], axis=1)
    width = unit_ref.shape[-1]
    unit = unit_ref[...]
    outside = jnp.concatenate([halo_ref[...], far_ref[...]], axis=0)
    dq_f, dv_f, odv_f = joined(0) * scale, joined(2), joined(4)
    dq, dk, dv = split(dq_f), split(joined(1)), split(dv_f)
    odk, odv = split(joined(3)), split(odv_f)
    qw, kw, vw = split(qw_ref[...]), split(kw_ref[...]), split(vw_ref[...])
    gnorm = dot3(dq, qw, 1, 1) + dot3(dk, kw, 1, 1) + dot3(dv, vw, 1, 1)
    gout = dot3(odk, kw, 1, 1) + dot3(odv, vw, 1, 1)
    gnorm_ref[...] = gnorm
    odd = place_ref[ODD].astype(f32)
    far = far_ref.shape[0] // groups
    for group in range(groups):
        at = group * 2 * BLOCK
        low, high = gout[at : at + BLOCK], gout[at + BLOCK : at + 2 * BLOCK]
        inner_ref[group] = low * odd + high * (1.0 - odd)
        outer_ref[group] = low * (1.0 - odd) + high * odd
        for level, gfar_ref in enumerate(gfar_refs):
            at = groups * 2 * BLOCK + group * far + level * BLOCK
            gfar_ref[group] = gout[at : at + BLOCK]
    first = place_ref[CORE].astype(f32)
    other_gib, own_gib = gib_refs[0][...], gib_refs[1][...]
    low_gib = own_gib * (1.0 - first) + other_gib * first
    high_gib = own_gib * first + other_gib * (1.0 - first)
    vec_ref[...] = jnp.concatenate(
        [
            jnp.sum(gnorm * unit, axis=0, keepdims=True)
            + jnp.sum(gout * outside, axis=0, keepdims=True),
            jnp.sum(gnorm, axis=0, keepdims=True) + jnp.sum(gout, axis=0, keepdims=True),
            jnp.sum(dq_f, axis=0, keepdims=True),
            jnp.sum(dv_f, axis=0, keepdims=True) + jnp.sum(odv_f, axis=0, keepdims=True),
            mid_ref[0:4, :],
            low_gib[:, :width],
            low_gib[:, width:],
            high_gib[:, :width],
            high_gib[:, width:],
            jnp.zeros((SPARE - 12, width), f32),
        ],
        axis=0,
    )


def first_grad_kernel(
    groups, span, place_ref, gmid_ref, gnorm_ref, got_ref, mine_ref, outer_ref, unit_ref, inv_ref,
    gain_ref, out_ref, total_ref,
):
    width = gmid_ref.shape[-1]
    runs = span // BLOCK
    for group in range(groups):
        own = slice(group * span, (group + 1) * span)
        four = (got_ref[group, BLOCK:, :] + mine_ref[group]) * (1.0 / runs)
        spread = jnp.broadcast_to(four.reshape(BLOCK, 1, width), (BLOCK, runs, width)).reshape(
            span, width
        )
        total_ref[own, :] = gnorm_ref[own, :] + spread
        inner_at = pl.ds(pl.multiple_of(group * span + place_ref[INNER], BLOCK), BLOCK)
        outer_at = pl.ds(pl.multiple_of(group * span + place_ref[OUTER], BLOCK), BLOCK)
        total_ref[inner_at, :] = total_ref[inner_at, :] + got_ref[group, :BLOCK, :]
        total_ref[outer_at, :] = total_ref[outer_at, :] + outer_ref[group]
    out_ref[...] = gmid_ref[...] + norm_grad(
        total_ref[...], unit_ref[...], inv_ref[...], gain_ref[...]
    )


def pair_matrix(few, many):
    row_ids = lax.broadcasted_iota(jnp.int32, (few, many), 0)
    col_ids = lax.broadcasted_iota(jnp.int32, (few, many), 1)
    return jnp.where(col_ids // 2 == row_ids, 0.5, 0.0).astype(bf16)


def coarser_kernel(slot, place_ref, own_ref, got_ref, out_ref):
    half = BLOCK // 2
    bit = place_ref[slot]
    matrix = pair_matrix(half, BLOCK)
    for ref, at in ((own_ref, bit), (got_ref, 1 - bit)):
        start = ref.shape[1] - BLOCK
        at = pl.multiple_of(at * half, half)
        for group in range(ref.shape[0]):
            out_ref[group, pl.ds(at, half), :] = exact_dot2(
                matrix, split(ref[group, start:, :])
            )


def finer_kernel(slot, with_rim, passing, place_ref, *refs):
    wide_ref, refs = refs[-1], refs[:-1]
    if passing:
        refs[-1][...] = refs[0][...]
        refs = refs[1:-1]
    mine_ref, send_ref = refs[-2:]
    *sums, part_ref = refs[: -2 - with_rim]
    half = BLOCK // 2
    bit = place_ref[slot]
    offset = send_ref.shape[1] - BLOCK
    matrix = pair_matrix(half, BLOCK)
    for group in range(mine_ref.shape[0]):
        if with_rim:
            send_ref[group, :BLOCK, :] = refs[-3][group]
        wide = sums[0][group]
        for other in sums[1:]:
            wide = wide + other[group]
        wide_ref[...] = wide

        def handed(at):
            at = pl.ds(pl.multiple_of(at * half, half), half)
            return exact_dot2(matrix, split(wide_ref[at, :]), 0, 0)

        mine_ref[group] = handed(bit)
        send_ref[group, offset:, :] = handed(1 - bit) + part_ref[group]


def fold_kernel(slot, size, extra, place_ref, keep_ref, got_ref, *refs):
    if extra == "fresh":
        fresh_ref, refs = refs[0], refs[1:]
    if slot is None:
        refs[0][...] = keep_ref[:size, :] + got_ref[:size, :]
        if extra:
            refs[1][...] = keep_ref[size:, :] + got_ref[size:, :]
        return
    half = size // 2
    bit = place_ref[slot]
    for target, side in zip(refs, (bit, 1 - bit)):
        at = pl.ds(pl.multiple_of(side * half, half), half)
        target[:half, :] = keep_ref[at, :] + got_ref[at, :]
        if extra == "fresh":
            target[half:, :] = fresh_ref[...]
        elif extra:
            target[half:, :] = keep_ref[size:, :] + got_ref[size:, :]


def share_kernel(size, extra, place_ref, keep_ref, got_ref, *refs):
    keep, send = refs
    keep[...] = keep_ref[...] + got_ref[...]
    send[...] = keep[...]


def join_kernel(slot, place_ref, own_ref, got_ref, *refs):
    out_ref = refs[-1]
    half = own_ref.shape[0]
    bit = place_ref[slot]
    for source, side in ((own_ref, bit), (got_ref, 1 - bit)):
        out_ref[pl.ds(pl.multiple_of(side * half, half), half), :] = source[...]
    if len(refs) == 2:
        out_ref[2 * half :, :] = refs[0][...]


def run_copies(copies, sems):
    copies = [
        pltpu.make_async_copy(source, target, sems.at[index])
        for index, (source, target) in enumerate(copies)
    ]
    for copy in copies:
        copy.start()
    for copy in copies:
        copy.wait()


def place_outer_kernel(place_ref, own_ref, sib_ref, out_ref, sems):
    core, size = place_ref[CORE], own_ref.shape[0]
    run_copies(
        [
            (source, out_ref.at[pl.ds(pl.multiple_of(side * size, size), size), :])
            for source, side in ((own_ref, core), (sib_ref, 1 - core))
        ],
        sems,
    )


def place_inner_kernel(place_ref, own_ref, sib_ref, out_ref, sems):
    core, size = place_ref[CORE], out_ref.shape[0]
    copies = []
    for source, side in ((own_ref, core), (sib_ref, 1 - core)):
        for index in range(2):
            at = pl.ds(pl.multiple_of((side * 2 + index) * size, size), size)
            copies.append((source.at[index * size : (index + 1) * size, :], out_ref.at[:, at]))
    run_copies(copies, sems)


def place_square_kernel(part, place_ref, own_ref, sib_ref, *refs):
    *outs, sems = refs[-5:]
    half = outs[0].shape[0] // 2
    core = place_ref[CORE]
    copies = []
    for slot, out_ref in enumerate(outs):
        down, across = slot // 2 * half, slot % 2 * half
        for source, side in ((own_ref, core), (sib_ref, 1 - core)):
            at = pl.ds(pl.multiple_of(side * half, half), half)
            copies.append(
                (
                    source.at[down : down + half, across : across + half],
                    out_ref.at[at, part * half : (part + 1) * half],
                )
            )
    run_copies(copies, sems)


def vectors_kernel(own_ref, sib_ref, *outs):
    last = own_ref.shape[0] - SPARE
    vec_ref = own_ref[last:, :] + sib_ref[last:, :]
    for index, out in enumerate(outs):
        if index < 8:
            out[...] = vec_ref[index : index + 1, :]
        else:
            width = vec_ref.shape[-1]
            for part in range(4):
                out[:, part * width : (part + 1) * width] = vec_ref[8 + part : 9 + part, :]


def level_tables(span, crossing):
    half = span // 2
    top = int(math.log2(span // BLOCK // 2)) + crossing
    local_top = top - crossing
    expand = np.zeros((span, span), np.float32)
    means = np.zeros((span, span), np.float32)
    levels, at = [], 0
    for level in range(1, top + 1):
        count = span >> level
        for row in range(count):
            expand[at + row, row << level : (row + 1) << level] = 1.0
            means[at + row, row << level : (row + 1) << level] = 0.5**level
        levels.append((level, at, count))
        at += count
    near = np.full((half + 2 * BLOCK, half), FAR, np.float32)
    for query_block in range(half // BLOCK):
        near[
            query_block * BLOCK : (query_block + 3) * BLOCK,
            query_block * BLOCK : (query_block + 1) * BLOCK,
        ] = 0.0
    local_rows = sum(count for level, _, count in levels if level <= local_top)
    coarse = np.full((local_rows + BLOCK * crossing, span), FAR, np.float32)
    for level, start, count in levels:
        if level <= local_top:
            for block in range(count // BLOCK):
                key = start + (block ^ 1) * BLOCK
                query = start + block * BLOCK
                coarse[key : key + BLOCK, query : query + BLOCK] = level
        else:
            key = local_rows + (level - local_top - 1) * BLOCK
            coarse[key : key + BLOCK, start : start + count] = level
    one = coarse[:half, :half]
    rest = coarse[half:, half:]
    twice = lambda table: jnp.asarray(np.concatenate([table, table], axis=1))
    return (
        jnp.asarray(expand, bf16),
        jnp.asarray(means, bf16),
        twice(near),
        twice(one),
        twice(rest),
    )


class Here:
    def __init__(self, span, seq_count, steps):
        self.span, self.seq_count, self.steps = span, seq_count, steps

    def __getitem__(self, slot):
        seq, batch = lax.axis_index("seq"), lax.axis_index("batch")
        odd, core = seq & 1, batch & 1
        if slot == INNER:
            return (1 - odd) * (self.span - BLOCK)
        if slot == OUTER:
            return odd * (self.span - BLOCK)
        if slot == ODD:
            return odd
        if slot == FIRST:
            return (seq == 0).astype(jnp.int32)
        if slot == LAST:
            return (seq == self.seq_count - 1).astype(jnp.int32)
        if slot == CORE:
            return core
        slot -= CORE + 1
        crossing = self.seq_count.bit_length() - 1
        if slot < crossing:
            return seq >> slot & 1
        sides = [(batch, seq)[axis] >> bit & 1 for axis, bit in self.steps[slot - crossing]]
        return sides[0] + core * (sides[1] - sides[0])


class Order:
    def __init__(self):
        self.last = None

    def call(self, kernel, outs, ins, tag="", scratch=(), limit=8, spaces=None, out_space=VMEM,
             aliases=None):
        shapes = tuple(
            shape if isinstance(shape, jax.ShapeDtypeStruct) else jax.ShapeDtypeStruct(shape, f32)
            for shape in outs
        )
        spaces, aliases = spaces or {}, aliases or {}
        given = [index for index, value in enumerate(ins) if not isinstance(value, Here)]
        count, before = len(given), [] if self.last is None else [self.last]
        first_out = count + len(before)
        last_out = first_out + len(outs)

        def body(*refs):
            refs[last_out][...] = jnp.zeros(TOKEN, f32)
            taken = list(ins)
            for index, ref in zip(given, refs):
                taken[index] = ref
            kernel(*taken, *refs[first_out:last_out], *refs[last_out + 1 :])

        *results, self.last = pl.pallas_call(
            body,
            out_shape=shapes + (jax.ShapeDtypeStruct(TOKEN, f32),),
            in_specs=[spaces.get(index, VMEM) for index in given] + [ANY] * len(before),
            out_specs=tuple(out_space for _ in outs) + (VMEM,),
            name=getattr(kernel, "func", kernel).__name__ + str(tag),
            scratch_shapes=list(scratch),
            input_output_aliases={given.index(index): out for index, out in aliases.items()},
            cost_estimate=pl.CostEstimate(
                flops=COST, bytes_accessed=0, transcendentals=0
            ),
            compiler_params=pltpu.CompilerParams(vmem_limit_bytes=limit << 20),
        )(*[ins[index] for index in given], *before)
        return results


class Everywhere:
    def __init__(self, batch_count, seq_count):
        self.counts = batch_count, seq_count
        across = batch_count.bit_length() - 1
        along = seq_count.bit_length() - 1
        wide = [(0, bit) for bit in range(1, across)]
        tail = [(1, bit) for bit in range(1, along)]
        self.steps = list(zip(wide + [(1, 0)] + tail, [(1, 0)] + wide + tail))
        self.core = ((0, 0), (0, 0))

    def swap(self, array, step):
        batch_count, seq_count = self.counts
        pairs = []
        for batch in range(batch_count):
            for seq in range(seq_count):
                axis, bit = step[batch % 2]
                other = (batch ^ 1 << bit, seq) if axis == 0 else (batch, seq ^ 1 << bit)
                pairs.append((batch * seq_count + seq, other[0] * seq_count + other[1]))
        return lax.ppermute(array, ("batch", "seq"), pairs)

    def chunk(self, call, place, slot, kept, got, extra=None):
        size, width = kept.shape
        more = 0 if extra is None else extra.shape[0]
        keep = kept
        for index, step in enumerate(self.steps):
            fresh = extra is not None and index == 0
            mode = "fresh" if fresh else extra is not None
            keep, send = call(
                functools.partial(fold_kernel, slot + index, size, mode),
                [(size // 2 + more, width)] * 2,
                [place, keep, got] + ([extra] if fresh else []),
            )
            size //= 2
            got = self.swap(send, step)
            if index + 2 == len(self.steps):
                break
            yield
        yield
        keep, send = call(
            functools.partial(share_kernel, size, more),
            [(size + more, width)] * 2, [place, keep, got],
        )
        got = self.swap(send, self.steps[-1])
        yield
        own = call(
            functools.partial(fold_kernel, None, size, extra is not None),
            [(size, width)] + ([(more, width)] if more else []), [place, keep, got],
        )
        own, rest = own[0], own[1:]
        for index in range(len(self.steps) - 2, -1, -1):
            got = self.swap(own, self.steps[index])
            yield
            last = list(rest) if index == 0 else []
            (own,) = call(
                functools.partial(join_kernel, slot + index),
                [(2 * size + (more if last else 0), width)], [place, own, got] + last,
            )
            size *= 2
        return own, self.swap(own, self.core)


class Run:
    def __init__(self, turns):
        self.turns, self.result = turns, None

    def step(self, count=1):
        for _ in range(count if self.result is None else 0):
            try:
                next(self.turns)
            except StopIteration as end:
                self.result = end.value


def per_device(
    inputs, norm_gain, norm_bias, query_weight, query_bias, key_weight, value_weight, value_bias,
    mixer_weight, mixer_bias, final_gain, final_bias, inner_weight, inner_bias, outer_weight,
    outer_bias, cotangent,
):
    groups, span, width = inputs.shape
    tokens = groups * span
    half = span // 2
    hidden_width = inner_weight.shape[1]
    block = hidden_width // 4
    seq_count, batch_count = lax.axis_size("seq"), lax.axis_size("batch")
    crossing = seq_count.bit_length() - 1
    far_rows = BLOCK * crossing
    expand, means, near, one, rest = level_tables(span, crossing)
    coarse = means.shape[0]
    row = lambda vec: vec.reshape(1, -1)
    scale = 1.0 / math.sqrt(width // HEADS)
    x = inputs.reshape(tokens, width)
    cot = cotangent.reshape(tokens, width)
    everywhere = Everywhere(batch_count, seq_count)
    seq_slot = CORE + 1
    step_slot = seq_slot + crossing
    place = Here(span, seq_count, everywhere.steps)
    inner_pairs = [(i, i ^ 1) for i in range(seq_count)]
    outer_pairs = [
        (i, j)
        for i in range(seq_count)
        for j in [i + 1 if i % 2 else i - 1]
        if 0 <= j < seq_count
    ]
    order = Order()
    gain, shift = row(norm_gain), row(norm_bias)
    part_of_feed = hidden_width // 2
    narrow = lambda *shape: jax.ShapeDtypeStruct(shape, bf16)
    at = types.SimpleNamespace(hidden={}, gib={}, pairs={}, kept={}, got={}, fine={}, rough={})
    sums, turns = {}, {}

    call = order.call

    def start_sum(name, send, extra=None):
        at.got[name] = everywhere.swap(send, everywhere.core)

    def turn(name):
        if name not in sums:
            turns[name] = 0
            extra = at.vec if name == "D" else None
            sums[name] = Run(
                everywhere.chunk(
                    lambda *rest: call(*rest, name + str(turns[name])), place, step_slot, at.kept[name], at.got[name],
                    extra,
                )
            )
        sums[name].step()
        turns[name] += 1

    def first_norm():
        at.unit, at.inv, at.inner_send, outer_send = call(
            functools.partial(first_norm_kernel, groups, span),
            [(tokens, width), (tokens, 1), (groups, 2 * BLOCK, width), (groups, BLOCK, width)],
            [place, x],
        )
        at.far = [lax.ppermute(at.inner_send, "seq", inner_pairs)]
        at.outer_got = lax.ppermute(outer_send, "seq", outer_pairs)
        at.coarse_own = at.inner_send

    def project(kinds):
        weights = {"q": query_weight, "k": key_weight, "v": value_weight}
        biases = {"q": [row(query_bias)], "k": [], "v": [row(value_bias)]}
        scales = {"q": scale * LOG2E, "k": None, "v": 1.0}
        outs = call(
            functools.partial(project_kernel, groups, span, [scales[kind] for kind in kinds]),
            [(tokens, width), (groups * coarse, width)] * len(kinds),
            [at.unit, gain, shift, means] + [weights[kind] for kind in kinds]
            + [bias for kind in kinds for bias in biases[kind]], kinds,
        )
        for index, kind in enumerate(kinds):
            at.fine[kind], at.rough[kind] = outs[2 * index], outs[2 * index + 1]

    def project_qk():
        project("qk")

    def project_v():
        project("v")

    def coarser():
        bit = len(at.far)
        (at.coarse_own,) = call(
            functools.partial(coarser_kernel, seq_slot + bit - 1),
            [(groups, BLOCK, width)], [place, at.coarse_own, at.far[-1]],
        )
        at.far.append(
            lax.ppermute(at.coarse_own, "seq", [(i, i ^ 1 << bit) for i in range(seq_count)])
        )

    def rest_coarser():
        while len(at.far) < crossing:
            coarser()

    def local():
        at.num, at.den, at.numc, at.denc, at.halo, at.hk, at.hv = call(
            functools.partial(local_kernel, groups, span),
            [(groups * width, span), (groups * HEADS, span), (groups * width, half),
             (groups * HEADS, half)] + [(groups * 2 * BLOCK, width)] * 3,
            [place] + [at.fine[kind] for kind in "qkv"] + [at.rough[kind] for kind in "qkv"]
            + [at.far[0], at.outer_got, gain, shift, key_weight, value_weight,
               row(value_bias), near, one],
            scratch=[pltpu.VMEM((2,) + near.shape, f32)],
        )

    def remote():
        ins = at.far + [x, at.num, at.den, at.numc, at.denc]
        ins += [at.rough[kind] for kind in "qkv"]
        ins += [
            gain, shift, key_weight, value_weight, row(value_bias), rest, expand, mixer_weight,
            row(mixer_bias), row(final_gain), row(final_bias), row(outer_bias), cot,
        ]
        (
            at.far_rows, at.rk, at.rv, at.mixed, at.rden, at.unit2, at.inv2,
            at.acc, *at.split
        ) = call(
            functools.partial(remote_kernel, groups, span, crossing),
            [(groups * far_rows, width)] * 3 + [(groups * width, span), (groups * HEADS, span),
             (tokens, width), (tokens, 1), (tokens, width)] + [narrow(tokens, width)] * 4,
            ins, scratch=[pltpu.VMEM((tokens, width), f32)],
        )

    def outer(own):
        joint, *at.hidden[own] = call(
            functools.partial(outer_kernel, own),
            [(part_of_feed, width)] + [narrow(tokens, part_of_feed)] * 2 + [(tokens, part_of_feed)],
            [place] + at.split + [inner_weight, row(inner_bias)], own, limit=16,
        )
        if own:
            at.kept["A"] = joint
        else:
            start_sum("A", joint)

    def inner(own):
        joint, at.gib[own], at.acc, at.gacc = call(
            functools.partial(inner_kernel, own),
            [(2 * width, part_of_feed // 2), (1, part_of_feed), (tokens, width), (tokens, width)],
            [place] + at.split + at.hidden[own] + [inner_weight, outer_weight, at.acc]
            + ([at.gacc] if own else []),
            own, limit=16,
        )
        if own:
            at.kept["B"] = joint
        else:
            start_sum("B", joint)

    def middle_grad():
        (
            at.gmid, at.gmw, at.vec_mid, at.gnum, at.gnumt, at.gden, at.gnumct,
            at.gdenc,
        ) = call(
            functools.partial(middle_grad_kernel, groups, span),
            [(tokens, width), (width, width), (8, width), (tokens, width), (groups * width, span),
             (groups * HEADS, span), (groups * width, coarse), (groups * HEADS, coarse)],
            [cot, at.gacc, at.unit2, at.inv2, row(final_gain), at.mixed, at.rden,
             mixer_weight, expand],
        )

    outside_rows = groups * (2 * BLOCK + far_rows)

    def pairs(part):
        at.pairs[part] = call(
            functools.partial(pairs_grad_kernel, groups, part, span),
            [(tokens, half_width)] * 3 + [(outside_rows, half_width)] * 2,
            [place] + [at.fine[kind] for kind in "qkv"] + [at.rough[kind] for kind in "qkv"]
            + [at.hk, at.hv, at.rk, at.rv, at.gnum, at.gnumt, at.gden, at.gnumct, at.gdenc, near, one,
               rest, means], part,
            scratch=[
                pltpu.VMEM((2,) + near.shape, f32),
                pltpu.VMEM((span + 2 * BLOCK, half_width), f32),
                pltpu.VMEM((span + 2 * BLOCK, half_width), f32),
                pltpu.VMEM((half + rest.shape[0], half_width), f32),
                pltpu.VMEM((half + rest.shape[0], half_width), f32),
                pltpu.VMEM((half_width, span), f32),
                pltpu.VMEM((half_width, coarse), f32),
            ],
        )

    half_width = width // 2

    def square(part):
        name = "CD"[part]
        at.kept[name], send = call(
            functools.partial(square_grad_kernel, part, scale),
            [(width, width)] * 2,
            [place, at.unit, at.halo, at.far_rows, gain, shift, at.gmw]
            + list(at.pairs[part]), part,
            scratch=[pltpu.VMEM((3, width, half_width), f32)],
        )
        start_sum(name, send)

    def rows_grad():
        at.vec, at.gnorm, at.inner_back, outer_back, *gfar = call(
            functools.partial(rows_grad_kernel, groups, crossing, scale),
            [(SPARE, width), (tokens, width)] + [(groups, BLOCK, width)] * (2 + crossing),
            [place, at.unit, at.halo, at.far_rows] + list(at.pairs[0])
            + list(at.pairs[1]) + [query_weight, key_weight, value_weight, at.vec_mid,
                                     at.gib[0], at.gib[1]],
        )
        at.outer_back = lax.ppermute(outer_back, "seq", outer_pairs)
        at.gfar = gfar
        at.back = [
            lax.ppermute(gfar[-1], "seq", [(i, i ^ 1 << crossing - 1) for i in range(seq_count)])
        ]
        at.back_bit = crossing - 1

    def finer():
        at.back_bit -= 1
        bit = at.back_bit
        rim = [] if bit else [at.inner_back]
        passing = [at.outer_back] if bit == crossing - 2 else []
        mine, send, *passed = call(
            functools.partial(finer_kernel, seq_slot + bit, len(rim), bool(passing)),
            [(groups, BLOCK, width), (groups, BLOCK * (1 + len(rim)), width)]
            + [value.shape for value in passing],
            [place] + passing + at.back + [at.gfar[bit]] + rim,
            scratch=[pltpu.VMEM((BLOCK, width), f32)],
        )
        if passed:
            at.outer_back = passed[0]
        at.back = [
            lax.ppermute(send, "seq", [(i, i ^ 1 << bit) for i in range(seq_count)]), mine
        ]

    def first_grad():
        while at.back_bit:
            finer()
        (at.inputs_grad,) = call(
            functools.partial(first_grad_kernel, groups, span),
            [(tokens, width)],
            [place, at.gmid, at.gnorm] + at.back
            + [at.outer_back, at.unit, at.inv, gain],
            scratch=[pltpu.VMEM((tokens, width), f32)],
        )

    def write(name, kernel, shapes, count, before=()):
        while name not in sums or sums[name].result is None:
            turn(name)
        ins = [place] + list(sums[name].result) + list(before)
        return call(
            kernel, shapes, ins, name, scratch=[pltpu.SemaphoreType.DMA((count,))],
            out_space=HBM, spaces={3 + index: HBM for index in range(len(before))},
            aliases={3 + index: index for index in range(len(before))},
        )

    def write_outer():
        at.gow = write("A", place_outer_kernel, [(hidden_width, width)], 2)

    def write_inner():
        at.giw = write("B", place_inner_kernel, [(width, hidden_width)], 4)

    def write_square(part):
        at.squares = write(
            "CD"[part], functools.partial(place_square_kernel, part), [(width, width)] * 4, 8,
            getattr(at, "squares", ()),
        )
        if part:
            at.vecs = call(
                vectors_kernel, [(1, width)] * 8 + [(1, hidden_width)],
                list(sums["D"].result),
            )

    acts = (
        first_norm, project_qk, project_v, coarser, rest_coarser, local, remote, outer, inner,
        middle_grad, pairs, square, rows_grad, finer, first_grad, write_outer, write_inner,
        write_square,
    )
    acts = {act.__name__: act for act in acts}
    for name in PLAN:
        if name.isupper():
            turn(name)
        else:
            acts[name.rstrip("01")](*[int(digit) for digit in name if digit.isdigit()])
    gng, gnb, gqb, gvb, gfg, gfb, gmb, gob, gib = [vec.reshape(-1) for vec in at.vecs]
    gqw, gkw, gvw, gmw = at.squares
    return (
        at.acc.reshape(inputs.shape), at.inputs_grad.reshape(inputs.shape), gng, gnb, gqw,
        gqb, gkw, gvw, gvb, gmw, gmb, gfg, gfb, at.giw[0], gib, at.gow[0], gob,
    )


def solution(mesh):
    split_spec = P("batch", "seq", None)
    return jax.shard_map(
        per_device,
        mesh=mesh,
        in_specs=(split_spec,) + (P(),) * 15 + (split_spec,),
        out_specs=(split_spec, split_spec) + (P(),) * 15,
        check_vma=False,
    )
```

```python
import functools
import math
import types

import jax
import jax.numpy as jnp
import numpy as np
from jax import lax
from jax.experimental import pallas as pl
from jax.experimental.pallas import tpu as pltpu
from jax.sharding import PartitionSpec as P

HEADS = 8
BLOCK = 16
LOG2E = 1.4426950408889634
LN2 = 0.6931471805599453
ROOT_HALF = 0.7071067811865476
INV_ROOT_TWO_PI = 0.3989422804014327
EPS = 1e-06
FAR = -1e30
SPARE = 16
TOKEN = (8, 128)
PLAN = (
    "first_norm", "project_qk", "project_v", "coarser", "rest_coarser", "local", "remote",
    "outer0", "outer1", "inner0", "A", "inner1", "B", "middle_grad", "pairs0", "square0", "B",
    "pairs1", "A", "B", "rows_grad", "B", "C", "A", "square1", "A", "finer", "D", "C", "B",
    "finer", "C", "D", "B", "A", "D", "C", "A", "C", "first_grad", "D", "A", "C", "B", "C", "D",
    "D", "B", "D", "C", "A", "write_inner", "D", "write_square0", "write_outer", "write_square1",
)
EARLY = "A"
COST = 10**10
INNER, OUTER, ODD, FIRST, LAST, CORE = range(6)

bf16 = jnp.bfloat16
f32 = jnp.float32
VMEM = pl.BlockSpec(memory_space=pltpu.VMEM)
ANY = pl.BlockSpec(memory_space=pl.ANY)
HBM = pl.BlockSpec(memory_space=pltpu.MemorySpace.HBM)


def split(value):
    high = value.astype(bf16)
    return high, (value - high.astype(f32)).astype(bf16)


def dg(left, right, left_dim=1, right_dim=0):
    return lax.dot_general(
        left, right, (((left_dim,), (right_dim,)), ((), ())), preferred_element_type=f32
    )


def dot3(left, right, left_dim=1, right_dim=0):
    return (
        dg(left[0], right[0], left_dim, right_dim)
        + dg(left[0], right[1], left_dim, right_dim)
        + dg(left[1], right[0], left_dim, right_dim)
    )


def dot2(left, exact, left_dim=1, right_dim=0):
    return dg(left[0], exact, left_dim, right_dim) + dg(left[1], exact, left_dim, right_dim)


def exact_dot2(exact, right, left_dim=1, right_dim=0):
    return dg(exact, right[0], left_dim, right_dim) + dg(exact, right[1], left_dim, right_dim)


def two_diagonal(pair_rows):
    half = pair_rows.shape[0] // 2
    zero = jnp.zeros((half, pair_rows.shape[1]), pair_rows.dtype)
    return jnp.concatenate(
        [
            jnp.concatenate([pair_rows[:half], zero], axis=1),
            jnp.concatenate([zero, pair_rows[half:]], axis=1),
        ],
        axis=0,
    )


def two_masked(pair_lanes):
    half = pair_lanes.shape[1] // 2
    lower = lax.broadcasted_iota(jnp.int32, pair_lanes.shape, 1) < half
    wide = pair_lanes.astype(f32)
    return jnp.concatenate(
        [jnp.where(lower, wide, 0.0), jnp.where(lower, 0.0, wide)], axis=0
    ).astype(bf16)


def take_diagonal(product):
    half, width = product.shape[0] // 2, product.shape[1] // 2
    return jnp.concatenate([product[:half, :width], product[half:, width:]], axis=0)


def pair_weights(keys, queries_t, bias):
    diag_high, diag_low = two_diagonal(queries_t[0]), two_diagonal(queries_t[1])
    scores = dg(
        jnp.concatenate([keys[0], keys[1], keys[0]], axis=1),
        jnp.concatenate([diag_high, diag_high, diag_low], axis=0),
    )
    return jnp.exp2(scores + bias)


def tile_forward(keys, values_t, queries_t, bias):
    weights = pair_weights(keys, queries_t, bias)
    denominator = jnp.sum(weights, axis=0, keepdims=True)
    high, low = split(weights)
    wide = dg(jnp.concatenate([values_t[0], values_t[1]], axis=0), high)
    size = values_t[0].shape[0]
    product = wide[:size] + wide[size:] + dg(values_t[0], low)
    width = denominator.shape[1] // 2
    return (
        take_diagonal(product),
        jnp.concatenate([denominator[:, :width], denominator[:, width:]], axis=0),
    )


def tile_backward(keys, keys_t, values, queries_t, queries_m, grads_t, grads_m, grad_den, bias):
    weights = pair_weights(keys, queries_t, bias)
    diag_high, diag_low = two_diagonal(grads_t[0]), two_diagonal(grads_t[1])
    grad_weights = (
        dg(
            jnp.concatenate([values[0], values[1], values[0]], axis=1),
            jnp.concatenate([diag_high, diag_high, diag_low], axis=0),
        )
        + grad_den
    )
    scores = split(weights * grad_weights)
    weights = split(weights)

    def gather(pairs, masked):
        wide = dg(pairs[0], jnp.concatenate([masked[0], masked[1]], axis=1))
        half = wide.shape[1] // 2
        return wide[:, :half] + wide[:, half:] + dg(pairs[1], masked[0])

    grad_values = gather(weights, grads_m)
    grad_keys = gather(scores, queries_m)
    wide = dg(jnp.concatenate([keys_t[0], keys_t[1]], axis=0), scores[0])
    size = keys_t[0].shape[0]
    product = wide[:size] + wide[size:] + dg(keys_t[0], scores[1])
    return take_diagonal(product), grad_keys, grad_values


def lanes(parts, start, size):
    return tuple(part[:, start : start + size] for part in parts)


def rows(parts, start, size):
    return tuple(part[start : start + size] for part in parts)


def block_of(parts, row, row_size, lane, lane_size):
    return tuple(part[row : row + row_size, lane : lane + lane_size] for part in parts)


def stack(first, second):
    return tuple(jnp.concatenate([one, two], axis=0) for one, two in zip(first, second))


def norm_rows(values):
    center = values - jnp.mean(values, axis=-1, keepdims=True)
    inverse = lax.rsqrt(jnp.mean(center * center, axis=-1, keepdims=True) + EPS)
    return center * inverse, inverse


def norm_grad(grad_rows, unit_rows, inverse, gain):
    grad_unit = grad_rows * gain
    return inverse * (
        grad_unit
        - jnp.mean(grad_unit, axis=-1, keepdims=True)
        - unit_rows * jnp.mean(grad_unit * unit_rows, axis=-1, keepdims=True)
    )


def first_norm_kernel(groups, span, place_ref, x_ref, unit_ref, inv_ref, inner_ref, outer_ref):
    width = x_ref.shape[-1]
    for group in range(groups):
        own = slice(group * span, (group + 1) * span)
        unit, inverse = norm_rows(x_ref[own, :])
        unit_ref[own, :] = unit
        inv_ref[own, :] = inverse
        runs = span // BLOCK
        inner_ref[group, BLOCK:, :] = jnp.mean(unit.reshape(BLOCK, runs, width), axis=1)
        inner_start = pl.multiple_of(group * span + place_ref[INNER], BLOCK)
        outer_start = pl.multiple_of(group * span + place_ref[OUTER], BLOCK)
        inner_ref[group, :BLOCK, :] = unit_ref[pl.ds(inner_start, BLOCK), :]
        outer_ref[group] = unit_ref[pl.ds(outer_start, BLOCK), :]


def project_kernel(groups, span, scales, unit_ref, gain_ref, shift_ref, mean_ref, *refs):
    count = len(scales)
    weights, refs = refs[:count], refs[count:]
    biased = [scale is not None for scale in scales]
    biases, outs = list(refs[: sum(biased)]), refs[sum(biased) :]
    normed = split(unit_ref[...] * gain_ref[...] + shift_ref[...])
    means = mean_ref[...]
    coarse = means.shape[0]
    for index, (weight, scale) in enumerate(zip(weights, scales)):
        result = dot3(normed, split(weight[...]))
        if scale is not None:
            result = result + biases.pop(0)[...]
            if scale != 1.0:
                result = result * scale
        outs[2 * index][...] = result
        for group in range(groups):
            part = split(result[group * span : (group + 1) * span])
            outs[2 * index + 1][group * coarse : (group + 1) * coarse, :] = exact_dot2(means, part)


def fill_bias(bias_ref, near_ref, place_ref):
    rows_total = near_ref.shape[0]
    bias_ref[0] = near_ref[...]
    bias_ref[1] = near_ref[...]
    before = place_ref[FIRST].astype(f32) * FAR
    after = place_ref[LAST].astype(f32) * FAR
    bias_ref[0, :BLOCK, :] = near_ref[:BLOCK, :] + before
    bias_ref[1, rows_total - BLOCK :, :] = near_ref[rows_total - BLOCK :, :] + after


def local_kernel(
    groups, span, place_ref, q_ref, k_ref, v_ref, qc_ref, kc_ref, vc_ref, inner_ref, outer_ref,
    gain_ref, shift_ref, kw_ref, vw_ref, vb_ref, near_ref, one_ref,
    num_ref, den_ref, numc_ref, denc_ref, halo_ref, hk_ref, hv_ref, bias_ref,
):
    width = q_ref.shape[-1]
    half = span // 2
    coarse = qc_ref.shape[0] // groups
    pairs = HEADS // 2
    pair_width = width // pairs
    tile_keys = half + 2 * BLOCK
    fill_bias(bias_ref, near_ref, place_ref)
    odd = place_ref[ODD].astype(f32)
    for group in range(groups):
        inner, outer = inner_ref[group, :BLOCK, :], outer_ref[group]
        at = group * 2 * BLOCK
        halo_ref[at : at + BLOCK, :] = inner * odd + outer * (1.0 - odd)
        halo_ref[at + BLOCK : at + 2 * BLOCK, :] = inner * (1.0 - odd) + outer * odd
    normed = split(halo_ref[...] * gain_ref[...] + shift_ref[...])
    halo_keys = dot3(normed, split(kw_ref[...]))
    halo_values = dot3(normed, split(vw_ref[...])) + vb_ref[...]
    hk_ref[...] = halo_keys
    hv_ref[...] = halo_values
    for group in range(groups):
        own = slice(group * span, (group + 1) * span)
        left = slice(group * 2 * BLOCK, group * 2 * BLOCK + BLOCK)
        right = slice(group * 2 * BLOCK + BLOCK, (group + 1) * 2 * BLOCK)
        own_c = slice(group * coarse, group * coarse + half)
        keys = split(jnp.concatenate([halo_keys[left], k_ref[own, :], halo_keys[right]], axis=0))
        values = jnp.concatenate([halo_values[left], v_ref[own, :], halo_values[right]], axis=0)
        values_t = split(values.T)
        queries_t = split(q_ref[own, :].T)
        keys_c = split(kc_ref[own_c, :])
        values_ct = split(vc_ref[own_c, :].T)
        queries_ct = split(qc_ref[own_c, :].T)
        for pair in range(pairs):
            at = pair * pair_width
            out = slice(group * width + at, group * width + at + pair_width)
            heads = slice((group * pairs + pair) * 2, (group * pairs + pair) * 2 + 2)
            for tile in range(2):
                num, den = tile_forward(
                    block_of(keys, tile * half, tile_keys, at, pair_width),
                    block_of(values_t, at, pair_width, tile * half, tile_keys),
                    block_of(queries_t, at, pair_width, tile * half, half),
                    bias_ref[tile],
                )
                num_ref[out, tile * half : (tile + 1) * half] = num
                den_ref[heads, tile * half : (tile + 1) * half] = den
            num, den = tile_forward(
                lanes(keys_c, at, pair_width),
                rows(values_ct, at, pair_width),
                rows(queries_ct, at, pair_width),
                one_ref[...],
            )
            numc_ref[out, :] = num
            denc_ref[heads, :] = den


def remote_kernel(
    groups, span, crossing, *refs
):
    far_parts, refs = refs[:crossing], refs[crossing:]
    (
        x_ref, num_ref, den_ref, numc_ref, denc_ref, qc_ref, kc_ref, vc_ref, gain_ref, shift_ref,
        kw_ref, vw_ref, vb_ref, rest_ref, expand_ref, mw_ref, mb_ref, fgain_ref, fshift_ref, ob_ref,
        cot_ref,
        far_ref, rk_ref, rv_ref, mixed_ref, rden_ref, unit_ref, inv_ref, acc_ref, fhigh_ref, flow_ref,
        chigh_ref, clow_ref, mid_ref,
    ) = refs
    width = x_ref.shape[-1]
    half = span // 2
    coarse = qc_ref.shape[0] // groups
    far = far_ref.shape[0] // groups
    pairs = HEADS // 2
    pair_width = width // pairs
    head_width = width // HEADS
    local_rest = rest_ref.shape[0] - far
    for group in range(groups):
        for level, part in enumerate(far_parts):
            at = group * far + level * BLOCK
            far_ref[at : at + BLOCK, :] = part[group, part.shape[1] - BLOCK :, :]
    normed = split(far_ref[...] * gain_ref[...] + shift_ref[...])
    far_keys = dot3(normed, split(kw_ref[...]))
    far_values = dot3(normed, split(vw_ref[...])) + vb_ref[...]
    rk_ref[...] = far_keys
    rv_ref[...] = far_values
    expand = expand_ref[...]
    for group in range(groups):
        rest = slice(group * coarse + half, group * coarse + half + local_rest)
        remote = slice(group * far, (group + 1) * far)
        keys = split(jnp.concatenate([kc_ref[rest, :], far_keys[remote]], axis=0))
        values_t = split(jnp.concatenate([vc_ref[rest, :], far_values[remote]], axis=0).T)
        queries_t = split(qc_ref[group * coarse + half : (group + 1) * coarse, :].T)
        nums, dens = [], []
        for pair in range(pairs):
            at = pair * pair_width
            num, den = tile_forward(
                lanes(keys, at, pair_width),
                rows(values_t, at, pair_width),
                rows(queries_t, at, pair_width),
                rest_ref[...],
            )
            nums.append(num)
            dens.append(den)
        own_t = slice(group * width, (group + 1) * width)
        own_h = slice(group * HEADS, (group + 1) * HEADS)
        numc = jnp.concatenate([numc_ref[own_t, :], jnp.concatenate(nums, axis=0)], axis=1)
        denc = jnp.concatenate([denc_ref[own_h, :], jnp.concatenate(dens, axis=0)], axis=1)
        num = num_ref[own_t, :] + dot2(split(numc), expand)
        den = den_ref[own_h, :] + dot2(split(denc), expand)
        inverse = 1.0 / den
        rden_ref[own_h, :] = inverse
        spread = jnp.concatenate(
            [
                jnp.broadcast_to(inverse[head : head + 1], (head_width, span))
                for head in range(HEADS)
            ],
            axis=0,
        )
        mixed_t = num * spread
        own = slice(group * span, (group + 1) * span)
        mixed_ref[own_t, :] = mixed_t
        mid_ref[own, :] = mixed_t.T
    middle = x_ref[...] + dot3(split(mid_ref[...]), split(mw_ref[...])) + mb_ref[...]
    unit, inverse = norm_rows(middle)
    unit_ref[...] = unit
    inv_ref[...] = inverse
    fhigh_ref[...], flow_ref[...] = split(unit * fgain_ref[...] + fshift_ref[...])
    chigh_ref[...], clow_ref[...] = split(cot_ref[...])
    acc_ref[...] = middle + ob_ref[...]


def half_of(own, place_ref, size):
    side = place_ref[CORE] if own else 1 - place_ref[CORE]
    return pl.ds(pl.multiple_of(side * size, size), size)


def outer_kernel(
    own, place_ref, fhigh_ref, flow_ref, chigh_ref, clow_ref, iw_ref, ib_ref,
    joint_ref, hhigh_ref, hlow_ref, slope_ref,
):
    units = half_of(own, place_ref, slope_ref.shape[1])
    inner = dot3((fhigh_ref[...], flow_ref[...]), split(iw_ref[:, units])) + ib_ref[:, units]
    cumulative = 0.5 * (1.0 + lax.erf(inner * ROOT_HALF))
    hidden = split(inner * cumulative)
    slope_ref[...] = cumulative + inner * jnp.exp(-0.5 * inner * inner) * INV_ROOT_TWO_PI
    hhigh_ref[...], hlow_ref[...] = hidden
    joint_ref[...] = dot3(hidden, (chigh_ref[...], clow_ref[...]), 0, 0)


def inner_kernel(
    own, place_ref, fhigh_ref, flow_ref, chigh_ref, clow_ref, hhigh_ref, hlow_ref, slope_ref,
    iw_ref, ow_ref, acc_ref, *refs
):
    giw_ref, gib_ref, nacc_ref, ngacc_ref = refs[-4:]
    units = half_of(own, place_ref, slope_ref.shape[1])
    cot = chigh_ref[...], clow_ref[...]
    hidden = hhigh_ref[...], hlow_ref[...]
    iw, ow = split(iw_ref[:, units]), split(ow_ref[units, :])
    grad_inner = dot3(cot, ow, 1, 1) * slope_ref[...]
    gib_ref[...] = jnp.sum(grad_inner, axis=0, keepdims=True)
    grad_inner = split(grad_inner)
    giw = dot3((fhigh_ref[...], flow_ref[...]), grad_inner, 0, 0)
    width = giw.shape[0]
    giw_ref[:width, :] = giw[:, :width]
    giw_ref[width:, :] = giw[:, width:]
    nacc_ref[...] = acc_ref[...] + dot3(hidden, ow)
    grad_fnorm = dot3(grad_inner, iw, 1, 1)
    ngacc_ref[...] = refs[0][...] + grad_fnorm if own else grad_fnorm


def middle_grad_kernel(
    groups, span, cot_ref, gf_ref, unit_ref, inv_ref, fgain_ref, mixed_ref, rden_ref, mw_ref,
    expand_ref,
    gmid_ref, gmw_ref, vec_ref, gnum_ref, gnumt_ref, gden_ref, gnumct_ref, gdenc_ref,
):
    width = cot_ref.shape[-1]
    head_width = width // HEADS
    cot = cot_ref[...]
    gf = gf_ref[...]
    unit = unit_ref[...]
    gmid = cot + norm_grad(gf, unit, inv_ref[...], fgain_ref[...])
    gmid_ref[...] = gmid
    vec_ref[0:1, :] = jnp.sum(gf * unit, axis=0, keepdims=True)
    vec_ref[1:2, :] = jnp.sum(gf, axis=0, keepdims=True)
    vec_ref[2:3, :] = jnp.sum(gmid, axis=0, keepdims=True)
    vec_ref[3:4, :] = jnp.sum(cot, axis=0, keepdims=True)
    gmid = split(gmid)
    expand = expand_ref[...]
    grad_mixed = dot3(gmid, split(mw_ref[...]), 1, 1)
    total = None
    for group in range(groups):
        own = slice(group * span, (group + 1) * span)
        own_t = slice(group * width, (group + 1) * width)
        own_h = slice(group * HEADS, (group + 1) * HEADS)
        mixed_t = mixed_ref[own_t, :]
        part = dot3(split(mixed_t), rows(gmid, group * span, span))
        total = part if total is None else total + part
        grad_t = grad_mixed[own].T
        inverse = rden_ref[own_h, :]
        spread = jnp.concatenate(
            [
                jnp.broadcast_to(inverse[head : head + 1], (head_width, span))
                for head in range(HEADS)
            ],
            axis=0,
        )
        product = grad_t * mixed_t
        dens = jnp.concatenate(
            [
                jnp.sum(product[head * head_width : (head + 1) * head_width], axis=0, keepdims=True)
                for head in range(HEADS)
            ],
            axis=0,
        )
        gden = -dens * inverse
        gnum_t = grad_t * spread
        gnumt_ref[own_t, :] = gnum_t
        gnum_ref[own, :] = gnum_t.T
        gden_ref[own_h, :] = gden
        gnumct_ref[own_t, :] = dot2(split(gnum_t), expand, 1, 1)
        gdenc_ref[own_h, :] = dot2(split(gden), expand, 1, 1)
    gmw_ref[...] = total


def pairs_grad_kernel(
    groups, part, span, place_ref, q_ref, k_ref, v_ref, qc_ref, kc_ref, vc_ref, hk_ref, hv_ref,
    rk_ref, rv_ref, gnum_ref, gnumt_ref, gden_ref, gnumct_ref, gdenc_ref, near_ref, one_ref,
    rest_ref, mean_ref,
    dq_ref, dk_ref, dv_ref, odk_ref, odv_ref,
    bias_ref, dkx_ref, dvx_ref, dkc_ref, dvc_ref, dqt_ref, dqct_ref,
):
    full = q_ref.shape[-1]
    width = full // 2
    half = span // 2
    coarse = qc_ref.shape[0] // groups
    far = rk_ref.shape[0] // groups
    pairs = HEADS // 4
    pair_width = width // pairs
    tile_keys = half + 2 * BLOCK
    local_rest = rest_ref.shape[0] - far
    local_coarse = half + local_rest
    rest_keys = local_rest + far
    ours = slice(part * width, (part + 1) * width)
    fill_bias(bias_ref, near_ref, place_ref)
    means = mean_ref[...]
    zero = jnp.zeros((coarse - local_coarse, width), f32)
    for group in range(groups):
        fine = slice(group * span, (group + 1) * span)
        rough = slice(group * coarse, group * coarse + coarse)
        near_rough = slice(group * coarse, group * coarse + local_coarse)
        left = slice(group * 2 * BLOCK, group * 2 * BLOCK + BLOCK)
        right = slice(group * 2 * BLOCK + BLOCK, (group + 1) * 2 * BLOCK)
        remote = slice(group * far, (group + 1) * far)
        ours_t = slice(group * full + part * width, group * full + (part + 1) * width)
        keys_f = jnp.concatenate(
            [hk_ref[left, ours], k_ref[fine, ours], hk_ref[right, ours]], axis=0
        )
        keys, keys_t = split(keys_f), split(keys_f.T)
        values = split(
            jnp.concatenate([hv_ref[left, ours], v_ref[fine, ours], hv_ref[right, ours]], axis=0)
        )
        q = q_ref[fine, ours]
        queries, queries_t = split(q), split(q.T)
        grads, grads_t = split(gnum_ref[fine, ours]), split(gnumt_ref[ours_t, :])
        keys_cf = jnp.concatenate([kc_ref[near_rough, ours], rk_ref[remote, ours]], axis=0)
        keys_c, keys_ct = split(keys_cf), split(keys_cf.T)
        values_c = split(
            jnp.concatenate([vc_ref[near_rough, ours], rv_ref[remote, ours]], axis=0)
        )
        qc = qc_ref[rough, ours]
        queries_c, queries_ct = split(qc), split(qc.T)
        gnumct = gnumct_ref[ours_t, :]
        grads_c, grads_ct = split(gnumct.T), split(gnumct)
        for pair in range(pairs):
            at = pair * pair_width
            cols = slice(at, at + pair_width)
            head = group * HEADS + part * (HEADS // 2) + 2 * pair

            def den_rows(ref, start):
                both = ref[head : head + 2, start : start + half]
                return jnp.concatenate([both[0:1], both[1:2]], axis=1)

            def masked(parts, start):
                return tuple(
                    two_masked(value) for value in block_of(parts, start, half, at, pair_width)
                )

            for tile in range(2):
                start = tile * half
                dq, dk, dv = tile_backward(
                    block_of(keys, start, tile_keys, at, pair_width),
                    block_of(keys_t, at, pair_width, start, tile_keys),
                    block_of(values, start, tile_keys, at, pair_width),
                    block_of(queries_t, at, pair_width, start, half),
                    masked(queries, start),
                    block_of(grads_t, at, pair_width, start, half),
                    masked(grads, start),
                    den_rows(gden_ref, start),
                    bias_ref[tile],
                )
                dqt_ref[cols, start : start + half] = dq
                if tile == 0:
                    dkx_ref[:tile_keys, cols] = dk
                    dvx_ref[:tile_keys, cols] = dv
                else:
                    shared = slice(start, start + 2 * BLOCK)
                    fresh = slice(start + 2 * BLOCK, start + tile_keys)
                    dkx_ref[shared, cols] = dkx_ref[shared, cols] + dk[: 2 * BLOCK]
                    dvx_ref[shared, cols] = dvx_ref[shared, cols] + dv[: 2 * BLOCK]
                    dkx_ref[fresh, cols] = dk[2 * BLOCK :]
                    dvx_ref[fresh, cols] = dv[2 * BLOCK :]
            for start, count, bias in ((0, half, one_ref), (half, rest_keys, rest_ref)):
                dq, dk, dv = tile_backward(
                    block_of(keys_c, start, count, at, pair_width),
                    block_of(keys_ct, at, pair_width, start, count),
                    block_of(values_c, start, count, at, pair_width),
                    block_of(queries_ct, at, pair_width, start, half),
                    masked(queries_c, start),
                    block_of(grads_ct, at, pair_width, start, half),
                    masked(grads_c, start),
                    den_rows(gdenc_ref, start),
                    bias[...],
                )
                dqct_ref[cols, start : start + half] = dq
                dkc_ref[start : start + count, cols] = dk
                dvc_ref[start : start + count, cols] = dv
        distant = slice(
            groups * 2 * BLOCK + group * far, groups * 2 * BLOCK + (group + 1) * far
        )
        odk_ref[distant, :] = dkc_ref[local_coarse:, :] * LN2
        odv_ref[distant, :] = dvc_ref[local_coarse:, :]
        odk_ref[left, :] = dkx_ref[:BLOCK, :] * LN2
        odk_ref[right, :] = dkx_ref[span + BLOCK :, :] * LN2
        odv_ref[left, :] = dvx_ref[:BLOCK, :]
        odv_ref[right, :] = dvx_ref[span + BLOCK :, :]

        def spread(ref):
            local = jnp.concatenate([ref[:local_coarse, :], zero], axis=0)
            return exact_dot2(means, split(local), 0, 0)

        dk_ref[fine, :] = (dkx_ref[BLOCK : span + BLOCK, :] + spread(dkc_ref)) * LN2
        dv_ref[fine, :] = dvx_ref[BLOCK : span + BLOCK, :] + spread(dvc_ref)
        dq_ref[fine, :] = (dqt_ref[...] + dot2(split(dqct_ref[...]), means)).T


def square_grad_kernel(
    part, scale, place_ref, unit_ref, halo_ref, far_ref, gain_ref, shift_ref, gmw_ref,
    dq_ref, dk_ref, dv_ref, odk_ref, odv_ref, own_ref, send_ref, full_ref,
):
    width = unit_ref.shape[-1]
    half = width // 2
    core = place_ref[CORE]
    mine = pl.ds(pl.multiple_of(core * half, half), half)
    other = pl.ds(pl.multiple_of((1 - core) * half, half), half)
    outside = jnp.concatenate([halo_ref[...], far_ref[...]], axis=0)
    normed = split(unit_ref[...] * gain_ref[...] + shift_ref[...])
    normed_out = split(outside * gain_ref[...] + shift_ref[...])
    full_ref[0] = dot3(normed, split(dq_ref[...] * scale), 0, 0)
    full_ref[1] = dot3(normed, split(dk_ref[...]), 0, 0) + dot3(
        normed_out, split(odk_ref[...]), 0, 0
    )
    full_ref[2] = dot3(normed, split(dv_ref[...]), 0, 0) + dot3(
        normed_out, split(odv_ref[...]), 0, 0
    )
    for target, at in ((own_ref, mine), (send_ref, other)):
        target[:half, :half] = full_ref[0, at, :]
        target[:half, half:] = full_ref[1, at, :]
        target[half:, :half] = full_ref[2, at, :]
        target[half:, half:] = gmw_ref[at, part * half : (part + 1) * half]


def rows_grad_kernel(groups, crossing, scale, place_ref, unit_ref, halo_ref, far_ref, *refs):
    parts, refs = (refs[:5], refs[5:10]), refs[10:]
    qw_ref, kw_ref, vw_ref, mid_ref = refs[:4]
    gib_refs, refs = refs[4:6], refs[6:]
    vec_ref, gnorm_ref, inner_ref, outer_ref = refs[:4]
    gfar_refs = refs[4:]
    joined = lambda index: jnp.concatenate([part[index][...] for part in parts], axis=1)
    width = unit_ref.shape[-1]
    unit = unit_ref[...]
    outside = jnp.concatenate([halo_ref[...], far_ref[...]], axis=0)
    dq_f, dv_f, odv_f = joined(0) * scale, joined(2), joined(4)
    dq, dk, dv = split(dq_f), split(joined(1)), split(dv_f)
    odk, odv = split(joined(3)), split(odv_f)
    qw, kw, vw = split(qw_ref[...]), split(kw_ref[...]), split(vw_ref[...])
    gnorm = dot3(dq, qw, 1, 1) + dot3(dk, kw, 1, 1) + dot3(dv, vw, 1, 1)
    gout = dot3(odk, kw, 1, 1) + dot3(odv, vw, 1, 1)
    gnorm_ref[...] = gnorm
    odd = place_ref[ODD].astype(f32)
    far = far_ref.shape[0] // groups
    for group in range(groups):
        at = group * 2 * BLOCK
        low, high = gout[at : at + BLOCK], gout[at + BLOCK : at + 2 * BLOCK]
        inner_ref[group] = low * odd + high * (1.0 - odd)
        outer_ref[group] = low * (1.0 - odd) + high * odd
        for level, gfar_ref in enumerate(gfar_refs):
            at = groups * 2 * BLOCK + group * far + level * BLOCK
            gfar_ref[group] = gout[at : at + BLOCK]
    first = place_ref[CORE].astype(f32)
    other_gib, own_gib = gib_refs[0][...], gib_refs[1][...]
    low_gib = own_gib * (1.0 - first) + other_gib * first
    high_gib = own_gib * first + other_gib * (1.0 - first)
    vec_ref[...] = jnp.concatenate(
        [
            jnp.sum(gnorm * unit, axis=0, keepdims=True)
            + jnp.sum(gout * outside, axis=0, keepdims=True),
            jnp.sum(gnorm, axis=0, keepdims=True) + jnp.sum(gout, axis=0, keepdims=True),
            jnp.sum(dq_f, axis=0, keepdims=True),
            jnp.sum(dv_f, axis=0, keepdims=True) + jnp.sum(odv_f, axis=0, keepdims=True),
            mid_ref[0:4, :],
            low_gib[:, :width],
            low_gib[:, width:],
            high_gib[:, :width],
            high_gib[:, width:],
            jnp.zeros((SPARE - 12, width), f32),
        ],
        axis=0,
    )


def first_grad_kernel(
    groups, span, place_ref, gmid_ref, gnorm_ref, got_ref, mine_ref, outer_ref, unit_ref, inv_ref,
    gain_ref, out_ref, total_ref,
):
    width = gmid_ref.shape[-1]
    runs = span // BLOCK
    for group in range(groups):
        own = slice(group * span, (group + 1) * span)
        four = (got_ref[group, BLOCK:, :] + mine_ref[group]) * (1.0 / runs)
        spread = jnp.broadcast_to(four.reshape(BLOCK, 1, width), (BLOCK, runs, width)).reshape(
            span, width
        )
        total_ref[own, :] = gnorm_ref[own, :] + spread
        inner_at = pl.ds(pl.multiple_of(group * span + place_ref[INNER], BLOCK), BLOCK)
        outer_at = pl.ds(pl.multiple_of(group * span + place_ref[OUTER], BLOCK), BLOCK)
        total_ref[inner_at, :] = total_ref[inner_at, :] + got_ref[group, :BLOCK, :]
        total_ref[outer_at, :] = total_ref[outer_at, :] + outer_ref[group]
    out_ref[...] = gmid_ref[...] + norm_grad(
        total_ref[...], unit_ref[...], inv_ref[...], gain_ref[...]
    )


def pair_matrix(few, many):
    row_ids = lax.broadcasted_iota(jnp.int32, (few, many), 0)
    col_ids = lax.broadcasted_iota(jnp.int32, (few, many), 1)
    return jnp.where(col_ids // 2 == row_ids, 0.5, 0.0).astype(bf16)


def coarser_kernel(slot, place_ref, own_ref, got_ref, out_ref):
    half = BLOCK // 2
    bit = place_ref[slot]
    matrix = pair_matrix(half, BLOCK)
    for ref, at in ((own_ref, bit), (got_ref, 1 - bit)):
        start = ref.shape[1] - BLOCK
        at = pl.multiple_of(at * half, half)
        for group in range(ref.shape[0]):
            out_ref[group, pl.ds(at, half), :] = exact_dot2(
                matrix, split(ref[group, start:, :])
            )


def finer_kernel(slot, with_rim, passing, place_ref, *refs):
    wide_ref, refs = refs[-1], refs[:-1]
    if passing:
        refs[-1][...] = refs[0][...]
        refs = refs[1:-1]
    mine_ref, send_ref = refs[-2:]
    *sums, part_ref = refs[: -2 - with_rim]
    half = BLOCK // 2
    bit = place_ref[slot]
    offset = send_ref.shape[1] - BLOCK
    matrix = pair_matrix(half, BLOCK)
    for group in range(mine_ref.shape[0]):
        if with_rim:
            send_ref[group, :BLOCK, :] = refs[-3][group]
        wide = sums[0][group]
        for other in sums[1:]:
            wide = wide + other[group]
        wide_ref[...] = wide

        def handed(at):
            at = pl.ds(pl.multiple_of(at * half, half), half)
            return exact_dot2(matrix, split(wide_ref[at, :]), 0, 0)

        mine_ref[group] = handed(bit)
        send_ref[group, offset:, :] = handed(1 - bit) + part_ref[group]


def fold_kernel(slot, size, extra, place_ref, keep_ref, got_ref, *refs):
    if extra == "fresh":
        fresh_ref, refs = refs[0], refs[1:]
    if slot is None:
        refs[0][...] = keep_ref[:size, :] + got_ref[:size, :]
        if extra:
            refs[1][...] = keep_ref[size:, :] + got_ref[size:, :]
        return
    half = size // 2
    bit = place_ref[slot]
    for target, side in zip(refs, (bit, 1 - bit)):
        at = pl.ds(pl.multiple_of(side * half, half), half)
        target[:half, :] = keep_ref[at, :] + got_ref[at, :]
        if extra == "fresh":
            target[half:, :] = fresh_ref[...]
        elif extra:
            target[half:, :] = keep_ref[size:, :] + got_ref[size:, :]


def share_kernel(size, extra, place_ref, keep_ref, got_ref, *refs):
    keep, send = refs
    keep[...] = keep_ref[...] + got_ref[...]
    send[...] = keep[...]


def join_kernel(slot, place_ref, own_ref, got_ref, *refs):
    out_ref = refs[-1]
    half = own_ref.shape[0]
    bit = place_ref[slot]
    for source, side in ((own_ref, bit), (got_ref, 1 - bit)):
        out_ref[pl.ds(pl.multiple_of(side * half, half), half), :] = source[...]
    if len(refs) == 2:
        out_ref[2 * half :, :] = refs[0][...]


def run_copies(copies, sems):
    copies = [
        pltpu.make_async_copy(source, target, sems.at[index])
        for index, (source, target) in enumerate(copies)
    ]
    for copy in copies:
        copy.start()
    for copy in copies:
        copy.wait()


def place_outer_kernel(place_ref, own_ref, sib_ref, out_ref, sems):
    core, size = place_ref[CORE], own_ref.shape[0]
    run_copies(
        [
            (source, out_ref.at[pl.ds(pl.multiple_of(side * size, size), size), :])
            for source, side in ((own_ref, core), (sib_ref, 1 - core))
        ],
        sems,
    )


def place_inner_kernel(place_ref, own_ref, sib_ref, out_ref, sems):
    core, size = place_ref[CORE], out_ref.shape[0]
    copies = []
    for source, side in ((own_ref, core), (sib_ref, 1 - core)):
        for index in range(2):
            at = pl.ds(pl.multiple_of((side * 2 + index) * size, size), size)
            copies.append((source.at[index * size : (index + 1) * size, :], out_ref.at[:, at]))
    run_copies(copies, sems)


def place_square_kernel(part, place_ref, own_ref, sib_ref, *refs):
    *outs, sems = refs[-5:]
    half = outs[0].shape[0] // 2
    core = place_ref[CORE]
    copies = []
    for slot, out_ref in enumerate(outs):
        down, across = slot // 2 * half, slot % 2 * half
        for source, side in ((own_ref, core), (sib_ref, 1 - core)):
            at = pl.ds(pl.multiple_of(side * half, half), half)
            copies.append(
                (
                    source.at[down : down + half, across : across + half],
                    out_ref.at[at, part * half : (part + 1) * half],
                )
            )
    run_copies(copies, sems)


def vectors_kernel(own_ref, sib_ref, *outs):
    last = own_ref.shape[0] - SPARE
    vec_ref = own_ref[last:, :] + sib_ref[last:, :]
    for index, out in enumerate(outs):
        if index < 8:
            out[...] = vec_ref[index : index + 1, :]
        else:
            width = vec_ref.shape[-1]
            for part in range(4):
                out[:, part * width : (part + 1) * width] = vec_ref[8 + part : 9 + part, :]


def level_tables(span, crossing):
    half = span // 2
    top = int(math.log2(span // BLOCK // 2)) + crossing
    local_top = top - crossing
    expand = np.zeros((span, span), np.float32)
    means = np.zeros((span, span), np.float32)
    levels, at = [], 0
    for level in range(1, top + 1):
        count = span >> level
        for row in range(count):
            expand[at + row, row << level : (row + 1) << level] = 1.0
            means[at + row, row << level : (row + 1) << level] = 0.5**level
        levels.append((level, at, count))
        at += count
    near = np.full((half + 2 * BLOCK, half), FAR, np.float32)
    for query_block in range(half // BLOCK):
        near[
            query_block * BLOCK : (query_block + 3) * BLOCK,
            query_block * BLOCK : (query_block + 1) * BLOCK,
        ] = 0.0
    local_rows = sum(count for level, _, count in levels if level <= local_top)
    coarse = np.full((local_rows + BLOCK * crossing, span), FAR, np.float32)
    for level, start, count in levels:
        if level <= local_top:
            for block in range(count // BLOCK):
                key = start + (block ^ 1) * BLOCK
                query = start + block * BLOCK
                coarse[key : key + BLOCK, query : query + BLOCK] = level
        else:
            key = local_rows + (level - local_top - 1) * BLOCK
            coarse[key : key + BLOCK, start : start + count] = level
    one = coarse[:half, :half]
    rest = coarse[half:, half:]
    twice = lambda table: jnp.asarray(np.concatenate([table, table], axis=1))
    return (
        jnp.asarray(expand, bf16),
        jnp.asarray(means, bf16),
        twice(near),
        twice(one),
        twice(rest),
    )


class Here:
    def __init__(self, span, seq_count, steps):
        self.span, self.seq_count, self.steps = span, seq_count, steps

    def __getitem__(self, slot):
        seq, batch = lax.axis_index("seq"), lax.axis_index("batch")
        odd, core = seq & 1, batch & 1
        if slot == INNER:
            return (1 - odd) * (self.span - BLOCK)
        if slot == OUTER:
            return odd * (self.span - BLOCK)
        if slot == ODD:
            return odd
        if slot == FIRST:
            return (seq == 0).astype(jnp.int32)
        if slot == LAST:
            return (seq == self.seq_count - 1).astype(jnp.int32)
        if slot == CORE:
            return core
        slot -= CORE + 1
        crossing = self.seq_count.bit_length() - 1
        if slot < crossing:
            return seq >> slot & 1
        sides = [(batch, seq)[axis] >> bit & 1 for axis, bit in self.steps[slot - crossing]]
        return sides[0] + core * (sides[1] - sides[0])


class Order:
    def __init__(self):
        self.last = None

    def call(self, kernel, outs, ins, tag="", scratch=(), limit=8, spaces=None, out_space=VMEM,
             aliases=None):
        shapes = tuple(
            shape if isinstance(shape, jax.ShapeDtypeStruct) else jax.ShapeDtypeStruct(shape, f32)
            for shape in outs
        )
        spaces, aliases = spaces or {}, aliases or {}
        given = [index for index, value in enumerate(ins) if not isinstance(value, Here)]
        count, before = len(given), [] if self.last is None else [self.last]
        first_out = count + len(before)
        last_out = first_out + len(outs)

        def body(*refs):
            refs[last_out][...] = jnp.zeros(TOKEN, f32)
            taken = list(ins)
            for index, ref in zip(given, refs):
                taken[index] = ref
            kernel(*taken, *refs[first_out:last_out], *refs[last_out + 1 :])

        *results, self.last = pl.pallas_call(
            body,
            out_shape=shapes + (jax.ShapeDtypeStruct(TOKEN, f32),),
            in_specs=[spaces.get(index, VMEM) for index in given] + [ANY] * len(before),
            out_specs=tuple(out_space for _ in outs) + (VMEM,),
            name=getattr(kernel, "func", kernel).__name__ + str(tag),
            scratch_shapes=list(scratch),
            input_output_aliases={given.index(index): out for index, out in aliases.items()},
            cost_estimate=pl.CostEstimate(
                flops=COST, bytes_accessed=0, transcendentals=0
            ),
            compiler_params=pltpu.CompilerParams(vmem_limit_bytes=limit << 20),
        )(*[ins[index] for index in given], *before)
        return results


class Everywhere:
    def __init__(self, batch_count, seq_count):
        self.counts = batch_count, seq_count
        across = batch_count.bit_length() - 1
        along = seq_count.bit_length() - 1
        wide = [(0, bit) for bit in range(1, across)]
        tail = [(1, bit) for bit in range(1, along)]
        self.steps = list(zip(wide + [(1, 0)] + tail, [(1, 0)] + wide + tail))
        self.early = [(tail[0], tail[0])] + [step for step in self.steps if step[0] != tail[0]]
        self.core = ((0, 0), (0, 0))

    def swap(self, array, step):
        batch_count, seq_count = self.counts
        pairs = []
        for batch in range(batch_count):
            for seq in range(seq_count):
                axis, bit = step[batch % 2]
                other = (batch ^ 1 << bit, seq) if axis == 0 else (batch, seq ^ 1 << bit)
                pairs.append((batch * seq_count + seq, other[0] * seq_count + other[1]))
        return lax.ppermute(array, ("batch", "seq"), pairs)

    def chunk(self, call, place, steps, slot, kept, got, extra=None):
        size, width = kept.shape
        more = 0 if extra is None else extra.shape[0]
        keep = kept
        for index, step in enumerate(steps):
            fresh = extra is not None and index == 0
            mode = "fresh" if fresh else extra is not None
            keep, send = call(
                functools.partial(fold_kernel, slot + index, size, mode),
                [(size // 2 + more, width)] * 2,
                [place, keep, got] + ([extra] if fresh else []),
            )
            size //= 2
            got = self.swap(send, step)
            if index + 2 == len(steps):
                break
            yield
        yield
        keep, send = call(
            functools.partial(share_kernel, size, more),
            [(size + more, width)] * 2, [place, keep, got],
        )
        got = self.swap(send, steps[-1])
        yield
        own = call(
            functools.partial(fold_kernel, None, size, extra is not None),
            [(size, width)] + ([(more, width)] if more else []), [place, keep, got],
        )
        own, rest = own[0], own[1:]
        for index in range(len(steps) - 2, -1, -1):
            got = self.swap(own, steps[index])
            yield
            last = list(rest) if index == 0 else []
            (own,) = call(
                functools.partial(join_kernel, slot + index),
                [(2 * size + (more if last else 0), width)], [place, own, got] + last,
            )
            size *= 2
        return own, self.swap(own, self.core)


class Run:
    def __init__(self, turns):
        self.turns, self.result = turns, None

    def step(self, count=1):
        for _ in range(count if self.result is None else 0):
            try:
                next(self.turns)
            except StopIteration as end:
                self.result = end.value


def per_device(
    inputs, norm_gain, norm_bias, query_weight, query_bias, key_weight, value_weight, value_bias,
    mixer_weight, mixer_bias, final_gain, final_bias, inner_weight, inner_bias, outer_weight,
    outer_bias, cotangent,
):
    groups, span, width = inputs.shape
    tokens = groups * span
    half = span // 2
    hidden_width = inner_weight.shape[1]
    block = hidden_width // 4
    seq_count, batch_count = lax.axis_size("seq"), lax.axis_size("batch")
    crossing = seq_count.bit_length() - 1
    far_rows = BLOCK * crossing
    expand, means, near, one, rest = level_tables(span, crossing)
    coarse = means.shape[0]
    row = lambda vec: vec.reshape(1, -1)
    scale = 1.0 / math.sqrt(width // HEADS)
    x = inputs.reshape(tokens, width)
    cot = cotangent.reshape(tokens, width)
    everywhere = Everywhere(batch_count, seq_count)
    seq_slot = CORE + 1
    step_slot = seq_slot + crossing
    place = Here(span, seq_count, everywhere.steps + everywhere.early)
    inner_pairs = [(i, i ^ 1) for i in range(seq_count)]
    outer_pairs = [
        (i, j)
        for i in range(seq_count)
        for j in [i + 1 if i % 2 else i - 1]
        if 0 <= j < seq_count
    ]
    order = Order()
    gain, shift = row(norm_gain), row(norm_bias)
    part_of_feed = hidden_width // 2
    narrow = lambda *shape: jax.ShapeDtypeStruct(shape, bf16)
    at = types.SimpleNamespace(hidden={}, gib={}, pairs={}, kept={}, got={}, fine={}, rough={})
    sums, turns = {}, {}

    call = order.call

    def start_sum(name, send, extra=None):
        at.got[name] = everywhere.swap(send, everywhere.core)

    def turn(name):
        if name not in sums:
            turns[name] = 0
            extra = at.vec if name == "D" else None
            early = name in EARLY
            steps = everywhere.early if early else everywhere.steps
            sums[name] = Run(
                everywhere.chunk(
                    lambda *rest: call(*rest, name + str(turns[name])), place, steps,
                    step_slot + early * len(steps), at.kept[name], at.got[name],
                    extra,
                )
            )
        sums[name].step()
        turns[name] += 1

    def first_norm():
        at.unit, at.inv, at.inner_send, outer_send = call(
            functools.partial(first_norm_kernel, groups, span),
            [(tokens, width), (tokens, 1), (groups, 2 * BLOCK, width), (groups, BLOCK, width)],
            [place, x],
        )
        at.far = [lax.ppermute(at.inner_send, "seq", inner_pairs)]
        at.outer_got = lax.ppermute(outer_send, "seq", outer_pairs)
        at.coarse_own = at.inner_send

    def project(kinds):
        weights = {"q": query_weight, "k": key_weight, "v": value_weight}
        biases = {"q": [row(query_bias)], "k": [], "v": [row(value_bias)]}
        scales = {"q": scale * LOG2E, "k": None, "v": 1.0}
        outs = call(
            functools.partial(project_kernel, groups, span, [scales[kind] for kind in kinds]),
            [(tokens, width), (groups * coarse, width)] * len(kinds),
            [at.unit, gain, shift, means] + [weights[kind] for kind in kinds]
            + [bias for kind in kinds for bias in biases[kind]], kinds,
        )
        for index, kind in enumerate(kinds):
            at.fine[kind], at.rough[kind] = outs[2 * index], outs[2 * index + 1]

    def project_qk():
        project("qk")

    def project_v():
        project("v")

    def coarser():
        bit = len(at.far)
        (at.coarse_own,) = call(
            functools.partial(coarser_kernel, seq_slot + bit - 1),
            [(groups, BLOCK, width)], [place, at.coarse_own, at.far[-1]],
        )
        at.far.append(
            lax.ppermute(at.coarse_own, "seq", [(i, i ^ 1 << bit) for i in range(seq_count)])
        )

    def rest_coarser():
        while len(at.far) < crossing:
            coarser()

    def local():
        at.num, at.den, at.numc, at.denc, at.halo, at.hk, at.hv = call(
            functools.partial(local_kernel, groups, span),
            [(groups * width, span), (groups * HEADS, span), (groups * width, half),
             (groups * HEADS, half)] + [(groups * 2 * BLOCK, width)] * 3,
            [place] + [at.fine[kind] for kind in "qkv"] + [at.rough[kind] for kind in "qkv"]
            + [at.far[0], at.outer_got, gain, shift, key_weight, value_weight,
               row(value_bias), near, one],
            scratch=[pltpu.VMEM((2,) + near.shape, f32)],
        )

    def remote():
        ins = at.far + [x, at.num, at.den, at.numc, at.denc]
        ins += [at.rough[kind] for kind in "qkv"]
        ins += [
            gain, shift, key_weight, value_weight, row(value_bias), rest, expand, mixer_weight,
            row(mixer_bias), row(final_gain), row(final_bias), row(outer_bias), cot,
        ]
        (
            at.far_rows, at.rk, at.rv, at.mixed, at.rden, at.unit2, at.inv2,
            at.acc, *at.split
        ) = call(
            functools.partial(remote_kernel, groups, span, crossing),
            [(groups * far_rows, width)] * 3 + [(groups * width, span), (groups * HEADS, span),
             (tokens, width), (tokens, 1), (tokens, width)] + [narrow(tokens, width)] * 4,
            ins, scratch=[pltpu.VMEM((tokens, width), f32)],
        )

    def outer(own):
        joint, *at.hidden[own] = call(
            functools.partial(outer_kernel, own),
            [(part_of_feed, width)] + [narrow(tokens, part_of_feed)] * 2 + [(tokens, part_of_feed)],
            [place] + at.split + [inner_weight, row(inner_bias)], own, limit=16,
        )
        if own:
            at.kept["A"] = joint
        else:
            start_sum("A", joint)

    def inner(own):
        joint, at.gib[own], at.acc, at.gacc = call(
            functools.partial(inner_kernel, own),
            [(2 * width, part_of_feed // 2), (1, part_of_feed), (tokens, width), (tokens, width)],
            [place] + at.split + at.hidden[own] + [inner_weight, outer_weight, at.acc]
            + ([at.gacc] if own else []),
            own, limit=16,
        )
        if own:
            at.kept["B"] = joint
        else:
            start_sum("B", joint)

    def middle_grad():
        (
            at.gmid, at.gmw, at.vec_mid, at.gnum, at.gnumt, at.gden, at.gnumct,
            at.gdenc,
        ) = call(
            functools.partial(middle_grad_kernel, groups, span),
            [(tokens, width), (width, width), (8, width), (tokens, width), (groups * width, span),
             (groups * HEADS, span), (groups * width, coarse), (groups * HEADS, coarse)],
            [cot, at.gacc, at.unit2, at.inv2, row(final_gain), at.mixed, at.rden,
             mixer_weight, expand],
        )

    outside_rows = groups * (2 * BLOCK + far_rows)

    def pairs(part):
        at.pairs[part] = call(
            functools.partial(pairs_grad_kernel, groups, part, span),
            [(tokens, half_width)] * 3 + [(outside_rows, half_width)] * 2,
            [place] + [at.fine[kind] for kind in "qkv"] + [at.rough[kind] for kind in "qkv"]
            + [at.hk, at.hv, at.rk, at.rv, at.gnum, at.gnumt, at.gden, at.gnumct, at.gdenc, near, one,
               rest, means], part,
            scratch=[
                pltpu.VMEM((2,) + near.shape, f32),
                pltpu.VMEM((span + 2 * BLOCK, half_width), f32),
                pltpu.VMEM((span + 2 * BLOCK, half_width), f32),
                pltpu.VMEM((half + rest.shape[0], half_width), f32),
                pltpu.VMEM((half + rest.shape[0], half_width), f32),
                pltpu.VMEM((half_width, span), f32),
                pltpu.VMEM((half_width, coarse), f32),
            ],
        )

    half_width = width // 2

    def square(part):
        name = "CD"[part]
        at.kept[name], send = call(
            functools.partial(square_grad_kernel, part, scale),
            [(width, width)] * 2,
            [place, at.unit, at.halo, at.far_rows, gain, shift, at.gmw]
            + list(at.pairs[part]), part,
            scratch=[pltpu.VMEM((3, width, half_width), f32)],
        )
        start_sum(name, send)

    def rows_grad():
        at.vec, at.gnorm, at.inner_back, outer_back, *gfar = call(
            functools.partial(rows_grad_kernel, groups, crossing, scale),
            [(SPARE, width), (tokens, width)] + [(groups, BLOCK, width)] * (2 + crossing),
            [place, at.unit, at.halo, at.far_rows] + list(at.pairs[0])
            + list(at.pairs[1]) + [query_weight, key_weight, value_weight, at.vec_mid,
                                     at.gib[0], at.gib[1]],
        )
        at.outer_back = lax.ppermute(outer_back, "seq", outer_pairs)
        at.gfar = gfar
        at.back = [
            lax.ppermute(gfar[-1], "seq", [(i, i ^ 1 << crossing - 1) for i in range(seq_count)])
        ]
        at.back_bit = crossing - 1

    def finer():
        at.back_bit -= 1
        bit = at.back_bit
        rim = [] if bit else [at.inner_back]
        passing = [at.outer_back] if bit == crossing - 2 else []
        mine, send, *passed = call(
            functools.partial(finer_kernel, seq_slot + bit, len(rim), bool(passing)),
            [(groups, BLOCK, width), (groups, BLOCK * (1 + len(rim)), width)]
            + [value.shape for value in passing],
            [place] + passing + at.back + [at.gfar[bit]] + rim,
            scratch=[pltpu.VMEM((BLOCK, width), f32)],
        )
        if passed:
            at.outer_back = passed[0]
        at.back = [
            lax.ppermute(send, "seq", [(i, i ^ 1 << bit) for i in range(seq_count)]), mine
        ]

    def first_grad():
        while at.back_bit:
            finer()
        (at.inputs_grad,) = call(
            functools.partial(first_grad_kernel, groups, span),
            [(tokens, width)],
            [place, at.gmid, at.gnorm] + at.back
            + [at.outer_back, at.unit, at.inv, gain],
            scratch=[pltpu.VMEM((tokens, width), f32)],
        )

    def write(name, kernel, shapes, count, before=()):
        while name not in sums or sums[name].result is None:
            turn(name)
        ins = [place] + list(sums[name].result) + list(before)
        return call(
            kernel, shapes, ins, name, scratch=[pltpu.SemaphoreType.DMA((count,))],
            out_space=HBM, spaces={3 + index: HBM for index in range(len(before))},
            aliases={3 + index: index for index in range(len(before))},
        )

    def write_outer():
        at.gow = write("A", place_outer_kernel, [(hidden_width, width)], 2)

    def write_inner():
        at.giw = write("B", place_inner_kernel, [(width, hidden_width)], 4)

    def write_square(part):
        at.squares = write(
            "CD"[part], functools.partial(place_square_kernel, part), [(width, width)] * 4, 8,
            getattr(at, "squares", ()),
        )
        if part:
            at.vecs = call(
                vectors_kernel, [(1, width)] * 8 + [(1, hidden_width)],
                list(sums["D"].result),
            )

    acts = (
        first_norm, project_qk, project_v, coarser, rest_coarser, local, remote, outer, inner,
        middle_grad, pairs, square, rows_grad, finer, first_grad, write_outer, write_inner,
        write_square,
    )
    acts = {act.__name__: act for act in acts}
    for name in PLAN:
        if name.isupper():
            turn(name)
        else:
            acts[name.rstrip("01")](*[int(digit) for digit in name if digit.isdigit()])
    gng, gnb, gqb, gvb, gfg, gfb, gmb, gob, gib = [vec.reshape(-1) for vec in at.vecs]
    gqw, gkw, gvw, gmw = at.squares
    return (
        at.acc.reshape(inputs.shape), at.inputs_grad.reshape(inputs.shape), gng, gnb, gqw,
        gqb, gkw, gvw, gvb, gmw, gmb, gfg, gfb, at.giw[0], gib, at.gow[0], gob,
    )


def solution(mesh):
    split_spec = P("batch", "seq", None)
    return jax.shard_map(
        per_device,
        mesh=mesh,
        in_specs=(split_spec,) + (P(),) * 15 + (split_spec,),
        out_specs=(split_spec, split_spec) + (P(),) * 15,
        check_vma=False,
    )
```
